32 devices in a mesh: dp: 16 (over z, x, core), head: 2 (over y).
Axes of the slice: x: 2, y: 2, z: 4, core: 2. Of those that a mesh axis runs over, the one named last changes fastest.
Arguments:
- tokens: bfloat16 [16384, 1024], P(('dp', 'head')), may hold values from -6 to 6
- lengths: int32 [16], P('dp'), may hold values from 128 to 1024, as said below
- decay: float32 [8], P('head'), may hold values from 0.00048828125 to 0.03125
- w_query: bfloat16 [1024, 1024], P(None, 'head'), may hold values from -0.1875 to 0.1875
- w_key: bfloat16 [1024, 1024], P(None, 'head'), may hold values from -0.1875 to 0.1875
- w_value: bfloat16 [1024, 1024], P(None, 'head'), may hold values from -0.1875 to 0.1875
- w_gate: bfloat16 [1024, 1024], P(None, 'head'), may hold values from -0.1875 to 0.1875
- w_out: bfloat16 [1024, 1024], P('head'), may hold values from -0.1875 to 0.1875
- f_value: bfloat16 [1024, 2816], P('dp', 'head'), may hold values from -0.1875 to 0.1875
- f_gate: bfloat16 [1024, 2816], P('dp', 'head'), may hold values from -0.1875 to 0.1875
- f_out: bfloat16 [2816, 1024], P('head', 'dp'), may hold values from -0.109375 to 0.109375
- cotangent: bfloat16 [16384, 1024], P(('dp', 'head')), may hold values from -6 to 6
Outputs:
- output: bfloat16 [16384, 1024], P(('dp', 'head'))
- d_tokens: float32 [16384, 1024], P(('dp', 'head'))
- d_w_query: float32 [1024, 1024], P(None, 'head')
- d_w_key: float32 [1024, 1024], P(None, 'head')
- d_w_value: float32 [1024, 1024], P(None, 'head')
- d_w_gate: float32 [1024, 1024], P(None, 'head')
- d_w_out: float32 [1024, 1024], P('head')
- d_f_value: float32 [1024, 2816], P('dp', 'head')
- d_f_gate: float32 [1024, 2816], P('dp', 'head')
- d_f_out: float32 [2816, 1024], P('head', 'dp')
The draws below stay inside these ranges and needn't reach their ends.
Inputs may be any that keep to these rules, and one draw needn't show every extreme that they name: `lengths`: each bucket holds a single slot, and that slot's sequence has length 1024.
All inputs are finite; a program needn't handle non-finite values.
Results may differ from the reference program's by a relative error of at most 0.022.
Values may be sent and summed in bfloat16 or wider, within the bound.
A program may use at most 192 MiB of HBM per device.

```python
import math
import jax
import jax.numpy as jnp
from jax import lax

D = 1024
H = 8
HD = 128
FF = 2816
SEQ_DEV = 1
SLOT = 1024
BLOCK = 512
TOK_DEV = 1024
SEQS = 16
TOKENS = 16384


def draw_lengths(key, part):
    groups = SEQS // SEQ_DEV
    base = jax.random.randint(jax.random.fold_in(key, 11), (groups, SEQ_DEV), SLOT // 8, SLOT + 1)
    chosen = jax.random.randint(jax.random.fold_in(key, 12), (groups, 1), 0, SEQ_DEV)
    filled = jnp.arange(SEQ_DEV, dtype=jnp.int32)[None, :] == chosen
    return jnp.where(filled, SLOT, base).reshape(groups * SEQ_DEV).astype(jnp.int32)


def block_scale(key, extent, cuts, least, high):
    level, own = 1.0, jax.random.fold_in(key, 6)
    for dim, blocks in cuts:
        draws = jnp.exp(jax.random.uniform(jax.random.fold_in(own, dim), (blocks,), jnp.float32, least / len(cuts), high / len(cuts)))
        level = level * jnp.repeat(draws, extent[dim] // blocks).reshape([-1 if axis == dim else 1 for axis in range(len(extent))])
    return level


def noise(rng, shape, scale, reach, pieces=(), kind=jnp.bfloat16):
    gain = block_scale(rng, shape, pieces, -0.22, 0.18) if pieces else 1.0
    values = jax.random.normal(rng, shape, jnp.float32) * scale * gain
    return jnp.minimum(jnp.maximum(values, -reach), reach).astype(kind)


def setup_inputs(seed: int = 0) -> dict:
    key_list = jax.random.split(jax.random.key(seed), 13)
    tokens = noise(key_list[0], (TOKENS, D), 1.0, 6.0, ((0, 32),))
    lengths = draw_lengths(jax.random.fold_in(key_list[12], 71), 0)
    decay = jnp.clip(jnp.exp(math.log(0.03125) - 4.158883 * jax.random.uniform(key_list[2], (H,), jnp.float32) ** block_scale(key_list[2], (H,), ((0, 2),), -0.2, 0.2)), 0.00048828125, 0.03125)
    w_query = noise(key_list[3], (D, D), D ** -0.5, 0.1875, ((1, 2),))
    w_key = noise(key_list[4], (D, D), D ** -0.5, 0.1875, ((1, 2),))
    w_value = noise(key_list[5], (D, D), D ** -0.5, 0.1875, ((1, 2),))
    w_gate = noise(key_list[6], (D, D), D ** -0.5, 0.1875, ((1, 2),))
    w_out = noise(key_list[7], (D, D), D ** -0.5, 0.1875, ((0, 2),))
    f_value = noise(key_list[8], (D, FF), D ** -0.5, 0.1875, ((0, 16), (1, 2)))
    f_gate = noise(key_list[9], (D, FF), D ** -0.5, 0.1875, ((0, 16), (1, 2)))
    f_out = noise(key_list[10], (FF, D), FF ** -0.5, 0.109375, ((0, 2), (1, 16)))
    cotangent = noise(key_list[11], (TOKENS, D), 1.0, 6.0, ((0, 32),))
    return dict(tokens=tokens, lengths=lengths, decay=decay, w_query=w_query, w_key=w_key, w_value=w_value, w_gate=w_gate, w_out=w_out, f_value=f_value, f_gate=f_gate, f_out=f_out, cotangent=cotangent)


@jax.custom_vjp
def low(v):
    return lax.optimization_barrier(v.astype(jnp.bfloat16)).astype(jnp.float32)

@jax.custom_vjp
def low_back(v):
    return v

def low_keep(v):
    return (low(v), None)

def low_pass(kept, grad):
    return (grad,)

def back_keep(v):
    return (v, None)

def back_low(kept, grad):
    return (low(grad),)
low.defvjp(low_keep, low_pass)
low_back.defvjp(back_keep, back_low)
epsilon = 1e-06

def product(left_side, right_side):
    return jnp.dot(left_side, right_side, precision=lax.Precision.HIGHEST, preferred_element_type=jnp.float32)

def exact(form, left_side, right_side):
    return jnp.einsum(form, left_side, right_side, precision=lax.Precision.HIGHEST)

def normalize(values):
    return values * lax.rsqrt(lax.optimization_barrier(jnp.mean(values * values, axis=-1, keepdims=True)) + epsilon)

def decay_tables(rates):
    offsets = jnp.arange(BLOCK).astype(jnp.float32)
    spread = offsets[:, None] - offsets[None, :]
    causal = spread >= 0
    within = jnp.where(causal[None], jnp.exp(-rates[:, None, None] * jnp.where(causal, spread, 0.0)[None]), 0.0)
    first_decay = jnp.exp(-rates[:, None] * (offsets[None, :] + 1.0))
    last_decay = jnp.exp(-rates[:, None] * (BLOCK - 1.0 - offsets[None, :]))
    block_decay = jnp.exp(-rates * BLOCK)
    return (within, first_decay, last_decay, block_decay)

def lightning(query, keys, values, rates):
    blocks = SLOT // BLOCK

    def arrange(tensor):
        return tensor.reshape(blocks, BLOCK, H, HD).transpose(0, 2, 1, 3)
    within, first_decay, last_decay, block_decay = decay_tables(rates)

    def advance(carried, inputs):
        query_blk, keys_blk, values_blk = inputs
        scores = low_back(exact('hbd,hcd->hbc', query_blk, keys_blk))
        weights = low(scores * within)
        inner_sum = exact('hbc,hcd->hbd', weights, values_blk)
        outer_sum = first_decay[:, :, None] * exact('hbd,hde->hbe', query_blk, carried)
        update = exact('hbd,hbe->hde', keys_blk * last_decay[:, :, None], values_blk)
        return (block_decay[:, None, None] * carried + update, inner_sum + outer_sum)
    initial = jnp.zeros((H, HD, HD), jnp.float32)
    final_state, mixed = lax.scan(jax.checkpoint(advance), initial, (arrange(query), arrange(keys), arrange(values)))
    return mixed.transpose(0, 2, 1, 3).reshape(SLOT, H * HD)

def layer(inputs, w_query, w_key, w_value, w_gate, w_out, f_value, f_gate, f_out, rates, keep_rows):
    normed = low(normalize(inputs))
    query_pre = low_back(product(normed, w_query))
    keys_pre = low_back(product(normed, w_key))
    values_pre = low_back(product(normed, w_value))
    gate_pre = low_back(product(normed, w_gate))
    query = low(jax.nn.silu(query_pre))
    keys = low(jax.nn.silu(keys_pre))
    values = low(values_pre)

    def per_sequence(triple):
        return lightning(triple[0], triple[1], triple[2], rates)
    shaped = (query.reshape(SEQ_DEV, SLOT, H, HD), keys.reshape(SEQ_DEV, SLOT, H, HD), values.reshape(SEQ_DEV, SLOT, H, HD))
    mixed = low_back(lax.map(per_sequence, shaped).reshape(TOK_DEV, D))
    gated = low(normalize(mixed) * gate_pre)
    middle = inputs + low_back(product(gated, w_out))
    mid_normed = low(normalize(middle))
    value_ffn = low_back(product(mid_normed, f_value))
    gate_ffn = low_back(product(mid_normed, f_gate))
    hidden = low(value_ffn * gate_ffn)
    return (middle + product(hidden, f_out)) * keep_rows[:, None]

def reference(tokens, lengths, decay, w_query, w_key, w_value, w_gate, w_out, f_value, f_gate, f_out, cotangent):
    weights = (w_query.astype(jnp.float32), w_key.astype(jnp.float32), w_value.astype(jnp.float32), w_gate.astype(jnp.float32), w_out.astype(jnp.float32), f_value.astype(jnp.float32), f_gate.astype(jnp.float32), f_out.astype(jnp.float32))
    row_index = jnp.arange(TOK_DEV, dtype=jnp.int32)
    slot_of = row_index // SLOT
    position = row_index % SLOT
    groups = TOKENS // TOK_DEV
    inputs_all = tokens.astype(jnp.float32).reshape(groups, TOK_DEV, D)
    grads_all = cotangent.astype(jnp.float32).reshape(groups, TOK_DEV, D)
    limits_all = lengths.reshape(groups, SEQ_DEV)

    def visit(totals, inputs):
        inputs_here, grads_here, limits_here = inputs
        keep_rows = (position < limits_here[slot_of]).astype(jnp.float32)

        def forward(values, params):
            return layer(values, params[0], params[1], params[2], params[3], params[4], params[5], params[6], params[7], decay, keep_rows)
        result, pullback = jax.vjp(forward, inputs_here, weights)
        d_inputs, d_params = pullback(grads_here)
        totals = tuple((total + addend for total, addend in zip(totals, d_params)))
        return (totals, (result.astype(jnp.bfloat16), d_inputs))
    initial = tuple((jnp.zeros_like(weight) for weight in weights))
    totals, (outputs, d_inputs) = lax.scan(visit, initial, (inputs_all, grads_all, limits_all))
    return (outputs.reshape(TOKENS, D), d_inputs.reshape(TOKENS, D), totals[0], totals[1], totals[2], totals[3], totals[4], totals[5], totals[6], totals[7])
```

```python
import jax
import jax.numpy as jnp
from jax import lax
from jax.experimental import pallas as pl
from jax.experimental.pallas import tpu as pltpu
from jax.sharding import PartitionSpec as P

D = 1024
HD = 128
SEQ_DEV = 1
SLOT = 1024
BLOCK = 512


epsilon = 1e-06


def normalize(values):
    factor = lax.rsqrt(jnp.mean(values * values, axis=-1, keepdims=True) + epsilon)
    return (values * factor, factor)


def norm_back(grad_normed, normed, factor):
    inner_sum = jnp.mean(grad_normed * normed, axis=-1, keepdims=True)
    return factor * (grad_normed - normed * inner_sum)


def silu_slope(values):
    sigmoid = jax.nn.sigmoid(values)
    return sigmoid * (1.0 + values * (1.0 - sigmoid))


def matmul(left_side, right_side):
    return jnp.dot(left_side, right_side, preferred_element_type=jnp.float32)


def matmul_right_t(left_side, right_side):
    return lax.dot_general(
        left_side, right_side, (((1,), (1,)), ((), ())), preferred_element_type=jnp.float32
    )


def matmul_left_t(left_side, right_side):
    return lax.dot_general(
        left_side, right_side, (((0,), (0,)), ((), ())), preferred_element_type=jnp.float32
    )


def exact(form, left_side, right_side):
    return jnp.einsum(form, left_side, right_side, precision=lax.Precision.HIGHEST)


def decay_tables(rates):
    offsets = jnp.arange(BLOCK).astype(jnp.float32)
    spread = offsets[:, None] - offsets[None, :]
    causal = spread >= 0
    within = jnp.where(
        causal[None], jnp.exp(-rates[:, None, None] * jnp.where(causal, spread, 0.0)[None]), 0.0
    )
    first_decay = jnp.exp(-rates[:, None] * (offsets[None, :] + 1.0))
    last_decay = jnp.exp(-rates[:, None] * (BLOCK - 1.0 - offsets[None, :]))
    block_decay = jnp.exp(-rates * BLOCK)
    return (within, first_decay, last_decay, block_decay)


def to_blocks(values, heads):
    shaped = values.reshape(SEQ_DEV, SLOT // BLOCK, BLOCK, heads, HD)
    return shaped.transpose(1, 0, 3, 2, 4)


def from_blocks(blocks):
    return blocks.transpose(1, 0, 3, 2, 4).reshape(-1, blocks.shape[2] * blocks.shape[4])


def lightning_forward(query, keys, values, tables):
    within, first_decay, last_decay, block_decay = tables

    def advance(carried, inputs):
        query_blk, keys_blk, values_blk = inputs
        scores = jnp.einsum(
            "shbd,shcd->shbc", query_blk, keys_blk, preferred_element_type=jnp.float32
        )
        weights = (scores * within[None]).astype(jnp.bfloat16)
        inner_sum = jnp.einsum(
            "shbc,shcd->shbd", weights, values_blk, preferred_element_type=jnp.float32
        )
        outer_sum = first_decay[None, :, :, None] * exact(
            "shbd,shde->shbe", query_blk.astype(jnp.float32), carried
        )
        keys_scaled = keys_blk.astype(jnp.float32) * last_decay[None, :, :, None]
        update = exact("shbd,shbe->shde", keys_scaled, values_blk.astype(jnp.float32))
        return (
            block_decay[None, :, None, None] * carried + update,
            (inner_sum + outer_sum, carried),
        )

    initial = jnp.zeros((SEQ_DEV, query.shape[2], HD, HD), jnp.float32)
    final_state, (mixed, states) = lax.scan(advance, initial, (query, keys, values))
    return (mixed, states)


def lightning_backward(query, keys, values, grads, states, tables):
    within, first_decay, last_decay, block_decay = tables

    def retreat(later_grad, inputs):
        query_blk, keys_blk, values_blk, grad_blk, carried = inputs
        scores = jnp.einsum(
            "shbd,shcd->shbc", query_blk, keys_blk, preferred_element_type=jnp.float32
        )
        weights = (scores * within[None]).astype(jnp.bfloat16)
        d_weights = jnp.einsum(
            "shbd,shcd->shbc", grad_blk, values_blk, preferred_element_type=jnp.float32
        )
        d_scores = (d_weights * within[None]).astype(jnp.bfloat16)
        d_query = jnp.einsum(
            "shbc,shcd->shbd", d_scores, keys_blk, preferred_element_type=jnp.float32
        )
        d_keys = jnp.einsum(
            "shbc,shbd->shcd", d_scores, query_blk, preferred_element_type=jnp.float32
        )
        d_values = jnp.einsum(
            "shbc,shbd->shcd", weights, grad_blk, preferred_element_type=jnp.float32
        )
        grad_scaled = grad_blk.astype(jnp.float32) * first_decay[None, :, :, None]
        keys_scaled = keys_blk.astype(jnp.float32) * last_decay[None, :, :, None]
        d_query = d_query + exact("shbe,shde->shbd", grad_scaled, carried)
        d_keys = d_keys + last_decay[None, :, :, None] * exact(
            "shbe,shde->shbd", values_blk.astype(jnp.float32), later_grad
        )
        d_values = d_values + exact("shbd,shde->shbe", keys_scaled, later_grad)
        earlier = block_decay[None, :, None, None] * later_grad + exact(
            "shbd,shbe->shde", query_blk.astype(jnp.float32), grad_scaled
        )
        return (earlier, (d_query, d_keys, d_values))

    initial = jnp.zeros((SEQ_DEV, query.shape[2], HD, HD), jnp.float32)
    first_grad, results = lax.scan(
        retreat, initial, (query, keys, values, grads, states), reverse=True
    )
    return results


def general_body(
    tokens,
    lengths,
    decay,
    w_query,
    w_key,
    w_value,
    w_gate,
    w_out,
    f_value,
    f_gate,
    f_out,
    cotangent,
):
    own_rows = tokens.shape[0]
    first_row = lax.axis_index("head") * own_rows
    heads_here = decay.shape[0]
    tables = decay_tables(decay)
    positions = first_row + jnp.arange(own_rows, dtype=jnp.int32)
    slot_match = (positions // SLOT)[:, None] == jnp.arange(SEQ_DEV, dtype=jnp.int32)[None, :]
    length_of = jnp.sum(jnp.where(slot_match, lengths[None, :], 0), axis=1)
    keep_rows = (positions % SLOT < length_of).astype(jnp.float32)[:, None]
    inputs_f = tokens.astype(jnp.float32)
    normed, scale_in = normalize(inputs_f)
    gathered = lax.all_gather(normed.astype(jnp.bfloat16), "head", axis=0, tiled=True)
    query_pre = matmul(gathered, w_query)
    keys_pre = matmul(gathered, w_key)
    values_pre = matmul(gathered, w_value)
    gate_pre = matmul(gathered, w_gate)
    query_blocks = to_blocks(jax.nn.silu(query_pre).astype(jnp.bfloat16), heads_here)
    keys_blocks = to_blocks(jax.nn.silu(keys_pre).astype(jnp.bfloat16), heads_here)
    values_blocks = to_blocks(values_pre.astype(jnp.bfloat16), heads_here)
    mixed_blocks, states = lightning_forward(query_blocks, keys_blocks, values_blocks, tables)
    mixed = from_blocks(mixed_blocks)
    squares = lax.psum(jnp.sum(mixed * mixed, axis=1), "head")
    scale_out = lax.rsqrt(squares / D + epsilon)[:, None]
    mixed_unit = mixed * scale_out
    gated = (mixed_unit * gate_pre).astype(jnp.bfloat16)
    branch = lax.psum_scatter(
        matmul(gated, w_out).astype(jnp.bfloat16), "head", scatter_dimension=0, tiled=True
    ).astype(jnp.float32)
    middle = inputs_f + branch
    mid_normed, scale_mid = normalize(middle)
    mid_all = lax.all_gather(mid_normed.astype(jnp.bfloat16), "head", axis=0, tiled=True)
    value_full, gate_full = (
        lax.all_gather(f_value, "dp", axis=0, tiled=True),
        lax.all_gather(f_gate, "dp", axis=0, tiled=True),
    )
    down_full = lax.all_gather(f_out, "dp", axis=1, tiled=True)
    value_ffn = matmul(mid_all, value_full)
    gate_ffn = matmul(mid_all, gate_full)
    hidden = (value_ffn * gate_ffn).astype(jnp.bfloat16)
    ffn_branch = lax.psum_scatter(
        matmul(hidden, down_full).astype(jnp.bfloat16), "head", scatter_dimension=0, tiled=True
    ).astype(jnp.float32)
    output = ((middle + ffn_branch) * keep_rows).astype(jnp.bfloat16)
    grad_out = cotangent.astype(jnp.float32) * keep_rows
    grad_all = lax.all_gather(grad_out.astype(jnp.bfloat16), "head", axis=0, tiled=True)
    grad_hidden = matmul_right_t(grad_all, down_full)
    d_value_ffn = (grad_hidden * gate_ffn).astype(jnp.bfloat16)
    d_gate_ffn = (grad_hidden * value_ffn).astype(jnp.bfloat16)
    d_mid_normed = lax.psum_scatter(
        (matmul_right_t(d_value_ffn, value_full) + matmul_right_t(d_gate_ffn, gate_full)).astype(
            jnp.bfloat16
        ),
        "head",
        scatter_dimension=0,
        tiled=True,
    ).astype(jnp.float32)
    grad_middle = grad_out + norm_back(d_mid_normed, mid_normed, scale_mid)
    joined = jnp.concatenate([d_value_ffn, d_gate_ffn], axis=1)
    hidden_here = hidden.shape[1]
    shares = lax.psum_scatter(
        jnp.concatenate(
            [matmul_left_t(mid_all, joined), matmul_left_t(grad_all, hidden)], axis=1
        ).astype(jnp.bfloat16),
        "dp",
        scatter_dimension=0,
        tiled=True,
    ).astype(jnp.float32)
    d_f_value = shares[:, :hidden_here]
    d_f_gate = shares[:, hidden_here : 2 * hidden_here]
    d_f_out = shares[:, 2 * hidden_here :].T
    grad_rows = lax.all_gather(grad_middle.astype(jnp.bfloat16), "head", axis=0, tiled=True)
    d_gated = matmul_right_t(grad_rows, w_out)
    d_w_out_local = matmul_left_t(gated, grad_rows)
    d_gate_pre = (d_gated * mixed_unit).astype(jnp.bfloat16)
    d_unit = d_gated * gate_pre
    inner_out = lax.psum(jnp.sum(d_unit * mixed_unit, axis=1), "head")
    d_mixed = (scale_out * (d_unit - mixed_unit * (inner_out / D)[:, None])).astype(jnp.bfloat16)
    d_query, d_keys, d_values = lightning_backward(
        query_blocks, keys_blocks, values_blocks, to_blocks(d_mixed, heads_here), states, tables
    )
    d_query_pre = (from_blocks(d_query) * silu_slope(query_pre)).astype(jnp.bfloat16)
    d_keys_pre = (from_blocks(d_keys) * silu_slope(keys_pre)).astype(jnp.bfloat16)
    d_values_pre = from_blocks(d_values).astype(jnp.bfloat16)
    total = matmul_right_t(d_query_pre, w_query) + matmul_right_t(d_keys_pre, w_key)
    d_normed = lax.psum_scatter(
        (total + matmul_right_t(d_values_pre, w_value) + matmul_right_t(d_gate_pre, w_gate)).astype(
            jnp.bfloat16
        ),
        "head",
        scatter_dimension=0,
        tiled=True,
    ).astype(jnp.float32)
    d_tokens = grad_middle + norm_back(d_normed, normed, scale_in)
    grads_attention = (
        lax.psum(matmul_left_t(gathered, d_query_pre).astype(jnp.bfloat16), "dp").astype(
            jnp.float32
        ),
        lax.psum(matmul_left_t(gathered, d_keys_pre).astype(jnp.bfloat16), "dp").astype(
            jnp.float32
        ),
        lax.psum(matmul_left_t(gathered, d_values_pre).astype(jnp.bfloat16), "dp").astype(
            jnp.float32
        ),
        lax.psum(matmul_left_t(gathered, d_gate_pre).astype(jnp.bfloat16), "dp").astype(
            jnp.float32
        ),
        lax.psum(d_w_out_local.astype(jnp.bfloat16), "dp").astype(jnp.float32),
    )
    return (
        output,
        d_tokens,
        grads_attention[0],
        grads_attention[1],
        grads_attention[2],
        grads_attention[3],
        grads_attention[4],
        d_f_value,
        d_f_gate,
        d_f_out,
    )


MESH = pl.DeviceIdType.MESH
NCH = 11
RA = 16
HR = 32
SP = 2
SPW = 2
RS_AT = (1, 2, 4, 6, 8)
NP = 4
CW = 512 // NP
NPIECE = 5 * NP
WG_AT = tuple(1 + 2 * k for k in range(8))
bf = jnp.bfloat16
f32 = jnp.float32
NT = (((1,), (1,)), ((), ()))


def dot(a, b):
    return jnp.dot(a, b, preferred_element_type=f32)


def dotnt(a, b):
    return lax.dot_general(a, b, NT, preferred_element_type=f32)


def place():
    d=lax.axis_index("dp")
    return d//4, (d//2)%2, d%2, lax.axis_index("head")
def dev(z,x,c,y): return ((z*2+x)*2+c, y)
def gather_kernel(s_ref, wq, wk, wv, wg, wo, W3, pq, pk, pv, pg, po, zs, zr, xs, xr, ys, yr, ds, dr, wys, wyr, wzs, wzr, wxs, wxr, wds, wdr, ls):
    z,x,c,y=place()
    zp=[lax.rem(z+r,4) for r in (1,2,3)]
    bar=pltpu.get_barrier_semaphore()
    peers=[dev(q,x,c,y) for q in zp]+[dev(z,1-x,c,y),dev(z,x,1-c,y),dev(z,x,c,1-y)]
    for p in peers: pl.semaphore_signal(bar,inc=1,device_id=p,device_id_type=MESH)
    pl.semaphore_wait(bar,len(peers))
    X=dev(z,1-x,c,y); Y=dev(z,x,c,1-y); C=dev(z,x,1-c,y)
    col=pl.ds(pl.multiple_of(y*128,128),128)
    own=[wq,wk,wv,wg,wo]; par=[pq,pk,pv,pg,po]
    def rc(src,dst,ss,rs,d): return pltpu.make_async_remote_copy(src_ref=src,dst_ref=dst,send_sem=ss,recv_sem=rs,device_id=d,device_id_type=MESH)
    loc=pltpu.make_async_copy(s_ref, W3.at[:,z,:,x,c,y], ls)
    loc.start()
    def st(k,i):
        if k==0:
            o=[]
            for n,q in enumerate(zp):
                t=W3.at[i,z,:,x,c,y]
                o.append(rc(s_ref.at[i],t,zs.at[i,n],zr.at[i,n],dev(q,x,c,y)))
            return o
        if k==1:
            a=W3.at[i,:,:,x,c,y,0:RA]; b=W3.at[i,:,:,x,c,y,RA:64]
            return [rc(a,a,xs.at[i,0],xr.at[i,0],X), rc(b,b,ys.at[i,0],yr.at[i,0],Y)]
        if k==2:
            a=W3.at[i,:,:,:,c,y,0:RA]; b=W3.at[i,:,:,x,c,:,RA:64]
            return [rc(b,b,xs.at[i,1],xr.at[i,1],X), rc(a,a,ys.at[i,1],yr.at[i,1],Y)]
        if k==3:
            a=W3.at[i,:,:,:,c]
            return [rc(a,a,ds.at[i],dr.at[i],C)]
    zb=lax.rem(z,2); ZP=dev(z+1-2*zb,x,c,y)
    def wst(k,j):
        if k==0: return [rc(own[j].at[zb,c],par[j].at[zb,c],wys.at[j],wyr.at[j],Y)]
        if k==1:
            a=par[j].at[zb,c]
            return [rc(a,a,wxs.at[j],wxr.at[j],ZP)]
        if k==2:
            a=par[j].at[:,c]
            return [rc(a,a,wds.at[j],wdr.at[j],C)]
        return []
    live={}
    def go(f,tag,k,i,n):
        if 0<=i<n:
            if k>0:
                for cp in live[(tag,k-1,i)]: cp.wait_recv()
            if k<4:
                live[(tag,k,i)]=f(k,i)
                for cp in live[(tag,k,i)]: cp.start()
    for t in range(NCH+4*SP):
        for k in (4,3,2,1,0):
            go(wst,"w",k,t-k*SPW,5)
        if t==min(1,SP-1): loc.wait()
        for k in (4,3,2,1,0):
            go(st,"f",k,t-k*SP,NCH)
    for cps in live.values():
        for cp in cps: cp.wait_send()
def gather_call(s, ws):
    D=pltpu.SemaphoreType.DMA
    bf=jnp.bfloat16
    outs=[jax.ShapeDtypeStruct((NCH,4,3,2,2,2,64,128),bf)]+[jax.ShapeDtypeStruct((2,2,256,512),bf)]*4+[jax.ShapeDtypeStruct((2,2,128,1024),bf)]
    A=pl.BlockSpec(memory_space=pl.ANY)
    sem=[(NCH,3),(NCH,3),(NCH,2),(NCH,2),(NCH,2),(NCH,2),(NCH,),(NCH,),(5,),(5,),(5,3),(5,3),(5,),(5,),(5,),(5,)]
    return pl.pallas_call(gather_kernel,out_shape=outs,in_specs=[pl.BlockSpec(memory_space=pltpu.VMEM)]+[A]*5,out_specs=[A]*6,
        scratch_shapes=[D(v) for v in sem]+[D(())],
        compiler_params=pltpu.CompilerParams(collective_id=1,has_side_effects=True,vmem_limit_bytes=60<<20))(s,*ws)
def prep(fv,fg,fo):
    s=jnp.stack([fv,fg,fo.T])
    return s.reshape(3,64,NCH,128).transpose(2,0,1,3)
def wviews(wq,wk,wv,wg,wo):
    return [w.reshape(2,2,256,512) for w in (wq,wk,wv,wg)]+[wo.reshape(2,2,128,1024)]
def ffn_kernel(mid, go, midT, goT, W3, out, dm, sh, G, RD, R1A, R1B, R2A, R2B, Q, RZ, WT, wsem, ds, dr, xs, xr, ys, yr, zs, zr):
    z,x,c,y=place()
    zp=[lax.rem(z+r,4) for r in (1,2,3)]
    X=dev(z,1-x,c,y); Y=dev(z,x,c,1-y); C=dev(z,x,1-c,y)
    bar=pltpu.get_barrier_semaphore()
    peers=[dev(q,x,c,y) for q in zp]+[X,Y,C]
    for p in peers: pl.semaphore_signal(bar,inc=1,device_id=p,device_id_type=MESH)
    pl.semaphore_wait(bar,len(peers))
    def rc(src,dst,ss,rs,d): return pltpu.make_async_remote_copy(src_ref=src,dst_ref=dst,send_sem=ss,recv_sem=rs,device_id=d,device_id_type=MESH)
    def wload(i,s):
        return [pltpu.make_async_copy(W3.at[i,:,:,:,:,h],WT.at[s,:,:,:,:,:,pl.ds(h*128,128)],wsem.at[s,h]) for h in (0,1)]
    for cp in wload(0,0): cp.start()
    out[...]=jnp.zeros_like(out); dm[...]=jnp.zeros_like(dm)
    def cps(k,i):
        if k==0: return [rc(G.at[i,1-c],RD.at[i],ds.at[i],dr.at[i],C)]
        if k==1: return [rc(G.at[i,c,:,:,1-x,:,0:HR],R1A.at[i],xs.at[i,0],xr.at[i,0],X),
                         rc(G.at[i,c,:,:,:,1-y,HR:64],R1B.at[i],ys.at[i,0],yr.at[i,0],Y)]
        if k==2: return [rc(G.at[i,c,:,:,x,1-y,0:HR],R2A.at[i],ys.at[i,1],yr.at[i,1],Y),
                         rc(G.at[i,c,:,:,1-x,y,HR:64],R2B.at[i],xs.at[i,1],xr.at[i,1],X)]
        if k==3: return [rc(Q.at[i,:,q],RZ.at[i,n],zs.at[i,n],zr.at[i,n],dev(q,x,c,y)) for n,q in enumerate(zp)]
    def reduce(k,i):
        if k==1: G[i,c]=(G[i,c].astype(f32)+RD[i].astype(f32)).astype(bf)
        if k==2:
            G[i,c,:,:,x,:,0:HR]=(G[i,c,:,:,x,:,0:HR].astype(f32)+R1A[i].astype(f32)).astype(bf)
            G[i,c,:,:,:,y,HR:64]=(G[i,c,:,:,:,y,HR:64].astype(f32)+R1B[i].astype(f32)).astype(bf)
        if k==3:
            Q[i,:,:,0:HR]=(G[i,c,:,:,x,y,0:HR].astype(f32)+R2A[i].astype(f32)).astype(bf)
            Q[i,:,:,HR:64]=(G[i,c,:,:,x,y,HR:64].astype(f32)+R2B[i].astype(f32)).astype(bf)
        if k==4:
            v=Q[i,:,z].astype(f32)
            for n in range(3): v=v+RZ[i,n].astype(f32)
            sh[:,:,pl.ds(pl.multiple_of(i*128,128),128)]=v
    def stages(t):
        for k in (4,3,2,1,0):
            i=t-RS_AT[k]
            @pl.when((i>=0)&(i<NCH))
            def _():
                if k>0:
                    for cp in cps(k-1,i): cp.wait_recv()
                if k==1:
                    for cp in cps(0,i): cp.wait_send()
                reduce(k,i)
        for k in (3,2,1,0):
            i=t-RS_AT[k]
            @pl.when((i>=0)&(i<NCH))
            def _():
                for cp in cps(k,i): cp.start()
    def body(t,_):
        stages(t)
        @pl.when(t<NCH)
        def _():
            s=lax.rem(t,2)
            for cp in wload(t,s): cp.wait()
            @pl.when(t+1<NCH)
            def _():
                for cp in wload(t+1,1-s): cp.start()
            fv=WT[s,:,0].reshape(1024,256); fg=WT[s,:,1].reshape(1024,256); fo=WT[s,:,2].reshape(1024,256)
            m=mid[...]; g_=go[...]
            v=dot(m,fv); g=dot(m,fg); gh=dot(g_,fo)
            hid=(v*g).astype(bf); dv=(gh*g).astype(bf); dg=(gh*v).astype(bf)
            out[...]+=dotnt(hid,fo)
            dm[...]+=dotnt(dv,fv)+dotnt(dg,fg)
            for tt,(L,R) in enumerate(((midT,dv),(midT,dg),(goT,hid))):
                r=dot(L[...],R).astype(bf).reshape(4,2,2,64,256)
                for cc in (0,1):
                    for h in (0,1):
                        G[t,cc,tt,:,:,h]=r[:,:,cc,:,h*128:h*128+128]
        return 0
    lax.fori_loop(0,NCH+RS_AT[4],body,0)
    def drain(i,_):
        for k in (1,2,3):
            for cp in cps(k,i): cp.wait_send()
        return 0
    lax.fori_loop(0,NCH,drain,0)
def ffn_call(mid,go,midT,goT,W3):
    D=pltpu.SemaphoreType.DMA; V=pltpu.VMEM
    A=pl.BlockSpec(memory_space=pl.ANY); VM=pl.BlockSpec(memory_space=pltpu.VMEM)
    scr=[V((NCH,2,3,4,2,2,64,128),bf),V((NCH,3,4,2,2,64,128),bf),V((NCH,3,4,2,HR,128),bf),V((NCH,3,4,2,64-HR,128),bf),
         V((NCH,3,4,HR,128),bf),V((NCH,3,4,64-HR,128),bf),V((NCH,3,4,64,128),bf),V((NCH,3,3,64,128),bf),V((2,4,3,2,2,64,256),bf),
         D((2,2)),D((NCH,)),D((NCH,)),D((NCH,2)),D((NCH,2)),D((NCH,2)),D((NCH,2)),D((NCH,3)),D((NCH,3))]
    return pl.pallas_call(ffn_kernel,out_shape=[jax.ShapeDtypeStruct((512,1024),f32)]*2+[jax.ShapeDtypeStruct((3,64,1408),f32)],
        in_specs=[VM]*4+[A],out_specs=[VM]*3,scratch_shapes=scr,
        compiler_params=pltpu.CompilerParams(collective_id=2,has_side_effects=True,vmem_limit_bytes=67043328))(mid,go,midT,goT,W3)
def wg_kernel(LT, R, O, G, RD, RY, RX, Q, RZ, ds, dr, ys, yr, xs, xr, zs, zr, z2s, z2r, x2s, x2r, d2s, d2r):
    z,x,c,y=place()
    zp=[lax.rem(z+r,4) for r in (1,2,3)]
    X=dev(z,1-x,c,y); Y=dev(z,x,c,1-y); C=dev(z,x,1-c,y)
    bar=pltpu.get_barrier_semaphore()
    peers=[dev(q,x,c,y) for q in zp]+[X,Y,C]
    for p in peers: pl.semaphore_signal(bar,inc=1,device_id=p,device_id_type=MESH)
    pl.semaphore_wait(bar,len(peers))
    def rc(src,dst,ss,rs,d): return pltpu.make_async_remote_copy(src_ref=src,dst_ref=dst,send_sem=ss,recv_sem=rs,device_id=d,device_id_type=MESH)
    def cps(k,i):
        if k==0: return [rc(G.at[i,1-c],RD.at[i],ds.at[i],dr.at[i],C)]
        if k==1: return [rc(G.at[i,c,1],RY.at[i],ys.at[i],yr.at[i],Y)]
        if k==2: return [rc(G.at[i,c,0,:,1-x],RX.at[i],xs.at[i],xr.at[i],X)]
        if k==3: return [rc(Q.at[i,q],RZ.at[i,n],zs.at[i,n],zr.at[i,n],dev(q,x,c,y)) for n,q in enumerate(zp)]
        if k==4: return [rc(O.at[i,z,x,c],O.at[i,z,x,c],z2s.at[i,n],z2r.at[i,n],dev(q,x,c,y)) for n,q in enumerate(zp)]
        if k==5: return [rc(O.at[i,:,x,c],O.at[i,:,x,c],x2s.at[i],x2r.at[i],X)]
        if k==6: return [rc(O.at[i,:,:,c],O.at[i,:,:,c],d2s.at[i],d2r.at[i],C)]
    def reduce(k,i):
        if k==1: G[i,c]=(G[i,c].astype(f32)+RD[i].astype(f32)).astype(bf)
        if k==2: G[i,c,0]=(G[i,c,0].astype(f32)+RY[i].astype(f32)).astype(bf)
        if k==3: Q[i]=(G[i,c,0,:,x].astype(f32)+RX[i].astype(f32)).astype(bf)
        if k==4:
            v=Q[i,z].astype(f32)
            for n in range(3): v=v+RZ[i,n].astype(f32)
            O[i,z,x,c]=v.astype(bf)
    def stages(t):
        for k in range(7,-1,-1):
            i=t-WG_AT[k]
            @pl.when((i>=0)&(i<NPIECE))
            def _():
                if k>0:
                    for cp in cps(k-1,i): cp.wait_recv()
                if k==1:
                    for cp in cps(0,i): cp.wait_send()
                reduce(k,i)
        for k in range(6,-1,-1):
            i=t-WG_AT[k]
            @pl.when((i>=0)&(i<NPIECE))
            def _():
                for cp in cps(k,i): cp.start()
    def body(t,_):
        stages(t)
        @pl.when(t<NPIECE)
        def _():
            j=t//NP; pp=lax.rem(t,NP)
            L=LT[jnp.minimum(j,1)]
            for b in (0,1):
                r=dot(L,R[j,b,:,pl.ds(pl.multiple_of(pp*CW,128),CW)]).astype(bf).reshape(4,2,2,64,CW)
                for cc in (0,1): G[t,cc,b]=r[:,:,cc]
        return 0
    lax.fori_loop(0,NPIECE+WG_AT[7],body,0)
    def drain(i,_):
        for k in (1,2,3,4,5,6):
            for cp in cps(k,i): cp.wait_send()
        return 0
    lax.fori_loop(0,NPIECE,drain,0)
def wg_call(LT,R):
    D=pltpu.SemaphoreType.DMA; V=pltpu.VMEM
    VM=pl.BlockSpec(memory_space=pltpu.VMEM)
    scr=[V((NPIECE,2,2,4,2,64,CW),bf),V((NPIECE,2,4,2,64,CW),bf),V((NPIECE,4,2,64,CW),bf),V((NPIECE,4,64,CW),bf),V((NPIECE,4,64,CW),bf),V((NPIECE,3,64,CW),bf)]
    n=(NPIECE,); m=(NPIECE,3)
    scr+=[D(v) for v in (n,n,n,n,n,n,m,m,m,m,n,n,n,n)]
    return pl.pallas_call(wg_kernel,out_shape=jax.ShapeDtypeStruct((NPIECE,4,2,2,64,CW),bf),
        in_specs=[VM]*2,out_specs=VM,scratch_shapes=scr,
        compiler_params=pltpu.CompilerParams(collective_id=3,has_side_effects=True,vmem_limit_bytes=67043328))(LT,R)

def fast_body(tokens, lengths, decay, w_query, w_key, w_value, w_gate, w_out, f_value, f_gate, f_out, cotangent):
    own_rows = tokens.shape[0]
    y = lax.axis_index("head")
    swap = [(0, 1), (1, 0)]
    rates = jnp.concatenate([decay, lax.ppermute(decay, "head", swap)])
    within, first_decay, last_decay, _ = decay_tables(rates)
    positions = y * own_rows + jnp.arange(own_rows, dtype=jnp.int32)
    keep_rows = (positions < lengths[0]).astype(f32)[:, None]
    inputs_f = tokens.astype(f32)
    normed, scale_in = normalize(inputs_f)
    normed_low = normed.astype(bf)
    W3, *parts = gather_call(prep(f_value, f_gate, f_out), wviews(w_query, w_key, w_value, w_gate, w_out))
    pq, pk, pv, pg = [p.reshape(1024, 512) for p in parts[:4]]
    po = parts[4].reshape(512, 1024)
    two = lambda a, b: jnp.concatenate([matmul(normed_low, a), matmul(normed_low, b)], axis=1)
    query_pre, keys_pre, values_pre, gate_pre = two(w_query, pq), two(w_key, pk), two(w_value, pv), two(w_gate, pg)
    heads = lambda t: t.reshape(own_rows, 8, HD).transpose(1, 0, 2)
    flat = lambda t: t.transpose(1, 0, 2).reshape(own_rows, 8 * HD)
    query = heads(jax.nn.silu(query_pre).astype(bf))
    keys = heads(jax.nn.silu(keys_pre).astype(bf))
    values = heads(values_pre.astype(bf))
    ein = lambda form, a, b: jnp.einsum(form, a, b, preferred_element_type=f32)
    swapped = lambda t: lax.ppermute(jnp.concatenate([t[4:], t[:4]]).astype(bf), "head", swap)
    keys_last = (keys.astype(f32) * last_decay[:, :, None]).astype(bf)
    update = ein("htd,hte->hde", keys_last, values)
    state = swapped(update)
    state = jnp.where(y == 1, state, jnp.zeros_like(state))
    weights = (ein("htd,hrd->htr", query, keys) * within).astype(bf)
    mixed = flat(ein("htr,hrd->htd", weights, values) + first_decay[:, :, None] * ein("htd,hde->hte", query, state))
    scale_out = lax.rsqrt(jnp.mean(mixed * mixed, axis=1, keepdims=True) + epsilon)
    mixed_unit = mixed * scale_out
    gated = (mixed_unit * gate_pre).astype(bf)
    middle = inputs_f + matmul(gated[:, :512], w_out) + matmul(gated[:, 512:], po)
    mid_normed, scale_mid = normalize(middle)
    mid_low = mid_normed.astype(bf)
    grad_out = cotangent.astype(f32) * keep_rows
    grad_low = grad_out.astype(bf)
    ffn, d_mid_normed, shares = ffn_call(mid_low, grad_low, mid_low.T, grad_low.T, W3)
    output = ((middle + ffn) * keep_rows).astype(bf)
    grad_middle = grad_out + norm_back(d_mid_normed, mid_normed, scale_mid)
    gm = grad_middle.astype(bf)
    d_gated = jnp.concatenate([matmul_right_t(gm, w_out), matmul_right_t(gm, po)], axis=1)
    d_gate_pre = (d_gated * mixed_unit).astype(bf)
    d_unit = d_gated * gate_pre
    d_mixed = heads(norm_back(d_unit, mixed_unit, scale_out).astype(bf))
    grad_first = (d_mixed.astype(f32) * first_decay[:, :, None]).astype(bf)
    later = swapped(ein("htd,hte->hde", query, grad_first))
    later = jnp.where(y == 0, later, jnp.zeros_like(later))
    d_scores = (ein("htd,hrd->htr", d_mixed, values) * within).astype(bf)
    d_query = ein("htr,hrd->htd", d_scores, keys) + ein("hte,hde->htd", grad_first, state)
    d_keys = ein("htr,htd->hrd", d_scores, query) + last_decay[:, :, None] * ein("hte,hde->htd", values, later)
    d_values = ein("htr,htd->hrd", weights, d_mixed) + ein("htd,hde->hte", keys_last, later)
    d_query_pre = (flat(d_query) * silu_slope(query_pre)).astype(bf)
    d_keys_pre = (flat(d_keys) * silu_slope(keys_pre)).astype(bf)
    d_values_pre = flat(d_values).astype(bf)
    total = 0.0
    for d, own, part in ((d_query_pre, w_query, pq), (d_keys_pre, w_key, pk), (d_values_pre, w_value, pv), (d_gate_pre, w_gate, pg)):
        total = total + matmul_right_t(d[:, :512], own) + matmul_right_t(d[:, 512:], part)
    d_tokens = grad_middle + norm_back(total, normed, scale_in)
    right = jnp.stack([t[:, h * 512 : h * 512 + 512] for t in (gated, d_gate_pre, d_values_pre, d_keys_pre, d_query_pre) for h in (0, 1)]).reshape(5, 2, 512, 512)
    grads = wg_call(jnp.stack([gm.T, normed_low.T]), right)
    grads = grads.reshape(5, NP, 1024, CW).transpose(0, 2, 1, 3).reshape(5, 1024, 512).astype(f32)
    return (output, d_tokens, grads[4], grads[3], grads[2], grads[1], grads[0].T, shares[0], shares[1], shares[2].T)


def solution(mesh):
    placed = (
        P(("dp", "head"), None),
        P("dp"),
        P("head"),
        P(None, "head"),
        P(None, "head"),
        P(None, "head"),
        P(None, "head"),
        P("head", None),
        P("dp", "head"),
        P("dp", "head"),
        P("head", "dp"),
        P(("dp", "head"), None),
    )
    fast = mesh.shape["dp"] == 16 and mesh.shape["head"] == 2
    return jax.shard_map(
        fast_body if fast else general_body,
        mesh=mesh,
        in_specs=placed,
        out_specs=(
            P(("dp", "head"), None),
            P(("dp", "head"), None),
            P(None, "head"),
            P(None, "head"),
            P(None, "head"),
            P(None, "head"),
            P("head", None),
            P("dp", "head"),
            P("dp", "head"),
            P("head", "dp"),
        ),
        check_vma=False,
    )
```

```python
import jax
import jax.numpy as jnp
from jax import lax
from jax.experimental import pallas as pl
from jax.experimental.pallas import tpu as pltpu
from jax.sharding import PartitionSpec as P

D = 1024
HD = 128
SEQ_DEV = 1
SLOT = 1024
BLOCK = 512


epsilon = 1e-06


def normalize(values):
    factor = lax.rsqrt(jnp.mean(values * values, axis=-1, keepdims=True) + epsilon)
    return (values * factor, factor)


def norm_back(grad_normed, normed, factor):
    inner_sum = jnp.mean(grad_normed * normed, axis=-1, keepdims=True)
    return factor * (grad_normed - normed * inner_sum)


def silu_slope(values):
    sigmoid = jax.nn.sigmoid(values)
    return sigmoid * (1.0 + values * (1.0 - sigmoid))


def matmul(left_side, right_side):
    return jnp.dot(left_side, right_side, preferred_element_type=jnp.float32)


def matmul_right_t(left_side, right_side):
    return lax.dot_general(
        left_side, right_side, (((1,), (1,)), ((), ())), preferred_element_type=jnp.float32
    )


def matmul_left_t(left_side, right_side):
    return lax.dot_general(
        left_side, right_side, (((0,), (0,)), ((), ())), preferred_element_type=jnp.float32
    )


def exact(form, left_side, right_side):
    return jnp.einsum(form, left_side, right_side, precision=lax.Precision.HIGHEST)


def decay_tables(rates):
    offsets = jnp.arange(BLOCK).astype(jnp.float32)
    spread = offsets[:, None] - offsets[None, :]
    causal = spread >= 0
    within = jnp.where(
        causal[None], jnp.exp(-rates[:, None, None] * jnp.where(causal, spread, 0.0)[None]), 0.0
    )
    first_decay = jnp.exp(-rates[:, None] * (offsets[None, :] + 1.0))
    last_decay = jnp.exp(-rates[:, None] * (BLOCK - 1.0 - offsets[None, :]))
    block_decay = jnp.exp(-rates * BLOCK)
    return (within, first_decay, last_decay, block_decay)


def to_blocks(values, heads):
    shaped = values.reshape(SEQ_DEV, SLOT // BLOCK, BLOCK, heads, HD)
    return shaped.transpose(1, 0, 3, 2, 4)


def from_blocks(blocks):
    return blocks.transpose(1, 0, 3, 2, 4).reshape(-1, blocks.shape[2] * blocks.shape[4])


def lightning_forward(query, keys, values, tables):
    within, first_decay, last_decay, block_decay = tables

    def advance(carried, inputs):
        query_blk, keys_blk, values_blk = inputs
        scores = jnp.einsum(
            "shbd,shcd->shbc", query_blk, keys_blk, preferred_element_type=jnp.float32
        )
        weights = (scores * within[None]).astype(jnp.bfloat16)
        inner_sum = jnp.einsum(
            "shbc,shcd->shbd", weights, values_blk, preferred_element_type=jnp.float32
        )
        outer_sum = first_decay[None, :, :, None] * exact(
            "shbd,shde->shbe", query_blk.astype(jnp.float32), carried
        )
        keys_scaled = keys_blk.astype(jnp.float32) * last_decay[None, :, :, None]
        update = exact("shbd,shbe->shde", keys_scaled, values_blk.astype(jnp.float32))
        return (
            block_decay[None, :, None, None] * carried + update,
            (inner_sum + outer_sum, carried),
        )

    initial = jnp.zeros((SEQ_DEV, query.shape[2], HD, HD), jnp.float32)
    final_state, (mixed, states) = lax.scan(advance, initial, (query, keys, values))
    return (mixed, states)


def lightning_backward(query, keys, values, grads, states, tables):
    within, first_decay, last_decay, block_decay = tables

    def retreat(later_grad, inputs):
        query_blk, keys_blk, values_blk, grad_blk, carried = inputs
        scores = jnp.einsum(
            "shbd,shcd->shbc", query_blk, keys_blk, preferred_element_type=jnp.float32
        )
        weights = (scores * within[None]).astype(jnp.bfloat16)
        d_weights = jnp.einsum(
            "shbd,shcd->shbc", grad_blk, values_blk, preferred_element_type=jnp.float32
        )
        d_scores = (d_weights * within[None]).astype(jnp.bfloat16)
        d_query = jnp.einsum(
            "shbc,shcd->shbd", d_scores, keys_blk, preferred_element_type=jnp.float32
        )
        d_keys = jnp.einsum(
            "shbc,shbd->shcd", d_scores, query_blk, preferred_element_type=jnp.float32
        )
        d_values = jnp.einsum(
            "shbc,shbd->shcd", weights, grad_blk, preferred_element_type=jnp.float32
        )
        grad_scaled = grad_blk.astype(jnp.float32) * first_decay[None, :, :, None]
        keys_scaled = keys_blk.astype(jnp.float32) * last_decay[None, :, :, None]
        d_query = d_query + exact("shbe,shde->shbd", grad_scaled, carried)
        d_keys = d_keys + last_decay[None, :, :, None] * exact(
            "shbe,shde->shbd", values_blk.astype(jnp.float32), later_grad
        )
        d_values = d_values + exact("shbd,shde->shbe", keys_scaled, later_grad)
        earlier = block_decay[None, :, None, None] * later_grad + exact(
            "shbd,shbe->shde", query_blk.astype(jnp.float32), grad_scaled
        )
        return (earlier, (d_query, d_keys, d_values))

    initial = jnp.zeros((SEQ_DEV, query.shape[2], HD, HD), jnp.float32)
    first_grad, results = lax.scan(
        retreat, initial, (query, keys, values, grads, states), reverse=True
    )
    return results


def general_body(
    tokens,
    lengths,
    decay,
    w_query,
    w_key,
    w_value,
    w_gate,
    w_out,
    f_value,
    f_gate,
    f_out,
    cotangent,
):
    own_rows = tokens.shape[0]
    first_row = lax.axis_index("head") * own_rows
    heads_here = decay.shape[0]
    tables = decay_tables(decay)
    positions = first_row + jnp.arange(own_rows, dtype=jnp.int32)
    slot_match = (positions // SLOT)[:, None] == jnp.arange(SEQ_DEV, dtype=jnp.int32)[None, :]
    length_of = jnp.sum(jnp.where(slot_match, lengths[None, :], 0), axis=1)
    keep_rows = (positions % SLOT < length_of).astype(jnp.float32)[:, None]
    inputs_f = tokens.astype(jnp.float32)
    normed, scale_in = normalize(inputs_f)
    gathered = lax.all_gather(normed.astype(jnp.bfloat16), "head", axis=0, tiled=True)
    query_pre = matmul(gathered, w_query)
    keys_pre = matmul(gathered, w_key)
    values_pre = matmul(gathered, w_value)
    gate_pre = matmul(gathered, w_gate)
    query_blocks = to_blocks(jax.nn.silu(query_pre).astype(jnp.bfloat16), heads_here)
    keys_blocks = to_blocks(jax.nn.silu(keys_pre).astype(jnp.bfloat16), heads_here)
    values_blocks = to_blocks(values_pre.astype(jnp.bfloat16), heads_here)
    mixed_blocks, states = lightning_forward(query_blocks, keys_blocks, values_blocks, tables)
    mixed = from_blocks(mixed_blocks)
    squares = lax.psum(jnp.sum(mixed * mixed, axis=1), "head")
    scale_out = lax.rsqrt(squares / D + epsilon)[:, None]
    mixed_unit = mixed * scale_out
    gated = (mixed_unit * gate_pre).astype(jnp.bfloat16)
    branch = lax.psum_scatter(
        matmul(gated, w_out).astype(jnp.bfloat16), "head", scatter_dimension=0, tiled=True
    ).astype(jnp.float32)
    middle = inputs_f + branch
    mid_normed, scale_mid = normalize(middle)
    mid_all = lax.all_gather(mid_normed.astype(jnp.bfloat16), "head", axis=0, tiled=True)
    value_full, gate_full = (
        lax.all_gather(f_value, "dp", axis=0, tiled=True),
        lax.all_gather(f_gate, "dp", axis=0, tiled=True),
    )
    down_full = lax.all_gather(f_out, "dp", axis=1, tiled=True)
    value_ffn = matmul(mid_all, value_full)
    gate_ffn = matmul(mid_all, gate_full)
    hidden = (value_ffn * gate_ffn).astype(jnp.bfloat16)
    ffn_branch = lax.psum_scatter(
        matmul(hidden, down_full).astype(jnp.bfloat16), "head", scatter_dimension=0, tiled=True
    ).astype(jnp.float32)
    output = ((middle + ffn_branch) * keep_rows).astype(jnp.bfloat16)
    grad_out = cotangent.astype(jnp.float32) * keep_rows
    grad_all = lax.all_gather(grad_out.astype(jnp.bfloat16), "head", axis=0, tiled=True)
    grad_hidden = matmul_right_t(grad_all, down_full)
    d_value_ffn = (grad_hidden * gate_ffn).astype(jnp.bfloat16)
    d_gate_ffn = (grad_hidden * value_ffn).astype(jnp.bfloat16)
    d_mid_normed = lax.psum_scatter(
        (matmul_right_t(d_value_ffn, value_full) + matmul_right_t(d_gate_ffn, gate_full)).astype(
            jnp.bfloat16
        ),
        "head",
        scatter_dimension=0,
        tiled=True,
    ).astype(jnp.float32)
    grad_middle = grad_out + norm_back(d_mid_normed, mid_normed, scale_mid)
    joined = jnp.concatenate([d_value_ffn, d_gate_ffn], axis=1)
    hidden_here = hidden.shape[1]
    shares = lax.psum_scatter(
        jnp.concatenate(
            [matmul_left_t(mid_all, joined), matmul_left_t(grad_all, hidden)], axis=1
        ).astype(jnp.bfloat16),
        "dp",
        scatter_dimension=0,
        tiled=True,
    ).astype(jnp.float32)
    d_f_value = shares[:, :hidden_here]
    d_f_gate = shares[:, hidden_here : 2 * hidden_here]
    d_f_out = shares[:, 2 * hidden_here :].T
    grad_rows = lax.all_gather(grad_middle.astype(jnp.bfloat16), "head", axis=0, tiled=True)
    d_gated = matmul_right_t(grad_rows, w_out)
    d_w_out_local = matmul_left_t(gated, grad_rows)
    d_gate_pre = (d_gated * mixed_unit).astype(jnp.bfloat16)
    d_unit = d_gated * gate_pre
    inner_out = lax.psum(jnp.sum(d_unit * mixed_unit, axis=1), "head")
    d_mixed = (scale_out * (d_unit - mixed_unit * (inner_out / D)[:, None])).astype(jnp.bfloat16)
    d_query, d_keys, d_values = lightning_backward(
        query_blocks, keys_blocks, values_blocks, to_blocks(d_mixed, heads_here), states, tables
    )
    d_query_pre = (from_blocks(d_query) * silu_slope(query_pre)).astype(jnp.bfloat16)
    d_keys_pre = (from_blocks(d_keys) * silu_slope(keys_pre)).astype(jnp.bfloat16)
    d_values_pre = from_blocks(d_values).astype(jnp.bfloat16)
    total = matmul_right_t(d_query_pre, w_query) + matmul_right_t(d_keys_pre, w_key)
    d_normed = lax.psum_scatter(
        (total + matmul_right_t(d_values_pre, w_value) + matmul_right_t(d_gate_pre, w_gate)).astype(
            jnp.bfloat16
        ),
        "head",
        scatter_dimension=0,
        tiled=True,
    ).astype(jnp.float32)
    d_tokens = grad_middle + norm_back(d_normed, normed, scale_in)
    grads_attention = (
        lax.psum(matmul_left_t(gathered, d_query_pre).astype(jnp.bfloat16), "dp").astype(
            jnp.float32
        ),
        lax.psum(matmul_left_t(gathered, d_keys_pre).astype(jnp.bfloat16), "dp").astype(
            jnp.float32
        ),
        lax.psum(matmul_left_t(gathered, d_values_pre).astype(jnp.bfloat16), "dp").astype(
            jnp.float32
        ),
        lax.psum(matmul_left_t(gathered, d_gate_pre).astype(jnp.bfloat16), "dp").astype(
            jnp.float32
        ),
        lax.psum(d_w_out_local.astype(jnp.bfloat16), "dp").astype(jnp.float32),
    )
    return (
        output,
        d_tokens,
        grads_attention[0],
        grads_attention[1],
        grads_attention[2],
        grads_attention[3],
        grads_attention[4],
        d_f_value,
        d_f_gate,
        d_f_out,
    )


MESH = pl.DeviceIdType.MESH
NCH = 11
RA = 16
HR = 32
SP = 2
SPW = 2
NWG = 20
NALL = NCH + NWG
RS_AT = (1, 2, 4, 6, 8)
AG_AT = (10, 12, 14)
TN = (((0,), (0,)), ((), ()))
bf = jnp.bfloat16
f32 = jnp.float32
NT = (((1,), (1,)), ((), ()))


def dot(a, b):
    return jnp.dot(a, b, preferred_element_type=f32)


def dotnt(a, b):
    return lax.dot_general(a, b, NT, preferred_element_type=f32)


def dottn(a, b):
    return lax.dot_general(a, b, TN, preferred_element_type=f32)


def place():
    d=lax.axis_index("dp")
    return d//4, (d//2)%2, d%2, lax.axis_index("head")
def dev(z,x,c,y): return ((z*2+x)*2+c, y)
def gather_kernel(s_ref, wq, wk, wv, wg, wo, W3, pq, pk, pv, pg, po, zs, zr, xs, xr, ys, yr, ds, dr, wys, wyr, wzs, wzr, wxs, wxr, wds, wdr, ls):
    z,x,c,y=place()
    zp=[lax.rem(z+r,4) for r in (1,2,3)]
    bar=pltpu.get_barrier_semaphore()
    peers=[dev(q,x,c,y) for q in zp]+[dev(z,1-x,c,y),dev(z,x,1-c,y),dev(z,x,c,1-y)]
    for p in peers: pl.semaphore_signal(bar,inc=1,device_id=p,device_id_type=MESH)
    pl.semaphore_wait(bar,len(peers))
    X=dev(z,1-x,c,y); Y=dev(z,x,c,1-y); C=dev(z,x,1-c,y)
    col=pl.ds(pl.multiple_of(y*128,128),128)
    own=[wq,wk,wv,wg,wo]; par=[pq,pk,pv,pg,po]
    def rc(src,dst,ss,rs,d): return pltpu.make_async_remote_copy(src_ref=src,dst_ref=dst,send_sem=ss,recv_sem=rs,device_id=d,device_id_type=MESH)
    loc=pltpu.make_async_copy(s_ref, W3.at[:,z,:,x,c,y], ls)
    loc.start()
    def st(k,i):
        if k==0:
            o=[]
            for n,q in enumerate(zp):
                t=W3.at[i,z,:,x,c,y]
                o.append(rc(s_ref.at[i],t,zs.at[i,n],zr.at[i,n],dev(q,x,c,y)))
            return o
        if k==1:
            a=W3.at[i,:,:,x,c,y,0:RA]; b=W3.at[i,:,:,x,c,y,RA:64]
            return [rc(a,a,xs.at[i,0],xr.at[i,0],X), rc(b,b,ys.at[i,0],yr.at[i,0],Y)]
        if k==2:
            a=W3.at[i,:,:,:,c,y,0:RA]; b=W3.at[i,:,:,x,c,:,RA:64]
            return [rc(b,b,xs.at[i,1],xr.at[i,1],X), rc(a,a,ys.at[i,1],yr.at[i,1],Y)]
        if k==3:
            a=W3.at[i,:,:,:,c]
            return [rc(a,a,ds.at[i],dr.at[i],C)]
    zb=lax.rem(z,2); ZP=dev(z+1-2*zb,x,c,y)
    def wst(k,j):
        if k==0: return [rc(own[j].at[zb,c],par[j].at[zb,c],wys.at[j],wyr.at[j],Y)]
        if k==1:
            a=par[j].at[zb,c]
            return [rc(a,a,wxs.at[j],wxr.at[j],ZP)]
        if k==2:
            a=par[j].at[:,c]
            return [rc(a,a,wds.at[j],wdr.at[j],C)]
        return []
    live={}
    def go(f,tag,k,i,n):
        if 0<=i<n:
            if k>0:
                for cp in live[(tag,k-1,i)]: cp.wait_recv()
            if k<4:
                live[(tag,k,i)]=f(k,i)
                for cp in live[(tag,k,i)]: cp.start()
    for t in range(NCH+4*SP):
        for k in (4,3,2,1,0):
            go(wst,"w",k,t-k*SPW,5)
        if t==min(1,SP-1): loc.wait()
        for k in (4,3,2,1,0):
            go(st,"f",k,t-k*SP,NCH)
    for cps in live.values():
        for cp in cps: cp.wait_send()
def gather_call(s, ws):
    D=pltpu.SemaphoreType.DMA
    bf=jnp.bfloat16
    outs=[jax.ShapeDtypeStruct((NCH,4,3,2,2,2,64,128),bf)]+[jax.ShapeDtypeStruct((2,2,256,512),bf)]*4+[jax.ShapeDtypeStruct((2,2,128,1024),bf)]
    A=pl.BlockSpec(memory_space=pl.ANY)
    sem=[(NCH,3),(NCH,3),(NCH,2),(NCH,2),(NCH,2),(NCH,2),(NCH,),(NCH,),(5,),(5,),(5,3),(5,3),(5,),(5,),(5,),(5,)]
    return pl.pallas_call(gather_kernel,out_shape=outs,in_specs=[pl.BlockSpec(memory_space=pltpu.VMEM)]+[A]*5,out_specs=[A]*6,
        scratch_shapes=[D(v) for v in sem]+[D(())],
        compiler_params=pltpu.CompilerParams(collective_id=1,has_side_effects=True,vmem_limit_bytes=60<<20))(s,*ws)
def prep(fv,fg,fo):
    s=jnp.stack([fv,fg,fo.T])
    return s.reshape(3,64,NCH,128).transpose(2,0,1,3)
def wviews(wq,wk,wv,wg,wo):
    return [w.reshape(2,2,256,512) for w in (wq,wk,wv,wg)]+[wo.reshape(2,2,128,1024)]
def backward_kernel(mid, go, rates, scal, state, W3, middle, gate, unit, gated, qpre, kpre, vals, normed, wq, wk, wv, wg, wo, pq, pk, pv, pg, po,
                    output, dtok, sh, O,
                    G, RD, R1, R2, Q, RZ, FN, WT, LT, ACC, DV, R, UN, NM, DMX, WB, WO, GS, GR,
                    wsem, lsem, bsem, gss, gsr, ds, dr, xs, xr, ys, yr, zs, zr, az_s, az_r, ax_s, ax_r, ad_s, ad_r, fl):
    z, x, c, y = place()
    zp = [lax.rem(z + r, 4) for r in (1, 2, 3)]
    X, Y, C = dev(z, 1 - x, c, y), dev(z, x, c, 1 - y), dev(z, x, 1 - c, y)
    bar = pltpu.get_barrier_semaphore()
    peers = [dev(q, x, c, y) for q in zp] + [X, Y, C]
    for p in peers:
        pl.semaphore_signal(bar, inc=1, device_id=p, device_id_type=MESH)

    def rc(src, dst, ss, rs, d):
        return pltpu.make_async_remote_copy(src_ref=src, dst_ref=dst, send_sem=ss, recv_sem=rs, device_id=d, device_id_type=MESH)

    def wload(i, s):
        return [pltpu.make_async_copy(W3.at[i, :, :, :, :, h], WT.at[s, :, :, :, :, :, pl.ds(h * 128, 128)], wsem.at[s, h]) for h in (0, 1)]

    loads = [pltpu.make_async_copy(a, b, lsem.at[n]) for n, (a, b) in enumerate(
        [(middle, ACC), (gated, R.at[0]), (gate, R.at[1]), (vals, R.at[2]), (kpre, R.at[3]), (qpre, R.at[4]), (unit, UN), (normed, NM), (wo, WO.at[0]), (po, WO.at[1])])]
    for cp in wload(0, 0):
        cp.start()
    for cp in loads:
        cp.start()
    mats = (wg, pg, wv, pv, wk, pk, wq, pq)

    def wbload(n):
        return pltpu.make_async_copy(mats[n], WB.at[n % 2], bsem.at[n % 2])

    wbload(0).start()
    wbload(1).start()
    LT[0] = mid[...].T
    LT[1] = go[...].T
    dtok[...] = jnp.zeros_like(dtok)
    loads[0].wait()
    pl.semaphore_wait(bar, len(peers))

    def cps(k, i, hr):
        g, s, n = lax.rem(i, NCH), lax.rem(i, 4), 3 if hr else 1
        if k == 0:
            return [rc(G.at[g, 1 - c, 0:n], RD.at[lax.rem(i, 2), 0:n], ds.at[i], dr.at[i], C)]
        if k == 1:
            o = [rc(G.at[g, c, 0:n, :, :, 1 - y, hr:64], R1.at[s, 0:n, :, :, hr:64], ys.at[i, 0], yr.at[i, 0], Y)]
            if hr:
                o.append(rc(G.at[g, c, 0:n, :, 1 - x, :, 0:hr], R1.at[s, 0:n, :, :, 0:hr], xs.at[i, 0], xr.at[i, 0], X))
            return o
        if k == 2:
            o = [rc(G.at[g, c, 0:n, :, 1 - x, y, hr:64], R2.at[s, 0:n, :, hr:64], xs.at[i, 1], xr.at[i, 1], X)]
            if hr:
                o.append(rc(G.at[g, c, 0:n, :, x, 1 - y, 0:hr], R2.at[s, 0:n, :, 0:hr], ys.at[i, 1], yr.at[i, 1], Y))
            return o
        if k == 3:
            return [rc(Q.at[s, 0:n, q], RZ.at[s, m, 0:n], zs.at[i, m], zr.at[i, m], dev(q, x, c, y)) for m, q in enumerate(zp)]

    def ags(k, w):
        if k == 0:
            f = FN.at[lax.rem(w, 4)]
            return [rc(f, O.at[w, z, x, c], az_s.at[w, n], az_r.at[w, n], dev(q, x, c, y)) for n, q in enumerate(zp)]
        if k == 1:
            return [rc(O.at[w, :, x, c], O.at[w, :, x, c], ax_s.at[w], ax_r.at[w], X)]
        if k == 2:
            return [rc(O.at[w, :, :, c], O.at[w, :, :, c], ad_s.at[w], ad_r.at[w], C)]

    def flush(w):
        return pltpu.make_async_copy(FN.at[lax.rem(w, 4)], O.at[w, z, x, c], fl.at[w])

    def reduce(k, i, hr):
        g, s, n = lax.rem(i, NCH), lax.rem(i, 4), 3 if hr else 1
        up = lambda v: v.astype(f32)
        if k == 1:
            G[g, c, 0:n] = (up(G[g, c, 0:n]) + up(RD[lax.rem(i, 2), 0:n])).astype(bf)
        if k == 2:
            if hr:
                G[g, c, 0:n, :, x, :, 0:hr] = (up(G[g, c, 0:n, :, x, :, 0:hr]) + up(R1[s, 0:n, :, :, 0:hr])).astype(bf)
            G[g, c, 0:n, :, :, y, hr:64] = (up(G[g, c, 0:n, :, :, y, hr:64]) + up(R1[s, 0:n, :, :, hr:64])).astype(bf)
        if k == 3:
            Q[s, 0:n] = (up(G[g, c, 0:n, :, x, y]) + up(R2[s, 0:n])).astype(bf)
        if k == 4:
            v = up(Q[s, 0:n, z])
            for m in range(3):
                v = v + up(RZ[s, m, 0:n])
            if hr:
                sh[:, :, pl.ds(pl.multiple_of(i * 128, 128), 128)] = v
            else:
                FN[lax.rem(i - NCH, 4)] = v[0].astype(bf)

    def arrive(k, i, hr):
        if k > 0:
            for cp in cps(k - 1, i, hr):
                cp.wait_recv()
        if k == 1:
            for cp in cps(0, i, hr):
                cp.wait_send()
        if k == 4:
            for kk in (1, 2, 3):
                for cp in cps(kk, i, hr):
                    cp.wait_send()
        reduce(k, i, hr)

    def leave(k, i, hr):
        for cp in cps(k, i, hr):
            cp.start()

    def both(f, k, t):
        i = t - RS_AT[k]

        @pl.when((i >= 0) & (i < NCH))
        def _():
            f(k, i, HR)

        @pl.when((i >= NCH) & (i < NALL))
        def _():
            f(k, i, 0)

    def ag_arrive(k, t):
        w = t - AG_AT[k] - NCH

        @pl.when((w >= 0) & (w < NWG))
        def _():
            for cp in ags(k, w):
                cp.wait_recv()
            if k == 0:
                for cp in ags(0, w):
                    cp.wait_send()
                flush(w).wait()

    def ag_leave(k, t):
        w = t - (AG_AT[k - 1] if k else RS_AT[4]) - NCH

        @pl.when((w >= 0) & (w < NWG))
        def _():
            for cp in ags(k, w):
                cp.start()
            if k == 0:
                flush(w).start()

    def stages(t):
        ag_arrive(2, t)
        ag_arrive(1, t)
        ag_arrive(0, t)
        ag_leave(2, t)
        both(arrive, 4, t)
        ag_leave(1, t)
        both(arrive, 3, t)
        ag_leave(0, t)
        both(arrive, 2, t)
        both(leave, 3, t)
        both(arrive, 1, t)
        for k in (2, 1, 0):
            both(leave, k, t)

    def store(g, t, r, own):
        r = r.astype(bf).reshape(4, 2, 2, 64, 256)
        for cc in (0, 1):
            G[g, cc, t, :, :, own] = r[:, :, cc, :, 0:128]
            G[g, cc, t, :, :, 1 - own] = r[:, :, cc, :, 128:256]

    def ffn(t):
        s = lax.rem(t, 2)
        for cp in wload(t, s):
            cp.wait()

        @pl.when(t + 1 < NCH)
        def _():
            for cp in wload(t + 1, 1 - s):
                cp.start()

        fv, fg, fo = [WT[s, :, n].reshape(1024, 256) for n in range(3)]
        m, g_ = mid[...], go[...]
        v, g, gh = dot(m, fv), dot(m, fg), dot(g_, fo)
        hid, dv, dg = (v * g).astype(bf), (gh * g).astype(bf), (gh * v).astype(bf)
        ACC[...] += dotnt(hid, fo)
        dtok[...] += dotnt(dv, fv) + dotnt(dg, fg)
        store(t, 0, dot(LT[0], dv), 0)
        store(t, 1, dot(LT[0], dg), 0)
        store(t, 2, dot(LT[1], hid), 0)

    def ffn_tick(t, _):
        stages(t)

        def one(n, _):
            ffn(n)
            return 0

        lax.fori_loop(jnp.maximum(2 * t - 1, 0), jnp.minimum(2 * t + 1, NCH), one, 0)
        return 0

    T = 6
    lax.fori_loop(0, T, ffn_tick, 0)
    stages(T)
    for cp in loads[1:]:
        cp.wait()
    keep, scale_mid, scale_out, scale_in = [scal[:, n : n + 1] for n in range(4)]
    output[...] = (ACC[...] * keep).astype(bf)
    n2 = mid[...].astype(f32)
    dm = dtok[...]
    gm = go[...].astype(f32) + scale_mid * (dm - n2 * jnp.mean(dm * n2, axis=1, keepdims=True))
    dtok[...] = gm
    gml = gm.astype(bf)
    LT[0] = gml.T
    LT[1] = NM[...].T
    for h in (0, 1):
        cols = slice(h * 512, h * 512 + 512)
        ACC[:, cols] = dotnt(gml, WO[h])
    dgt, un = ACC[...], UN[...].astype(f32)
    du = dgt * R[1].astype(f32)
    R[1] = (dgt * un).astype(bf)
    DMX[...] = (scale_out * (du - un * jnp.mean(du * un, axis=1, keepdims=True))).astype(bf)

    def head(h):
        return pl.ds(pl.multiple_of(h * 128, 128), 128)

    def silu(v):
        return v * jax.nn.sigmoid(v)

    tau = lax.broadcasted_iota(jnp.int32, (512, 1), 0).astype(f32)
    rho = lax.broadcasted_iota(jnp.int32, (1, 512), 1).astype(f32)

    def first(h, _):
        hs = head(h)
        q = silu(R[4, :, hs].astype(f32)).astype(bf)
        gf = (DMX[:, hs].astype(f32) * jnp.exp(-rates[h] * (tau + 1.0))).astype(bf)
        GS[lax.rem(h + 4, 8)] = dottn(q, gf).astype(bf)
        return 0

    lax.fori_loop(0, 8, first, 0)
    stages(T + 1)
    later = rc(GS, GR, gss, gsr, Y)
    later.start()
    ti = lax.broadcasted_iota(jnp.int32, (512, 512), 0)
    ri = lax.broadcasted_iota(jnp.int32, (512, 512), 1)

    def pair(h, _):
        hs = head(h)
        qp, kp = R[4, :, hs].astype(f32), R[3, :, hs].astype(f32)
        q, k, v, dmx = silu(qp).astype(bf), silu(kp).astype(bf), R[2, :, hs], DMX[:, hs]
        cf, rf = jnp.exp(-rates[h] * (tau + 1.0)), jnp.exp(rates[h] * (rho + 1.0))
        within = jnp.where(ti >= ri, cf * rf, 0.0)
        wt = (dotnt(q, k) * within).astype(bf)
        dsc = (dotnt(dmx, v) * within).astype(bf)
        gf = (dmx.astype(f32) * cf).astype(bf)
        dq = dot(dsc, k) + dotnt(gf, state[h])
        ACC[:, hs] = dottn(dsc, q)
        DV[:, hs] = dottn(wt, dmx)
        sq = jax.nn.sigmoid(qp)
        R[4, :, hs] = (dq * (sq * (1.0 + qp * (1.0 - sq)))).astype(bf)
        return 0

    stages(T + 2)
    lax.fori_loop(0, 4, pair, 0)
    stages(T + 3)
    lax.fori_loop(4, 8, pair, 0)
    stages(T + 4)
    later.wait()
    live = (y == 0).astype(f32)

    def finish(h, _):
        hs = head(h)
        gin = (GR[h].astype(f32) * live).astype(bf)
        kp = R[3, :, hs].astype(f32)
        sk = jax.nn.sigmoid(kp)
        k = (kp * sk).astype(bf)
        lf = jnp.exp(-rates[h] * (511.0 - tau))
        kl = (k.astype(f32) * lf).astype(bf)
        dk = ACC[:, hs] + lf * dotnt(R[2, :, hs], gin)
        R[2, :, hs] = (DV[:, hs] + dot(kl, gin)).astype(bf)
        R[3, :, hs] = (dk * (sk * (1.0 + kp * (1.0 - sk)))).astype(bf)
        return 0

    lax.fori_loop(0, 8, finish, 0)
    def wgrad(p):
        j, cp = p // 4, lax.rem(p, 4)
        lo = pl.multiple_of(cp * 128, 128)
        rr = jnp.concatenate([R[j, :, pl.ds(lo, 128)], R[j, :, pl.ds(lo + 512, 128)]], axis=1)
        store(lax.rem(p, NCH), 0, dot(LT[jnp.minimum(j, 1)], rr), y)

    def wg_tick(t, _):
        stages(t)
        p = t - NCH
        wgrad(p)
        for n in range(8):
            @pl.when(p == n)
            def _():
                wbload(n).wait()

        @pl.when(p < 8)
        def _():
            j, h = 1 + p // 2, lax.rem(p, 2)
            part = dotnt(R[j, :, pl.ds(pl.multiple_of(h * 512, 128), 512)], WB[h])
            ACC[...] = jnp.where(p == 0, 0.0, ACC[...]) + part

        for n in range(6):
            @pl.when(p == n)
            def _():
                wbload(n + 2).start()

        @pl.when(p == 8)
        def _():
            n1 = NM[...].astype(f32)
            dn = ACC[...]
            dtok[...] = dtok[...] + scale_in * (dn - n1 * jnp.mean(dn * n1, axis=1, keepdims=True))

        return 0

    lax.fori_loop(NCH, NCH + NWG, wg_tick, 0)
    def tail(t, _):
        stages(t)
        return 0

    lax.fori_loop(NALL, NALL + AG_AT[2], tail, 0)

    def drain(w, _):
        for k in (1, 2):
            for cp in ags(k, w):
                cp.wait_send()
        return 0

    lax.fori_loop(0, NWG, drain, 0)


def backward_call(mid, go, rates, scal, state, *rest):
    D, V = pltpu.SemaphoreType.DMA, pltpu.VMEM
    A, VM = pl.BlockSpec(memory_space=pl.ANY), pl.BlockSpec(memory_space=pltpu.VMEM)
    act = (512, 1024)
    scratch = [V((NCH, 2, 3, 4, 2, 2, 64, 128), bf), V((2, 3, 4, 2, 2, 64, 128), bf),
               V((4, 3, 4, 2, 64, 128), bf), V((4, 3, 4, 64, 128), bf),
               V((4, 3, 4, 64, 128), bf), V((4, 3, 3, 64, 128), bf), V((4, 64, 128), bf), V((2, 4, 3, 2, 2, 64, 256), bf),
               V((2, 1024, 512), bf), V(act, f32), V(act, f32), V((5,) + act, bf), V(act, bf), V(act, bf), V(act, bf),
               V((2, 1024, 512), bf), V((2, 512, 1024), bf), V((8, 128, 128), bf), V((8, 128, 128), bf)]
    n = NALL
    scratch += [D(s) for s in ((2, 2), (10,), (2,), (), (), (n,), (n,), (n, 2), (n, 2), (n, 2), (n, 2), (n, 3), (n, 3),
                               (NWG, 3), (NWG, 3), (NWG,), (NWG,), (NWG,), (NWG,), (NWG,))]
    S = jax.ShapeDtypeStruct
    return pl.pallas_call(
        backward_kernel,
        out_shape=[S(act, bf), S(act, f32), S((3, 64, 1408), f32), S((NWG, 4, 2, 2, 64, 128), bf)],
        in_specs=[VM] * 2 + [pl.BlockSpec(memory_space=pltpu.SMEM)] + [VM] * 2 + [A] * 19,
        out_specs=[VM] * 3 + [A],
        scratch_shapes=scratch,
        compiler_params=pltpu.CompilerParams(collective_id=2, has_side_effects=True, vmem_limit_bytes=67043328),
    )(mid, go, rates, scal, state, *rest)
def finish_kernel(o, sh, d_query, d_key, d_value, d_gate, d_out, d_f_value, d_f_gate, d_f_out):
    for n in range(4):
        cols = slice(n * 128, n * 128 + 128)
        d_out[cols, :] = o[n].astype(f32).T
        d_gate[:, cols] = o[4 + n].astype(f32)
        d_value[:, cols] = o[8 + n].astype(f32)
        d_key[:, cols] = o[12 + n].astype(f32)
        d_query[:, cols] = o[16 + n].astype(f32)

    @pl.when(pl.program_id(0) == 0)
    def _():
        d_f_value[...] = sh[0]
        d_f_gate[...] = sh[1]
        d_f_out[...] = sh[2].T


def finish_call(o, sh):
    S = jax.ShapeDtypeStruct
    whole = lambda *s: pl.BlockSpec(s, lambda i: (0,) * len(s))
    return pl.pallas_call(
        finish_kernel,
        grid=(4,),
        out_shape=[S((1024, 512), f32)] * 4 + [S((512, 1024), f32)] + [S((64, 1408), f32)] * 2 + [S((1408, 64), f32)],
        in_specs=[pl.BlockSpec((20, 256, 128), lambda i: (0, i, 0)), whole(3, 64, 1408)],
        out_specs=[pl.BlockSpec((256, 512), lambda i: (i, 0))] * 4 + [pl.BlockSpec((512, 256), lambda i: (0, i))] + [whole(64, 1408)] * 2 + [whole(1408, 64)],
        compiler_params=pltpu.CompilerParams(vmem_limit_bytes=48 << 20),
    )(o, sh)

def fast_body(tokens, lengths, decay, w_query, w_key, w_value, w_gate, w_out, f_value, f_gate, f_out, cotangent):
    own_rows = tokens.shape[0]
    y = lax.axis_index("head")
    swap = [(0, 1), (1, 0)]
    rates = jnp.concatenate([decay, lax.ppermute(decay, "head", swap)])
    within, first_decay, last_decay, _ = decay_tables(rates)
    positions = y * own_rows + jnp.arange(own_rows, dtype=jnp.int32)
    keep_rows = (positions < lengths[0]).astype(f32)[:, None]
    inputs_f = tokens.astype(f32)
    normed, scale_in = normalize(inputs_f)
    normed_low = normed.astype(bf)
    W3, *parts = gather_call(prep(f_value, f_gate, f_out), wviews(w_query, w_key, w_value, w_gate, w_out))
    pq, pk, pv, pg = [p.reshape(1024, 512) for p in parts[:4]]
    po = parts[4].reshape(512, 1024)
    two = lambda a, b: jnp.concatenate([matmul(normed_low, a), matmul(normed_low, b)], axis=1)
    query_pre, keys_pre, values_pre, gate_pre = two(w_query, pq), two(w_key, pk), two(w_value, pv), two(w_gate, pg)
    heads = lambda t: t.reshape(own_rows, 8, HD).transpose(1, 0, 2)
    flat = lambda t: t.transpose(1, 0, 2).reshape(own_rows, 8 * HD)
    query = heads(jax.nn.silu(query_pre).astype(bf))
    keys = heads(jax.nn.silu(keys_pre).astype(bf))
    values = heads(values_pre.astype(bf))
    ein = lambda form, a, b: jnp.einsum(form, a, b, preferred_element_type=f32)
    swapped = lambda t: lax.ppermute(jnp.concatenate([t[4:], t[:4]]).astype(bf), "head", swap)
    keys_last = (keys.astype(f32) * last_decay[:, :, None]).astype(bf)
    update = ein("htd,hte->hde", keys_last, values)
    state = swapped(update)
    state = jnp.where(y == 1, state, jnp.zeros_like(state))
    weights = (ein("htd,hrd->htr", query, keys) * within).astype(bf)
    mixed = flat(ein("htr,hrd->htd", weights, values) + first_decay[:, :, None] * ein("htd,hde->hte", query, state))
    scale_out = lax.rsqrt(jnp.mean(mixed * mixed, axis=1, keepdims=True) + epsilon)
    mixed_unit = mixed * scale_out
    gated = (mixed_unit * gate_pre).astype(bf)
    middle = inputs_f + matmul(gated[:, :512], w_out) + matmul(gated[:, 512:], po)
    mid_normed, scale_mid = normalize(middle)
    mid_low = mid_normed.astype(bf)
    grad_out = cotangent.astype(f32) * keep_rows
    grad_low = grad_out.astype(bf)
    scal = jnp.concatenate([keep_rows, scale_mid, scale_out, scale_in], axis=1)
    view = lambda p: p.reshape(1024, 512)
    output, d_tokens, shares, grads = backward_call(
        mid_low, grad_low, rates, scal, state, W3, middle, gate_pre.astype(bf), mixed_unit.astype(bf), gated,
        query_pre.astype(bf), keys_pre.astype(bf), values_pre.astype(bf), normed_low,
        w_query, w_key, w_value, w_gate, w_out, pq, pk, pv, pg, po)
    d_query, d_key, d_value, d_gate, d_out, d_f_value, d_f_gate, d_f_out = finish_call(grads.reshape(NWG, 1024, 128), shares)
    return (output, d_tokens, d_query, d_key, d_value, d_gate, d_out, d_f_value, d_f_gate, d_f_out)


def solution(mesh):
    placed = (
        P(("dp", "head"), None),
        P("dp"),
        P("head"),
        P(None, "head"),
        P(None, "head"),
        P(None, "head"),
        P(None, "head"),
        P("head", None),
        P("dp", "head"),
        P("dp", "head"),
        P("head", "dp"),
        P(("dp", "head"), None),
    )
    fast = mesh.shape["dp"] == 16 and mesh.shape["head"] == 2
    return jax.shard_map(
        fast_body if fast else general_body,
        mesh=mesh,
        in_specs=placed,
        out_specs=(
            P(("dp", "head"), None),
            P(("dp", "head"), None),
            P(None, "head"),
            P(None, "head"),
            P(None, "head"),
            P(None, "head"),
            P("head", None),
            P("dp", "head"),
            P("dp", "head"),
            P("head", "dp"),
        ),
        check_vma=False,
    )
```

```python
import jax
import jax.numpy as jnp
from jax import lax
from jax.experimental import pallas as pl
from jax.experimental.pallas import tpu as pltpu
from jax.sharding import PartitionSpec as P

D = 1024
HD = 128
SEQ_DEV = 1
SLOT = 1024
BLOCK = 512


epsilon = 1e-06


def normalize(values):
    factor = lax.rsqrt(jnp.mean(values * values, axis=-1, keepdims=True) + epsilon)
    return (values * factor, factor)


def norm_back(grad_normed, normed, factor):
    inner_sum = jnp.mean(grad_normed * normed, axis=-1, keepdims=True)
    return factor * (grad_normed - normed * inner_sum)


def silu_slope(values):
    sigmoid = jax.nn.sigmoid(values)
    return sigmoid * (1.0 + values * (1.0 - sigmoid))


def matmul(left_side, right_side):
    return jnp.dot(left_side, right_side, preferred_element_type=jnp.float32)


def matmul_right_t(left_side, right_side):
    return lax.dot_general(
        left_side, right_side, (((1,), (1,)), ((), ())), preferred_element_type=jnp.float32
    )


def matmul_left_t(left_side, right_side):
    return lax.dot_general(
        left_side, right_side, (((0,), (0,)), ((), ())), preferred_element_type=jnp.float32
    )


def exact(form, left_side, right_side):
    return jnp.einsum(form, left_side, right_side, precision=lax.Precision.HIGHEST)


def decay_tables(rates):
    offsets = jnp.arange(BLOCK).astype(jnp.float32)
    spread = offsets[:, None] - offsets[None, :]
    causal = spread >= 0
    within = jnp.where(
        causal[None], jnp.exp(-rates[:, None, None] * jnp.where(causal, spread, 0.0)[None]), 0.0
    )
    first_decay = jnp.exp(-rates[:, None] * (offsets[None, :] + 1.0))
    last_decay = jnp.exp(-rates[:, None] * (BLOCK - 1.0 - offsets[None, :]))
    block_decay = jnp.exp(-rates * BLOCK)
    return (within, first_decay, last_decay, block_decay)


def to_blocks(values, heads):
    shaped = values.reshape(SEQ_DEV, SLOT // BLOCK, BLOCK, heads, HD)
    return shaped.transpose(1, 0, 3, 2, 4)


def from_blocks(blocks):
    return blocks.transpose(1, 0, 3, 2, 4).reshape(-1, blocks.shape[2] * blocks.shape[4])


def lightning_forward(query, keys, values, tables):
    within, first_decay, last_decay, block_decay = tables

    def advance(carried, inputs):
        query_blk, keys_blk, values_blk = inputs
        scores = jnp.einsum(
            "shbd,shcd->shbc", query_blk, keys_blk, preferred_element_type=jnp.float32
        )
        weights = (scores * within[None]).astype(jnp.bfloat16)
        inner_sum = jnp.einsum(
            "shbc,shcd->shbd", weights, values_blk, preferred_element_type=jnp.float32
        )
        outer_sum = first_decay[None, :, :, None] * exact(
            "shbd,shde->shbe", query_blk.astype(jnp.float32), carried
        )
        keys_scaled = keys_blk.astype(jnp.float32) * last_decay[None, :, :, None]
        update = exact("shbd,shbe->shde", keys_scaled, values_blk.astype(jnp.float32))
        return (
            block_decay[None, :, None, None] * carried + update,
            (inner_sum + outer_sum, carried),
        )

    initial = jnp.zeros((SEQ_DEV, query.shape[2], HD, HD), jnp.float32)
    final_state, (mixed, states) = lax.scan(advance, initial, (query, keys, values))
    return (mixed, states)


def lightning_backward(query, keys, values, grads, states, tables):
    within, first_decay, last_decay, block_decay = tables

    def retreat(later_grad, inputs):
        query_blk, keys_blk, values_blk, grad_blk, carried = inputs
        scores = jnp.einsum(
            "shbd,shcd->shbc", query_blk, keys_blk, preferred_element_type=jnp.float32
        )
        weights = (scores * within[None]).astype(jnp.bfloat16)
        d_weights = jnp.einsum(
            "shbd,shcd->shbc", grad_blk, values_blk, preferred_element_type=jnp.float32
        )
        d_scores = (d_weights * within[None]).astype(jnp.bfloat16)
        d_query = jnp.einsum(
            "shbc,shcd->shbd", d_scores, keys_blk, preferred_element_type=jnp.float32
        )
        d_keys = jnp.einsum(
            "shbc,shbd->shcd", d_scores, query_blk, preferred_element_type=jnp.float32
        )
        d_values = jnp.einsum(
            "shbc,shbd->shcd", weights, grad_blk, preferred_element_type=jnp.float32
        )
        grad_scaled = grad_blk.astype(jnp.float32) * first_decay[None, :, :, None]
        keys_scaled = keys_blk.astype(jnp.float32) * last_decay[None, :, :, None]
        d_query = d_query + exact("shbe,shde->shbd", grad_scaled, carried)
        d_keys = d_keys + last_decay[None, :, :, None] * exact(
            "shbe,shde->shbd", values_blk.astype(jnp.float32), later_grad
        )
        d_values = d_values + exact("shbd,shde->shbe", keys_scaled, later_grad)
        earlier = block_decay[None, :, None, None] * later_grad + exact(
            "shbd,shbe->shde", query_blk.astype(jnp.float32), grad_scaled
        )
        return (earlier, (d_query, d_keys, d_values))

    initial = jnp.zeros((SEQ_DEV, query.shape[2], HD, HD), jnp.float32)
    first_grad, results = lax.scan(
        retreat, initial, (query, keys, values, grads, states), reverse=True
    )
    return results


def general_body(
    tokens,
    lengths,
    decay,
    w_query,
    w_key,
    w_value,
    w_gate,
    w_out,
    f_value,
    f_gate,
    f_out,
    cotangent,
):
    own_rows = tokens.shape[0]
    first_row = lax.axis_index("head") * own_rows
    heads_here = decay.shape[0]
    tables = decay_tables(decay)
    positions = first_row + jnp.arange(own_rows, dtype=jnp.int32)
    slot_match = (positions // SLOT)[:, None] == jnp.arange(SEQ_DEV, dtype=jnp.int32)[None, :]
    length_of = jnp.sum(jnp.where(slot_match, lengths[None, :], 0), axis=1)
    keep_rows = (positions % SLOT < length_of).astype(jnp.float32)[:, None]
    inputs_f = tokens.astype(jnp.float32)
    normed, scale_in = normalize(inputs_f)
    gathered = lax.all_gather(normed.astype(jnp.bfloat16), "head", axis=0, tiled=True)
    query_pre = matmul(gathered, w_query)
    keys_pre = matmul(gathered, w_key)
    values_pre = matmul(gathered, w_value)
    gate_pre = matmul(gathered, w_gate)
    query_blocks = to_blocks(jax.nn.silu(query_pre).astype(jnp.bfloat16), heads_here)
    keys_blocks = to_blocks(jax.nn.silu(keys_pre).astype(jnp.bfloat16), heads_here)
    values_blocks = to_blocks(values_pre.astype(jnp.bfloat16), heads_here)
    mixed_blocks, states = lightning_forward(query_blocks, keys_blocks, values_blocks, tables)
    mixed = from_blocks(mixed_blocks)
    squares = lax.psum(jnp.sum(mixed * mixed, axis=1), "head")
    scale_out = lax.rsqrt(squares / D + epsilon)[:, None]
    mixed_unit = mixed * scale_out
    gated = (mixed_unit * gate_pre).astype(jnp.bfloat16)
    branch = lax.psum_scatter(
        matmul(gated, w_out).astype(jnp.bfloat16), "head", scatter_dimension=0, tiled=True
    ).astype(jnp.float32)
    middle = inputs_f + branch
    mid_normed, scale_mid = normalize(middle)
    mid_all = lax.all_gather(mid_normed.astype(jnp.bfloat16), "head", axis=0, tiled=True)
    value_full, gate_full = (
        lax.all_gather(f_value, "dp", axis=0, tiled=True),
        lax.all_gather(f_gate, "dp", axis=0, tiled=True),
    )
    down_full = lax.all_gather(f_out, "dp", axis=1, tiled=True)
    value_ffn = matmul(mid_all, value_full)
    gate_ffn = matmul(mid_all, gate_full)
    hidden = (value_ffn * gate_ffn).astype(jnp.bfloat16)
    ffn_branch = lax.psum_scatter(
        matmul(hidden, down_full).astype(jnp.bfloat16), "head", scatter_dimension=0, tiled=True
    ).astype(jnp.float32)
    output = ((middle + ffn_branch) * keep_rows).astype(jnp.bfloat16)
    grad_out = cotangent.astype(jnp.float32) * keep_rows
    grad_all = lax.all_gather(grad_out.astype(jnp.bfloat16), "head", axis=0, tiled=True)
    grad_hidden = matmul_right_t(grad_all, down_full)
    d_value_ffn = (grad_hidden * gate_ffn).astype(jnp.bfloat16)
    d_gate_ffn = (grad_hidden * value_ffn).astype(jnp.bfloat16)
    d_mid_normed = lax.psum_scatter(
        (matmul_right_t(d_value_ffn, value_full) + matmul_right_t(d_gate_ffn, gate_full)).astype(
            jnp.bfloat16
        ),
        "head",
        scatter_dimension=0,
        tiled=True,
    ).astype(jnp.float32)
    grad_middle = grad_out + norm_back(d_mid_normed, mid_normed, scale_mid)
    joined = jnp.concatenate([d_value_ffn, d_gate_ffn], axis=1)
    hidden_here = hidden.shape[1]
    shares = lax.psum_scatter(
        jnp.concatenate(
            [matmul_left_t(mid_all, joined), matmul_left_t(grad_all, hidden)], axis=1
        ).astype(jnp.bfloat16),
        "dp",
        scatter_dimension=0,
        tiled=True,
    ).astype(jnp.float32)
    d_f_value = shares[:, :hidden_here]
    d_f_gate = shares[:, hidden_here : 2 * hidden_here]
    d_f_out = shares[:, 2 * hidden_here :].T
    grad_rows = lax.all_gather(grad_middle.astype(jnp.bfloat16), "head", axis=0, tiled=True)
    d_gated = matmul_right_t(grad_rows, w_out)
    d_w_out_local = matmul_left_t(gated, grad_rows)
    d_gate_pre = (d_gated * mixed_unit).astype(jnp.bfloat16)
    d_unit = d_gated * gate_pre
    inner_out = lax.psum(jnp.sum(d_unit * mixed_unit, axis=1), "head")
    d_mixed = (scale_out * (d_unit - mixed_unit * (inner_out / D)[:, None])).astype(jnp.bfloat16)
    d_query, d_keys, d_values = lightning_backward(
        query_blocks, keys_blocks, values_blocks, to_blocks(d_mixed, heads_here), states, tables
    )
    d_query_pre = (from_blocks(d_query) * silu_slope(query_pre)).astype(jnp.bfloat16)
    d_keys_pre = (from_blocks(d_keys) * silu_slope(keys_pre)).astype(jnp.bfloat16)
    d_values_pre = from_blocks(d_values).astype(jnp.bfloat16)
    total = matmul_right_t(d_query_pre, w_query) + matmul_right_t(d_keys_pre, w_key)
    d_normed = lax.psum_scatter(
        (total + matmul_right_t(d_values_pre, w_value) + matmul_right_t(d_gate_pre, w_gate)).astype(
            jnp.bfloat16
        ),
        "head",
        scatter_dimension=0,
        tiled=True,
    ).astype(jnp.float32)
    d_tokens = grad_middle + norm_back(d_normed, normed, scale_in)
    grads_attention = (
        lax.psum(matmul_left_t(gathered, d_query_pre).astype(jnp.bfloat16), "dp").astype(
            jnp.float32
        ),
        lax.psum(matmul_left_t(gathered, d_keys_pre).astype(jnp.bfloat16), "dp").astype(
            jnp.float32
        ),
        lax.psum(matmul_left_t(gathered, d_values_pre).astype(jnp.bfloat16), "dp").astype(
            jnp.float32
        ),
        lax.psum(matmul_left_t(gathered, d_gate_pre).astype(jnp.bfloat16), "dp").astype(
            jnp.float32
        ),
        lax.psum(d_w_out_local.astype(jnp.bfloat16), "dp").astype(jnp.float32),
    )
    return (
        output,
        d_tokens,
        grads_attention[0],
        grads_attention[1],
        grads_attention[2],
        grads_attention[3],
        grads_attention[4],
        d_f_value,
        d_f_gate,
        d_f_out,
    )


MESH = pl.DeviceIdType.MESH
NCH = 11
RA = 24
HR = 32
SP = 2
SPW = 2
NWG = 20
NALL = NCH + NWG
RS_AT = (1, 2, 4, 6, 8)
AG_AT = (10, 12, 14)
TN = (((0,), (0,)), ((), ()))
bf = jnp.bfloat16
f32 = jnp.float32
NT = (((1,), (1,)), ((), ()))


def dot(a, b):
    return jnp.dot(a, b, preferred_element_type=f32)


def dotnt(a, b):
    return lax.dot_general(a, b, NT, preferred_element_type=f32)


def dottn(a, b):
    return lax.dot_general(a, b, TN, preferred_element_type=f32)


def place():
    d=lax.axis_index("dp")
    return d//4, (d//2)%2, d%2, lax.axis_index("head")
def dev(z,x,c,y): return ((z*2+x)*2+c, y)
def forward_kernel(tokens, cot, lengths, dec, fv, fg, fo, wq, wk, wv, wg, wo,
                   state, scal, rates, mid, go, W3, pq, pk, pv, pg, po, middle, gate, unit, gated, qpre, kpre, vals, normed,
                   S, WV, WO, GT, MX, BQ, BK, AG_, AU, AD, AV, AN, QB, KB, GS, GR,
                   zs, zr, xs, xr, ys, yr, ds, dr, wys, wyr, wxs, wxr, wds, wdr, gss, gsr, rss, rsr, ls, ws, os):
    z, x, c, y = place()
    zp = [lax.rem(z + r, 4) for r in (1, 2, 3)]
    X, Y, C = dev(z, 1 - x, c, y), dev(z, x, c, 1 - y), dev(z, x, 1 - c, y)
    zb = lax.rem(z, 2)
    ZP = dev(z + 1 - 2 * zb, x, c, y)
    bar = pltpu.get_barrier_semaphore()
    peers = [dev(q, x, c, y) for q in zp] + [X, Y, C]
    for p in peers:
        pl.semaphore_signal(bar, inc=1, device_id=p, device_id_type=MESH)
    own, par = (wq, wk, wv, wg, wo), (pq, pk, pv, pg, po)

    def rc(src, dst, ss, rs, d):
        return pltpu.make_async_remote_copy(src_ref=src, dst_ref=dst, send_sem=ss, recv_sem=rs, device_id=d, device_id_type=MESH)

    def wload(j, h):
        src = (own if h == 0 else par)[j]
        dst = WV.at[2 * j + h] if j < 4 else WO.at[h]
        return pltpu.make_async_copy(src, dst, ws.at[2 * j + h])

    for j in range(5):
        wload(j, 0).start()
    for i in range(NCH):
        S[i, 0] = fv[:, i * 128 : i * 128 + 128]
        S[i, 1] = fg[:, i * 128 : i * 128 + 128]
        S[i, 2] = fo[i * 128 : i * 128 + 128, :].T
    rates[0] = dec[...]
    pl.semaphore_wait(bar, len(peers))
    mine = pltpu.make_async_copy(S, W3.at[:, z, :, x, c, y], ls)
    mine.start()
    rate = rc(dec, rates.at[1], rss, rsr, Y)

    def st(k, i):
        if k == 0:
            return [rc(S.at[i], W3.at[i, z, :, x, c, y], zs.at[i, n], zr.at[i, n], dev(q, x, c, y)) for n, q in enumerate(zp)]
        if k == 1:
            a, b = W3.at[i, :, :, x, c, y, 0:RA], W3.at[i, :, :, x, c, y, RA:64]
            return [rc(a, a, xs.at[i, 0], xr.at[i, 0], X), rc(b, b, ys.at[i, 0], yr.at[i, 0], Y)]
        if k == 2:
            a, b = W3.at[i, :, :, :, c, y, 0:RA], W3.at[i, :, :, x, c, :, RA:64]
            return [rc(b, b, xs.at[i, 1], xr.at[i, 1], X), rc(a, a, ys.at[i, 1], yr.at[i, 1], Y)]
        a = W3.at[i, :, :, :, c]
        return [rc(a, a, ds.at[i], dr.at[i], C)]

    def quarter(r):
        n = r.shape[0] // 4
        return lambda a, b: r.at[pl.ds(pl.multiple_of((2 * a + b) * n, 128), n)]

    def wst(k, j):
        if k == 0:
            return [rc(quarter(own[j])(zb, c), quarter(par[j])(zb, c), wys.at[j], wyr.at[j], Y)]
        if k == 1:
            a = quarter(par[j])(zb, c)
            return [rc(a, a, wxs.at[j], wxr.at[j], ZP)]
        return [rc(quarter(par[j])(b, c), quarter(par[j])(b, c), wds.at[j, b], wdr.at[j, b], C) for b in (0, 1)]

    live = {}

    def go_on(f, tag, k, i, n, last):
        if 0 <= i < n:
            if k > 0:
                for cp in live[(tag, k - 1, i)]:
                    cp.wait_recv()
            if k < last:
                live[(tag, k, i)] = f(k, i)
                for cp in live[(tag, k, i)]:
                    cp.start()

    def tick(t):
        for k in (3, 2, 1, 0):
            go_on(wst, 0, k, t - k * SPW, 5, 3)
        if t == 1:
            mine.wait()
        for k in (4, 3, 2, 1, 0):
            go_on(st, 1, k, t - k * SP, NCH, 4)

    outs = []

    def put(src, dst):
        cp = pltpu.make_async_copy(src, dst, os.at[len(outs)])
        cp.start()
        outs.append(cp)

    def head(h):
        return pl.ds(pl.multiple_of(h * 128, 128), 128)

    tau = lax.broadcasted_iota(jnp.int32, (512, 1), 0).astype(f32)
    rho = lax.broadcasted_iota(jnp.int32, (1, 512), 1).astype(f32)

    def rate_of(h):
        return rates[h // 4, pl.ds(lax.rem(h, 4), 1), 0:1]

    def norm_rows():
        v = tokens[...].astype(f32)
        f = lax.rsqrt(jnp.mean(v * v, axis=1, keepdims=True) + epsilon)
        scal[:, 3:4] = f
        AN[...] = (v * f).astype(bf)
        put(AN, normed)
        pos = lax.broadcasted_iota(jnp.int32, (512, 1), 0) + y * 512
        keep = (pos < lengths[0]).astype(f32)
        scal[:, 0:1] = keep
        go[...] = (cot[...].astype(f32) * keep).astype(bf)

    def project(j, h):
        cols = slice(h * 512, h * 512 + 512)
        v = dot(AN[...], WV[2 * j + h])
        if j == 0:
            BQ[:, cols] = v.astype(bf)
            QB[:, cols] = (v * jax.nn.sigmoid(v)).astype(bf)
        if j == 1:
            BK[:, cols] = v.astype(bf)
            KB[:, cols] = (v * jax.nn.sigmoid(v)).astype(bf)
        if j == 2:
            AV[:, cols] = v.astype(bf)
        if j == 3:
            GT[:, cols] = v
            AG_[:, cols] = v.astype(bf)

    def project_own(*js):
        for j in js:
            wload(j, 0).wait()
            project(j, 0)

    def project_part(j):
        wload(j, 1).wait()
        project(j, 1)
        put(*((BQ, qpre), (BK, kpre), (AV, vals), (AG_, gate))[j])

    def update(h, _):
        hs = head(h)
        kl = (KB[:, hs].astype(f32) * jnp.exp(-rate_of(h) * (511.0 - tau))).astype(bf)
        GS[lax.rem(h + 4, 8)] = dottn(kl, AV[:, hs]).astype(bf)
        return 0

    hand = rc(GS, GR, gss, gsr, Y)
    ti = lax.broadcasted_iota(jnp.int32, (512, 512), 0)
    ri = lax.broadcasted_iota(jnp.int32, (512, 512), 1)

    def inner(h, _):
        hs = head(h)
        r = rate_of(h)
        within = jnp.where(ti >= ri, jnp.exp(-r * (tau + 1.0)) * jnp.exp(r * (rho + 1.0)), 0.0)
        MX[:, hs] = dot((dotnt(QB[:, hs], KB[:, hs]) * within).astype(bf), AV[:, hs])
        return 0

    alive = (y == 1).astype(f32)

    def outer(h, _):
        hs = head(h)
        s = (GR[h].astype(f32) * alive).astype(bf)
        state[h] = s
        MX[:, hs] = MX[:, hs] + jnp.exp(-rate_of(h) * (tau + 1.0)) * dot(QB[:, hs], s)
        return 0

    def gating():
        m = MX[...]
        f = lax.rsqrt(jnp.mean(m * m, axis=1, keepdims=True) + epsilon)
        scal[:, 2:3] = f
        u = m * f
        AU[...] = u.astype(bf)
        put(AU, unit)
        AD[...] = (u * GT[...]).astype(bf)
        put(AD, gated)

    def middle_rows():
        wload(4, 0).wait()
        wload(4, 1).wait()
        m = tokens[...].astype(f32) + dot(AD[:, 0:512], WO[0]) + dot(AD[:, 512:1024], WO[1])
        f = lax.rsqrt(jnp.mean(m * m, axis=1, keepdims=True) + epsilon)
        scal[:, 1:2] = f
        MX[...] = m
        put(MX, middle)
        mid[...] = (m * f).astype(bf)

    loops = lambda f, a, b: lax.fori_loop(a, b, f, 0)
    W = 3 * SPW
    for t in range(NCH + 4 * SP):
        tick(t)
        if t == 0:
            rate.start()
            norm_rows()
        if t == 1:
            project_own(0, 1)
        if t == 2:
            project_own(2, 3)
        if W <= t < W + 5:
            wload(t - W, 1).start()
        if W + 1 <= t < W + 5:
            project_part(t - W - 1)
        if t == W + 3:
            rate.wait()
            loops(update, 0, 8)
            hand.start()
        if t == W + 4:
            loops(inner, 0, 8)
        if t == W + 6:
            hand.wait()
            loops(outer, 0, 8)
            gating()
            middle_rows()
    for cps in live.values():
        for cp in cps:
            cp.wait_send()
    for cp in outs:
        cp.wait()


def forward_call(*ins):
    D, V, S = pltpu.SemaphoreType.DMA, pltpu.VMEM, jax.ShapeDtypeStruct
    A, VM = pl.BlockSpec(memory_space=pl.ANY), pl.BlockSpec(memory_space=pltpu.VMEM)
    act, w = (512, 1024), (1024, 512)
    outs = [S((8, 128, 128), bf), S((512, 4), f32), S((2, 8, 128), f32), S(act, bf), S(act, bf),
            S((NCH, 4, 3, 2, 2, 2, 64, 128), bf)] + [S(w, bf)] * 4 + [S(act, bf), S(act, f32)] + [S(act, bf)] * 7
    scratch = [V((NCH, 3, 64, 128), bf), V((8,) + w, bf), V((2,) + act, bf), V(act, f32), V(act, f32)] + [V(act, bf)] * 9
    scratch += [V((8, 128, 128), bf)] * 2
    n = (NCH,)
    scratch += [D(s) for s in ((NCH, 3), (NCH, 3), (NCH, 2), (NCH, 2), (NCH, 2), (NCH, 2), n, n, (5,), (5,), (5,), (5,), (5, 2), (5, 2), (), (), (), (), (), (10,), (8,))]
    return pl.pallas_call(
        forward_kernel,
        out_shape=outs,
        in_specs=[VM, VM, pl.BlockSpec(memory_space=pltpu.SMEM)] + [VM] * 4 + [A] * 5,
        out_specs=[VM] * 5 + [A] * 14,
        scratch_shapes=scratch,
        compiler_params=pltpu.CompilerParams(collective_id=1, has_side_effects=True, vmem_limit_bytes=67043328),
    )(*ins)
def backward_kernel(mid, go, rates, scal, state, W3, middle, gate, unit, gated, qpre, kpre, vals, normed, wq, wk, wv, wg, wo, pq, pk, pv, pg, po,
                    output, dtok, sh, O,
                    G, RD, R1, R2, Q, RZ, FN, WT, LT, ACC, DV, R, UN, NM, DMX, WB, WO, GS, GR,
                    wsem, lsem, bsem, gss, gsr, ds, dr, xs, xr, ys, yr, zs, zr, az_s, az_r, ax_s, ax_r, ad_s, ad_r, fl):
    z, x, c, y = place()
    zp = [lax.rem(z + r, 4) for r in (1, 2, 3)]
    X, Y, C = dev(z, 1 - x, c, y), dev(z, x, c, 1 - y), dev(z, x, 1 - c, y)
    bar = pltpu.get_barrier_semaphore()
    peers = [dev(q, x, c, y) for q in zp] + [X, Y, C]
    for p in peers:
        pl.semaphore_signal(bar, inc=1, device_id=p, device_id_type=MESH)

    def rc(src, dst, ss, rs, d):
        return pltpu.make_async_remote_copy(src_ref=src, dst_ref=dst, send_sem=ss, recv_sem=rs, device_id=d, device_id_type=MESH)

    def wload(i, s):
        return [pltpu.make_async_copy(W3.at[i, :, :, :, :, h], WT.at[s, :, :, :, :, :, pl.ds(h * 128, 128)], wsem.at[s, h]) for h in (0, 1)]

    loads = [pltpu.make_async_copy(a, b, lsem.at[n]) for n, (a, b) in enumerate(
        [(middle, ACC), (gated, R.at[0]), (gate, R.at[1]), (vals, R.at[2]), (kpre, R.at[3]), (qpre, R.at[4]), (unit, UN), (normed, NM), (wo, WO.at[0]), (po, WO.at[1])])]
    for cp in wload(0, 0):
        cp.start()
    for cp in loads:
        cp.start()
    mats = (wg, pg, wv, pv, wk, pk, wq, pq)

    def wbload(n):
        return pltpu.make_async_copy(mats[n], WB.at[n % 2], bsem.at[n % 2])

    wbload(0).start()
    wbload(1).start()
    LT[0] = mid[...].T
    LT[1] = go[...].T
    dtok[...] = jnp.zeros_like(dtok)
    loads[0].wait()
    pl.semaphore_wait(bar, len(peers))

    def cps(k, i, hr):
        g, s, n = lax.rem(i, NCH), lax.rem(i, 4), 3 if hr else 1
        if k == 0:
            return [rc(G.at[g, 1 - c, 0:n], RD.at[lax.rem(i, 2), 0:n], ds.at[i], dr.at[i], C)]
        if k == 1:
            o = [rc(G.at[g, c, 0:n, :, :, 1 - y, hr:64], R1.at[s, 0:n, :, :, hr:64], ys.at[i, 0], yr.at[i, 0], Y)]
            if hr:
                o.append(rc(G.at[g, c, 0:n, :, 1 - x, :, 0:hr], R1.at[s, 0:n, :, :, 0:hr], xs.at[i, 0], xr.at[i, 0], X))
            return o
        if k == 2:
            o = [rc(G.at[g, c, 0:n, :, 1 - x, y, hr:64], R2.at[s, 0:n, :, hr:64], xs.at[i, 1], xr.at[i, 1], X)]
            if hr:
                o.append(rc(G.at[g, c, 0:n, :, x, 1 - y, 0:hr], R2.at[s, 0:n, :, 0:hr], ys.at[i, 1], yr.at[i, 1], Y))
            return o
        if k == 3:
            return [rc(Q.at[s, 0:n, q], RZ.at[s, m, 0:n], zs.at[i, m], zr.at[i, m], dev(q, x, c, y)) for m, q in enumerate(zp)]

    def ags(k, w):
        if k == 0:
            f = FN.at[lax.rem(w, 4)]
            return [rc(f, O.at[w, z, x, c], az_s.at[w, n], az_r.at[w, n], dev(q, x, c, y)) for n, q in enumerate(zp)]
        if k == 1:
            return [rc(O.at[w, :, x, c], O.at[w, :, x, c], ax_s.at[w], ax_r.at[w], X)]
        if k == 2:
            return [rc(O.at[w, :, :, c], O.at[w, :, :, c], ad_s.at[w], ad_r.at[w], C)]

    def flush(w):
        return pltpu.make_async_copy(FN.at[lax.rem(w, 4)], O.at[w, z, x, c], fl.at[w])

    def reduce(k, i, hr):
        g, s, n = lax.rem(i, NCH), lax.rem(i, 4), 3 if hr else 1
        up = lambda v: v.astype(f32)
        if k == 1:
            G[g, c, 0:n] = (up(G[g, c, 0:n]) + up(RD[lax.rem(i, 2), 0:n])).astype(bf)
        if k == 2:
            if hr:
                G[g, c, 0:n, :, x, :, 0:hr] = (up(G[g, c, 0:n, :, x, :, 0:hr]) + up(R1[s, 0:n, :, :, 0:hr])).astype(bf)
            G[g, c, 0:n, :, :, y, hr:64] = (up(G[g, c, 0:n, :, :, y, hr:64]) + up(R1[s, 0:n, :, :, hr:64])).astype(bf)
        if k == 3:
            Q[s, 0:n] = (up(G[g, c, 0:n, :, x, y]) + up(R2[s, 0:n])).astype(bf)
        if k == 4:
            v = up(Q[s, 0:n, z])
            for m in range(3):
                v = v + up(RZ[s, m, 0:n])
            if hr:
                sh[:, :, pl.ds(pl.multiple_of(i * 128, 128), 128)] = v
            else:
                FN[lax.rem(i - NCH, 4)] = v[0].astype(bf)

    def arrive(k, i, hr):
        if k > 0:
            for cp in cps(k - 1, i, hr):
                cp.wait_recv()
        if k == 1:
            for cp in cps(0, i, hr):
                cp.wait_send()
        if k == 4:
            for kk in (1, 2, 3):
                for cp in cps(kk, i, hr):
                    cp.wait_send()
        reduce(k, i, hr)

    def leave(k, i, hr):
        for cp in cps(k, i, hr):
            cp.start()

    def both(f, k, t):
        i = t - RS_AT[k]

        @pl.when((i >= 0) & (i < NCH))
        def _():
            f(k, i, HR)

        @pl.when((i >= NCH) & (i < NALL))
        def _():
            f(k, i, 0)

    def ag_arrive(k, t):
        w = t - AG_AT[k] - NCH

        @pl.when((w >= 0) & (w < NWG))
        def _():
            for cp in ags(k, w):
                cp.wait_recv()
            if k == 0:
                for cp in ags(0, w):
                    cp.wait_send()
                flush(w).wait()

    def ag_leave(k, t):
        w = t - (AG_AT[k - 1] if k else RS_AT[4]) - NCH

        @pl.when((w >= 0) & (w < NWG))
        def _():
            for cp in ags(k, w):
                cp.start()
            if k == 0:
                flush(w).start()

    def stages(t):
        ag_arrive(2, t)
        ag_arrive(1, t)
        ag_arrive(0, t)
        ag_leave(2, t)
        both(arrive, 4, t)
        ag_leave(1, t)
        both(arrive, 3, t)
        ag_leave(0, t)
        both(arrive, 2, t)
        both(leave, 3, t)
        both(arrive, 1, t)
        for k in (2, 1, 0):
            both(leave, k, t)

    def store(g, t, r, own):
        r = r.astype(bf).reshape(4, 2, 2, 64, 256)
        for cc in (0, 1):
            G[g, cc, t, :, :, own] = r[:, :, cc, :, 0:128]
            G[g, cc, t, :, :, 1 - own] = r[:, :, cc, :, 128:256]

    def ffn(t):
        s = lax.rem(t, 2)
        for cp in wload(t, s):
            cp.wait()

        @pl.when(t + 1 < NCH)
        def _():
            for cp in wload(t + 1, 1 - s):
                cp.start()

        fv, fg, fo = [WT[s, :, n].reshape(1024, 256) for n in range(3)]
        m, g_ = mid[...], go[...]
        v, g, gh = dot(m, fv), dot(m, fg), dot(g_, fo)
        hid, dv, dg = (v * g).astype(bf), (gh * g).astype(bf), (gh * v).astype(bf)
        ACC[...] += dotnt(hid, fo)
        dtok[...] += dotnt(dv, fv) + dotnt(dg, fg)
        store(t, 0, dot(LT[0], dv), 0)
        store(t, 1, dot(LT[0], dg), 0)
        store(t, 2, dot(LT[1], hid), 0)

    def ffn_tick(t, _):
        stages(t)

        def one(n, _):
            ffn(n)
            return 0

        lax.fori_loop(jnp.maximum(2 * t - 1, 0), jnp.minimum(2 * t + 1, NCH), one, 0)
        return 0

    T = 6
    lax.fori_loop(0, T, ffn_tick, 0)
    stages(T)
    for cp in loads[1:]:
        cp.wait()
    keep, scale_mid, scale_out, scale_in = [scal[:, n : n + 1] for n in range(4)]
    output[...] = (ACC[...] * keep).astype(bf)
    n2 = mid[...].astype(f32)
    dm = dtok[...]
    gm = go[...].astype(f32) + scale_mid * (dm - n2 * jnp.mean(dm * n2, axis=1, keepdims=True))
    dtok[...] = gm
    gml = gm.astype(bf)
    LT[0] = gml.T
    LT[1] = NM[...].T
    for h in (0, 1):
        cols = slice(h * 512, h * 512 + 512)
        ACC[:, cols] = dotnt(gml, WO[h])
    dgt, un = ACC[...], UN[...].astype(f32)
    du = dgt * R[1].astype(f32)
    R[1] = (dgt * un).astype(bf)
    DMX[...] = (scale_out * (du - un * jnp.mean(du * un, axis=1, keepdims=True))).astype(bf)

    def head(h):
        return pl.ds(pl.multiple_of(h * 128, 128), 128)

    def silu(v):
        return v * jax.nn.sigmoid(v)

    def rate_of(h):
        return rates[h // 4, pl.ds(lax.rem(h, 4), 1), 0:1]

    tau = lax.broadcasted_iota(jnp.int32, (512, 1), 0).astype(f32)
    rho = lax.broadcasted_iota(jnp.int32, (1, 512), 1).astype(f32)

    def first(h, _):
        hs = head(h)
        q = silu(R[4, :, hs].astype(f32)).astype(bf)
        gf = (DMX[:, hs].astype(f32) * jnp.exp(-rate_of(h) * (tau + 1.0))).astype(bf)
        GS[lax.rem(h + 4, 8)] = dottn(q, gf).astype(bf)
        return 0

    lax.fori_loop(0, 8, first, 0)
    stages(T + 1)
    later = rc(GS, GR, gss, gsr, Y)
    later.start()
    ti = lax.broadcasted_iota(jnp.int32, (512, 512), 0)
    ri = lax.broadcasted_iota(jnp.int32, (512, 512), 1)

    def pair(h, _):
        hs = head(h)
        qp, kp = R[4, :, hs].astype(f32), R[3, :, hs].astype(f32)
        q, k, v, dmx = silu(qp).astype(bf), silu(kp).astype(bf), R[2, :, hs], DMX[:, hs]
        cf, rf = jnp.exp(-rate_of(h) * (tau + 1.0)), jnp.exp(rate_of(h) * (rho + 1.0))
        within = jnp.where(ti >= ri, cf * rf, 0.0)
        wt = (dotnt(q, k) * within).astype(bf)
        dsc = (dotnt(dmx, v) * within).astype(bf)
        gf = (dmx.astype(f32) * cf).astype(bf)
        dq = dot(dsc, k) + dotnt(gf, state[h])
        ACC[:, hs] = dottn(dsc, q)
        DV[:, hs] = dottn(wt, dmx)
        sq = jax.nn.sigmoid(qp)
        R[4, :, hs] = (dq * (sq * (1.0 + qp * (1.0 - sq)))).astype(bf)
        return 0

    stages(T + 2)
    lax.fori_loop(0, 4, pair, 0)
    stages(T + 3)
    lax.fori_loop(4, 8, pair, 0)
    stages(T + 4)
    later.wait()
    live = (y == 0).astype(f32)

    def finish(h, _):
        hs = head(h)
        gin = (GR[h].astype(f32) * live).astype(bf)
        kp = R[3, :, hs].astype(f32)
        sk = jax.nn.sigmoid(kp)
        k = (kp * sk).astype(bf)
        lf = jnp.exp(-rate_of(h) * (511.0 - tau))
        kl = (k.astype(f32) * lf).astype(bf)
        dk = ACC[:, hs] + lf * dotnt(R[2, :, hs], gin)
        R[2, :, hs] = (DV[:, hs] + dot(kl, gin)).astype(bf)
        R[3, :, hs] = (dk * (sk * (1.0 + kp * (1.0 - sk)))).astype(bf)
        return 0

    lax.fori_loop(0, 8, finish, 0)
    def wgrad(p):
        j, cp = p // 4, lax.rem(p, 4)
        lo = pl.multiple_of(cp * 128, 128)
        rr = jnp.concatenate([R[j, :, pl.ds(lo, 128)], R[j, :, pl.ds(lo + 512, 128)]], axis=1)
        store(lax.rem(p, NCH), 0, dot(LT[jnp.minimum(j, 1)], rr), y)

    def wg_tick(t, _):
        stages(t)
        p = t - NCH
        wgrad(p)
        for n in range(8):
            @pl.when(p == n)
            def _():
                wbload(n).wait()

        @pl.when(p < 8)
        def _():
            j, h = 1 + p // 2, lax.rem(p, 2)
            part = dotnt(R[j, :, pl.ds(pl.multiple_of(h * 512, 128), 512)], WB[h])
            ACC[...] = jnp.where(p == 0, 0.0, ACC[...]) + part

        for n in range(6):
            @pl.when(p == n)
            def _():
                wbload(n + 2).start()

        @pl.when(p == 8)
        def _():
            n1 = NM[...].astype(f32)
            dn = ACC[...]
            dtok[...] = dtok[...] + scale_in * (dn - n1 * jnp.mean(dn * n1, axis=1, keepdims=True))

        return 0

    lax.fori_loop(NCH, NCH + NWG, wg_tick, 0)
    def tail(t, _):
        stages(t)
        return 0

    lax.fori_loop(NALL, NALL + AG_AT[2], tail, 0)

    def drain(w, _):
        for k in (1, 2):
            for cp in ags(k, w):
                cp.wait_send()
        return 0

    lax.fori_loop(0, NWG, drain, 0)


def backward_call(mid, go, rates, scal, state, *rest):
    D, V = pltpu.SemaphoreType.DMA, pltpu.VMEM
    A, VM = pl.BlockSpec(memory_space=pl.ANY), pl.BlockSpec(memory_space=pltpu.VMEM)
    act = (512, 1024)
    scratch = [V((NCH, 2, 3, 4, 2, 2, 64, 128), bf), V((2, 3, 4, 2, 2, 64, 128), bf),
               V((4, 3, 4, 2, 64, 128), bf), V((4, 3, 4, 64, 128), bf),
               V((4, 3, 4, 64, 128), bf), V((4, 3, 3, 64, 128), bf), V((4, 64, 128), bf), V((2, 4, 3, 2, 2, 64, 256), bf),
               V((2, 1024, 512), bf), V(act, f32), V(act, f32), V((5,) + act, bf), V(act, bf), V(act, bf), V(act, bf),
               V((2, 1024, 512), bf), V((2, 512, 1024), bf), V((8, 128, 128), bf), V((8, 128, 128), bf)]
    n = NALL
    scratch += [D(s) for s in ((2, 2), (10,), (2,), (), (), (n,), (n,), (n, 2), (n, 2), (n, 2), (n, 2), (n, 3), (n, 3),
                               (NWG, 3), (NWG, 3), (NWG,), (NWG,), (NWG,), (NWG,), (NWG,))]
    S = jax.ShapeDtypeStruct
    return pl.pallas_call(
        backward_kernel,
        out_shape=[S(act, bf), S(act, f32), S((3, 64, 1408), f32), S((NWG, 4, 2, 2, 64, 128), bf)],
        in_specs=[VM] * 5 + [A] * 19,
        out_specs=[VM] * 3 + [A],
        scratch_shapes=scratch,
        compiler_params=pltpu.CompilerParams(collective_id=2, has_side_effects=True, vmem_limit_bytes=67043328),
    )(mid, go, rates, scal, state, *rest)
def finish_kernel(o, sh, d_query, d_key, d_value, d_gate, d_out, d_f_value, d_f_gate, d_f_out):
    for n in range(4):
        cols = slice(n * 128, n * 128 + 128)
        d_out[cols, :] = o[n].astype(f32).T
        d_gate[:, cols] = o[4 + n].astype(f32)
        d_value[:, cols] = o[8 + n].astype(f32)
        d_key[:, cols] = o[12 + n].astype(f32)
        d_query[:, cols] = o[16 + n].astype(f32)

    @pl.when(pl.program_id(0) == 0)
    def _():
        d_f_value[...] = sh[0]
        d_f_gate[...] = sh[1]
        d_f_out[...] = sh[2].T


def finish_call(o, sh):
    S = jax.ShapeDtypeStruct
    whole = lambda *s: pl.BlockSpec(s, lambda i: (0,) * len(s))
    return pl.pallas_call(
        finish_kernel,
        grid=(4,),
        out_shape=[S((1024, 512), f32)] * 4 + [S((512, 1024), f32)] + [S((64, 1408), f32)] * 2 + [S((1408, 64), f32)],
        in_specs=[pl.BlockSpec((20, 256, 128), lambda i: (0, i, 0)), whole(3, 64, 1408)],
        out_specs=[pl.BlockSpec((256, 512), lambda i: (i, 0))] * 4 + [pl.BlockSpec((512, 256), lambda i: (0, i))] + [whole(64, 1408)] * 2 + [whole(1408, 64)],
        compiler_params=pltpu.CompilerParams(vmem_limit_bytes=48 << 20),
    )(o, sh)

def fast_body(tokens, lengths, decay, w_query, w_key, w_value, w_gate, w_out, f_value, f_gate, f_out, cotangent):
    dec = jnp.concatenate([jnp.broadcast_to(decay[:, None], (4, 128)), jnp.zeros((4, 128), f32)])
    weights = (w_query, w_key, w_value, w_gate, w_out)
    state, scal, rates, mid, go, W3, pq, pk, pv, pg, po, middle, *acts = forward_call(
        tokens, cotangent, lengths, dec, f_value, f_gate, f_out, *weights)
    output, d_tokens, shares, grads = backward_call(mid, go, rates, scal, state, W3, middle, *acts, *weights, pq, pk, pv, pg, po)
    d_query, d_key, d_value, d_gate, d_out, d_f_value, d_f_gate, d_f_out = finish_call(grads.reshape(NWG, 1024, 128), shares)
    return (output, d_tokens, d_query, d_key, d_value, d_gate, d_out, d_f_value, d_f_gate, d_f_out)


def solution(mesh):
    placed = (
        P(("dp", "head"), None),
        P("dp"),
        P("head"),
        P(None, "head"),
        P(None, "head"),
        P(None, "head"),
        P(None, "head"),
        P("head", None),
        P("dp", "head"),
        P("dp", "head"),
        P("head", "dp"),
        P(("dp", "head"), None),
    )
    fast = mesh.shape["dp"] == 16 and mesh.shape["head"] == 2
    return jax.shard_map(
        fast_body if fast else general_body,
        mesh=mesh,
        in_specs=placed,
        out_specs=(
            P(("dp", "head"), None),
            P(("dp", "head"), None),
            P(None, "head"),
            P(None, "head"),
            P(None, "head"),
            P(None, "head"),
            P("head", None),
            P("dp", "head"),
            P("dp", "head"),
            P("head", "dp"),
        ),
        check_vma=False,
    )
```

```python
import jax
import jax.numpy as jnp
from jax import lax
from jax.experimental import pallas as pl
from jax.experimental.pallas import tpu as pltpu
from jax.sharding import PartitionSpec as P

D = 1024
HD = 128
SEQ_DEV = 1
SLOT = 1024
BLOCK = 512


epsilon = 1e-06


def normalize(values):
    factor = lax.rsqrt(jnp.mean(values * values, axis=-1, keepdims=True) + epsilon)
    return (values * factor, factor)


def norm_back(grad_normed, normed, factor):
    inner_sum = jnp.mean(grad_normed * normed, axis=-1, keepdims=True)
    return factor * (grad_normed - normed * inner_sum)


def silu_slope(values):
    sigmoid = jax.nn.sigmoid(values)
    return sigmoid * (1.0 + values * (1.0 - sigmoid))


def matmul(left_side, right_side):
    return jnp.dot(left_side, right_side, preferred_element_type=jnp.float32)


def matmul_right_t(left_side, right_side):
    return lax.dot_general(
        left_side, right_side, (((1,), (1,)), ((), ())), preferred_element_type=jnp.float32
    )


def matmul_left_t(left_side, right_side):
    return lax.dot_general(
        left_side, right_side, (((0,), (0,)), ((), ())), preferred_element_type=jnp.float32
    )


def exact(form, left_side, right_side):
    return jnp.einsum(form, left_side, right_side, precision=lax.Precision.HIGHEST)


def decay_tables(rates):
    offsets = jnp.arange(BLOCK).astype(jnp.float32)
    spread = offsets[:, None] - offsets[None, :]
    causal = spread >= 0
    within = jnp.where(
        causal[None], jnp.exp(-rates[:, None, None] * jnp.where(causal, spread, 0.0)[None]), 0.0
    )
    first_decay = jnp.exp(-rates[:, None] * (offsets[None, :] + 1.0))
    last_decay = jnp.exp(-rates[:, None] * (BLOCK - 1.0 - offsets[None, :]))
    block_decay = jnp.exp(-rates * BLOCK)
    return (within, first_decay, last_decay, block_decay)


def to_blocks(values, heads):
    shaped = values.reshape(SEQ_DEV, SLOT // BLOCK, BLOCK, heads, HD)
    return shaped.transpose(1, 0, 3, 2, 4)


def from_blocks(blocks):
    return blocks.transpose(1, 0, 3, 2, 4).reshape(-1, blocks.shape[2] * blocks.shape[4])


def lightning_forward(query, keys, values, tables):
    within, first_decay, last_decay, block_decay = tables

    def advance(carried, inputs):
        query_blk, keys_blk, values_blk = inputs
        scores = jnp.einsum(
            "shbd,shcd->shbc", query_blk, keys_blk, preferred_element_type=jnp.float32
        )
        weights = (scores * within[None]).astype(jnp.bfloat16)
        inner_sum = jnp.einsum(
            "shbc,shcd->shbd", weights, values_blk, preferred_element_type=jnp.float32
        )
        outer_sum = first_decay[None, :, :, None] * exact(
            "shbd,shde->shbe", query_blk.astype(jnp.float32), carried
        )
        keys_scaled = keys_blk.astype(jnp.float32) * last_decay[None, :, :, None]
        update = exact("shbd,shbe->shde", keys_scaled, values_blk.astype(jnp.float32))
        return (
            block_decay[None, :, None, None] * carried + update,
            (inner_sum + outer_sum, carried),
        )

    initial = jnp.zeros((SEQ_DEV, query.shape[2], HD, HD), jnp.float32)
    final_state, (mixed, states) = lax.scan(advance, initial, (query, keys, values))
    return (mixed, states)


def lightning_backward(query, keys, values, grads, states, tables):
    within, first_decay, last_decay, block_decay = tables

    def retreat(later_grad, inputs):
        query_blk, keys_blk, values_blk, grad_blk, carried = inputs
        scores = jnp.einsum(
            "shbd,shcd->shbc", query_blk, keys_blk, preferred_element_type=jnp.float32
        )
        weights = (scores * within[None]).astype(jnp.bfloat16)
        d_weights = jnp.einsum(
            "shbd,shcd->shbc", grad_blk, values_blk, preferred_element_type=jnp.float32
        )
        d_scores = (d_weights * within[None]).astype(jnp.bfloat16)
        d_query = jnp.einsum(
            "shbc,shcd->shbd", d_scores, keys_blk, preferred_element_type=jnp.float32
        )
        d_keys = jnp.einsum(
            "shbc,shbd->shcd", d_scores, query_blk, preferred_element_type=jnp.float32
        )
        d_values = jnp.einsum(
            "shbc,shbd->shcd", weights, grad_blk, preferred_element_type=jnp.float32
        )
        grad_scaled = grad_blk.astype(jnp.float32) * first_decay[None, :, :, None]
        keys_scaled = keys_blk.astype(jnp.float32) * last_decay[None, :, :, None]
        d_query = d_query + exact("shbe,shde->shbd", grad_scaled, carried)
        d_keys = d_keys + last_decay[None, :, :, None] * exact(
            "shbe,shde->shbd", values_blk.astype(jnp.float32), later_grad
        )
        d_values = d_values + exact("shbd,shde->shbe", keys_scaled, later_grad)
        earlier = block_decay[None, :, None, None] * later_grad + exact(
            "shbd,shbe->shde", query_blk.astype(jnp.float32), grad_scaled
        )
        return (earlier, (d_query, d_keys, d_values))

    initial = jnp.zeros((SEQ_DEV, query.shape[2], HD, HD), jnp.float32)
    first_grad, results = lax.scan(
        retreat, initial, (query, keys, values, grads, states), reverse=True
    )
    return results


def general_body(
    tokens,
    lengths,
    decay,
    w_query,
    w_key,
    w_value,
    w_gate,
    w_out,
    f_value,
    f_gate,
    f_out,
    cotangent,
):
    own_rows = tokens.shape[0]
    first_row = lax.axis_index("head") * own_rows
    heads_here = decay.shape[0]
    tables = decay_tables(decay)
    positions = first_row + jnp.arange(own_rows, dtype=jnp.int32)
    slot_match = (positions // SLOT)[:, None] == jnp.arange(SEQ_DEV, dtype=jnp.int32)[None, :]
    length_of = jnp.sum(jnp.where(slot_match, lengths[None, :], 0), axis=1)
    keep_rows = (positions % SLOT < length_of).astype(jnp.float32)[:, None]
    inputs_f = tokens.astype(jnp.float32)
    normed, scale_in = normalize(inputs_f)
    gathered = lax.all_gather(normed.astype(jnp.bfloat16), "head", axis=0, tiled=True)
    query_pre = matmul(gathered, w_query)
    keys_pre = matmul(gathered, w_key)
    values_pre = matmul(gathered, w_value)
    gate_pre = matmul(gathered, w_gate)
    query_blocks = to_blocks(jax.nn.silu(query_pre).astype(jnp.bfloat16), heads_here)
    keys_blocks = to_blocks(jax.nn.silu(keys_pre).astype(jnp.bfloat16), heads_here)
    values_blocks = to_blocks(values_pre.astype(jnp.bfloat16), heads_here)
    mixed_blocks, states = lightning_forward(query_blocks, keys_blocks, values_blocks, tables)
    mixed = from_blocks(mixed_blocks)
    squares = lax.psum(jnp.sum(mixed * mixed, axis=1), "head")
    scale_out = lax.rsqrt(squares / D + epsilon)[:, None]
    mixed_unit = mixed * scale_out
    gated = (mixed_unit * gate_pre).astype(jnp.bfloat16)
    branch = lax.psum_scatter(
        matmul(gated, w_out).astype(jnp.bfloat16), "head", scatter_dimension=0, tiled=True
    ).astype(jnp.float32)
    middle = inputs_f + branch
    mid_normed, scale_mid = normalize(middle)
    mid_all = lax.all_gather(mid_normed.astype(jnp.bfloat16), "head", axis=0, tiled=True)
    value_full, gate_full = (
        lax.all_gather(f_value, "dp", axis=0, tiled=True),
        lax.all_gather(f_gate, "dp", axis=0, tiled=True),
    )
    down_full = lax.all_gather(f_out, "dp", axis=1, tiled=True)
    value_ffn = matmul(mid_all, value_full)
    gate_ffn = matmul(mid_all, gate_full)
    hidden = (value_ffn * gate_ffn).astype(jnp.bfloat16)
    ffn_branch = lax.psum_scatter(
        matmul(hidden, down_full).astype(jnp.bfloat16), "head", scatter_dimension=0, tiled=True
    ).astype(jnp.float32)
    output = ((middle + ffn_branch) * keep_rows).astype(jnp.bfloat16)
    grad_out = cotangent.astype(jnp.float32) * keep_rows
    grad_all = lax.all_gather(grad_out.astype(jnp.bfloat16), "head", axis=0, tiled=True)
    grad_hidden = matmul_right_t(grad_all, down_full)
    d_value_ffn = (grad_hidden * gate_ffn).astype(jnp.bfloat16)
    d_gate_ffn = (grad_hidden * value_ffn).astype(jnp.bfloat16)
    d_mid_normed = lax.psum_scatter(
        (matmul_right_t(d_value_ffn, value_full) + matmul_right_t(d_gate_ffn, gate_full)).astype(
            jnp.bfloat16
        ),
        "head",
        scatter_dimension=0,
        tiled=True,
    ).astype(jnp.float32)
    grad_middle = grad_out + norm_back(d_mid_normed, mid_normed, scale_mid)
    joined = jnp.concatenate([d_value_ffn, d_gate_ffn], axis=1)
    hidden_here = hidden.shape[1]
    shares = lax.psum_scatter(
        jnp.concatenate(
            [matmul_left_t(mid_all, joined), matmul_left_t(grad_all, hidden)], axis=1
        ).astype(jnp.bfloat16),
        "dp",
        scatter_dimension=0,
        tiled=True,
    ).astype(jnp.float32)
    d_f_value = shares[:, :hidden_here]
    d_f_gate = shares[:, hidden_here : 2 * hidden_here]
    d_f_out = shares[:, 2 * hidden_here :].T
    grad_rows = lax.all_gather(grad_middle.astype(jnp.bfloat16), "head", axis=0, tiled=True)
    d_gated = matmul_right_t(grad_rows, w_out)
    d_w_out_local = matmul_left_t(gated, grad_rows)
    d_gate_pre = (d_gated * mixed_unit).astype(jnp.bfloat16)
    d_unit = d_gated * gate_pre
    inner_out = lax.psum(jnp.sum(d_unit * mixed_unit, axis=1), "head")
    d_mixed = (scale_out * (d_unit - mixed_unit * (inner_out / D)[:, None])).astype(jnp.bfloat16)
    d_query, d_keys, d_values = lightning_backward(
        query_blocks, keys_blocks, values_blocks, to_blocks(d_mixed, heads_here), states, tables
    )
    d_query_pre = (from_blocks(d_query) * silu_slope(query_pre)).astype(jnp.bfloat16)
    d_keys_pre = (from_blocks(d_keys) * silu_slope(keys_pre)).astype(jnp.bfloat16)
    d_values_pre = from_blocks(d_values).astype(jnp.bfloat16)
    total = matmul_right_t(d_query_pre, w_query) + matmul_right_t(d_keys_pre, w_key)
    d_normed = lax.psum_scatter(
        (total + matmul_right_t(d_values_pre, w_value) + matmul_right_t(d_gate_pre, w_gate)).astype(
            jnp.bfloat16
        ),
        "head",
        scatter_dimension=0,
        tiled=True,
    ).astype(jnp.float32)
    d_tokens = grad_middle + norm_back(d_normed, normed, scale_in)
    grads_attention = (
        lax.psum(matmul_left_t(gathered, d_query_pre).astype(jnp.bfloat16), "dp").astype(
            jnp.float32
        ),
        lax.psum(matmul_left_t(gathered, d_keys_pre).astype(jnp.bfloat16), "dp").astype(
            jnp.float32
        ),
        lax.psum(matmul_left_t(gathered, d_values_pre).astype(jnp.bfloat16), "dp").astype(
            jnp.float32
        ),
        lax.psum(matmul_left_t(gathered, d_gate_pre).astype(jnp.bfloat16), "dp").astype(
            jnp.float32
        ),
        lax.psum(d_w_out_local.astype(jnp.bfloat16), "dp").astype(jnp.float32),
    )
    return (
        output,
        d_tokens,
        grads_attention[0],
        grads_attention[1],
        grads_attention[2],
        grads_attention[3],
        grads_attention[4],
        d_f_value,
        d_f_gate,
        d_f_out,
    )


MESH = pl.DeviceIdType.MESH
NCH = 11
RA = 24
HR = 32
SP = 2
SPW = 2
NEAR = 2
MEET = 13
NWG = 20
NALL = NCH + NWG
RS_AT = (1, 2, 4, 6, 8)
AG_AT = (10, 12, 14)
TN = (((0,), (0,)), ((), ()))
bf = jnp.bfloat16
f32 = jnp.float32
NT = (((1,), (1,)), ((), ()))


def dot(a, b):
    return jnp.dot(a, b, preferred_element_type=f32)


def dotnt(a, b):
    return lax.dot_general(a, b, NT, preferred_element_type=f32)


def dottn(a, b):
    return lax.dot_general(a, b, TN, preferred_element_type=f32)


def place():
    d=lax.axis_index("dp")
    return d//4, (d//2)%2, d%2, lax.axis_index("head")
def dev(z,x,c,y): return ((z*2+x)*2+c, y)
def layer_kernel(tokens, cot, lengths, dec, fv, fg, fo, wq, wk, wv, wg, wo,
                 output, dtok, sh, O, W3, pq, pk, pv, pg, po,
                 S, WV, WO, G, RD, R1, R2, Q, RZ, FN, WT, LT, ACC, DV, R, UN, NM, DMX, mid, go, scal, rates, state, GS, GR, GS2, GR2,
                 zs, zr, xs, xr, ys, yr, nxs, nxr, nys, nyr, ds, dr, wys, wyr, wxs, wxr, wds, wdr, gss, gsr, rss, rsr, ls, ws,
                 wsem, bsem, g2s, g2r, e_s, e_r, fx_s, fx_r, fy_s, fy_r, fz_s, fz_r, az_s, az_r, ax_s, ax_r, ad_s, ad_r, fl):
    z, x, c, y = place()
    zp = [lax.rem(z + r, 4) for r in (1, 2, 3)]
    X, Y, C = dev(z, 1 - x, c, y), dev(z, x, c, 1 - y), dev(z, x, 1 - c, y)
    zb = lax.rem(z, 2)
    ZP = dev(z + 1 - 2 * zb, x, c, y)
    bar = pltpu.get_barrier_semaphore()
    peers = [dev(q, x, c, y) for q in zp] + [X, Y, C]
    for p in peers:
        pl.semaphore_signal(bar, inc=1, device_id=p, device_id_type=MESH)
    own, par = (wq, wk, wv, wg, wo), (pq, pk, pv, pg, po)

    def rc(src, dst, ss, rs, d):
        return pltpu.make_async_remote_copy(src_ref=src, dst_ref=dst, send_sem=ss, recv_sem=rs, device_id=d, device_id_type=MESH)

    def wload(j, h):
        src = (own if h == 0 else par)[j]
        dst = WV.at[j] if j < 4 else WO.at[h]
        return pltpu.make_async_copy(src, dst, ws.at[2 * j + h])

    for j in range(5):
        wload(j, 0).start()
    for i in range(NCH):
        S[i, 0] = fv[:, i * 128 : i * 128 + 128]
        S[i, 1] = fg[:, i * 128 : i * 128 + 128]
        S[i, 2] = fo[:, i * 128 : i * 128 + 128]
    rates[0] = dec[...]
    dtok[...] = jnp.zeros_like(dtok)
    pl.semaphore_wait(bar, len(peers))
    mine = pltpu.make_async_copy(S, W3.at[:, z, :, x, c, y], ls)
    mine.start()
    rate = rc(dec, rates.at[1], rss, rsr, Y)

    far = [lax.rem(z + r, 4) for r in (3, 2, 1)]

    def st(k, i):
        if k == 0:
            return [rc(S.at[i], W3.at[i, z, :, x, c, y], zs.at[i, n], zr.at[i, n], dev(q, x, c, y)) for n, q in enumerate(zp)]
        if k == 1:
            o = []
            for n, q in enumerate(far):
                a, b = W3.at[i, q, :, x, c, y, 0:RA], W3.at[i, q, :, x, c, y, RA:64]
                o += [rc(a, a, xs.at[i, 0, n], xr.at[i, 0, n], X), rc(b, b, ys.at[i, 0, n], yr.at[i, 0, n], Y)]
            return o
        if k == 2:
            o = []
            for n, q in enumerate(far):
                a, b = W3.at[i, q, :, :, c, y, 0:RA], W3.at[i, q, :, x, c, :, RA:64]
                o += [rc(b, b, xs.at[i, 1, n], xr.at[i, 1, n], X), rc(a, a, ys.at[i, 1, n], yr.at[i, 1, n], Y)]
            return o
        a = W3.at[i, :, :, :, c]
        return [rc(a, a, ds.at[i], dr.at[i], C)]

    def near(k):
        if k == 0:
            return [rc(S.at[:, :, 0:RA], W3.at[:, z, :, x, c, y, 0:RA], nxs.at[0], nxr.at[0], X),
                    rc(S.at[:, :, RA:64], W3.at[:, z, :, x, c, y, RA:64], nys.at[0], nyr.at[0], Y)]
        a, b = W3.at[:, z, :, :, c, y, 0:RA], W3.at[:, z, :, x, c, :, RA:64]
        return [rc(b, b, nxs.at[1], nxr.at[1], X), rc(a, a, nys.at[1], nyr.at[1], Y)]

    def quarter(r):
        n = r.shape[0] // 4
        return lambda a, b: r.at[pl.ds(pl.multiple_of((2 * a + b) * n, 128), n)]

    def wst(k, j):
        if k == 0:
            return [rc(quarter(own[j])(zb, c), quarter(par[j])(zb, c), wys.at[j], wyr.at[j], Y)]
        if k == 1:
            a = quarter(par[j])(zb, c)
            return [rc(a, a, wxs.at[j], wxr.at[j], ZP)]
        return [rc(quarter(par[j])(b, c), quarter(par[j])(b, c), wds.at[j, b], wdr.at[j, b], C) for b in (0, 1)]

    def near_step(k):
        if k == 1:
            mine.wait()
        if k > 0:
            for cp in near(k - 1):
                cp.wait_recv()
        if k < 2:
            for cp in near(k):
                cp.start()

    def weight_step(k, j):
        if k > 0:
            for cp in wst(k - 1, j):
                cp.wait_recv()
        if k < 3:
            for cp in wst(k, j):
                cp.start()

    def gather_step(k, i):
        came = st(k - 1, i) if k > 0 else []
        new = st(k, i) if k < 4 else []
        parts = 3 if k in (1, 2) else 1
        for m in range(parts):
            for cp in came[m * len(came) // parts : (m + 1) * len(came) // parts]:
                cp.wait_recv()
            for cp in new[m * len(new) // parts : (m + 1) * len(new) // parts]:
                cp.start()

    def gather_tick(t):
        for k in (4, 3, 2, 1, 0):
            i = t - k * SP

            @pl.when((i >= 0) & (i < NCH))
            def _():
                gather_step(k, i)

    def tick(t):
        if t == 0:
            near_step(0)
        for k in (3, 2, 1, 0):
            if 0 <= t - k * SPW < 5:
                weight_step(k, t - k * SPW)
        if t == NEAR:
            near_step(1)
        if t == 3 * SP:
            near_step(2)
        gather_tick(t)

    def silu(v):
        return v * jax.nn.sigmoid(v)

    def head(h):
        return pl.ds(pl.multiple_of(h * 128, 128), 128)

    tau = lax.broadcasted_iota(jnp.int32, (512, 1), 0).astype(f32)
    rho = lax.broadcasted_iota(jnp.int32, (1, 512), 1).astype(f32)

    def rate_of(h):
        return rates[h // 4, pl.ds(lax.rem(h, 4), 1), 0:1]

    def norm_rows():
        v = tokens[...].astype(f32)
        f = lax.rsqrt(jnp.mean(v * v, axis=1, keepdims=True) + epsilon)
        scal[:, 3:4] = f
        NM[...] = (v * f).astype(bf)
        pos = lax.broadcasted_iota(jnp.int32, (512, 1), 0) + y * 512
        keep = (pos < lengths[0]).astype(f32)
        scal[:, 0:1] = keep
        go[...] = (cot[...].astype(f32) * keep).astype(bf)
        LT[1] = go[...].T

    def project(j, h):
        cols = slice(h * 512, h * 512 + 512)
        v = dot(NM[...], WV[j])
        if j == 0:
            R[4, :, cols] = v.astype(bf)
            DMX[:, cols] = (v * jax.nn.sigmoid(v)).astype(bf)
        if j == 1:
            R[3, :, cols] = v.astype(bf)
            UN[:, cols] = (v * jax.nn.sigmoid(v)).astype(bf)
        if j == 2:
            R[2, :, cols] = v.astype(bf)
        if j == 3:
            DV[:, cols] = v
            R[1, :, cols] = v.astype(bf)

    def project_own(*js):
        for j in js:
            wload(j, 0).wait()
            project(j, 0)

    def project_part(j):
        wload(j, 1).wait()
        project(j, 1)

    def update(h, _):
        hs = head(h)
        kl = (UN[:, hs].astype(f32) * jnp.exp(-rate_of(h) * (511.0 - tau))).astype(bf)
        GS[lax.rem(h + 4, 8)] = dottn(kl, R[2, :, hs]).astype(bf)
        return 0

    hand = rc(GS, GR, gss, gsr, Y)
    ti = lax.broadcasted_iota(jnp.int32, (512, 512), 0)
    ri = lax.broadcasted_iota(jnp.int32, (512, 512), 1)

    def inner(h, _):
        hs = head(h)
        r = rate_of(h)
        within = jnp.where(ti >= ri, jnp.exp(-r * (tau + 1.0)) * jnp.exp(r * (rho + 1.0)), 0.0)
        ACC[:, hs] = dot((dotnt(DMX[:, hs], UN[:, hs]) * within).astype(bf), R[2, :, hs])
        return 0

    alive = (y == 1).astype(f32)

    def outer(h, _):
        hs = head(h)
        s = (GR[h].astype(f32) * alive).astype(bf)
        state[h] = s
        ACC[:, hs] = ACC[:, hs] + jnp.exp(-rate_of(h) * (tau + 1.0)) * dot(DMX[:, hs], s)
        return 0

    def gating():
        m = ACC[...]
        f = lax.rsqrt(jnp.mean(m * m, axis=1, keepdims=True) + epsilon)
        scal[:, 2:3] = f
        u = m * f
        UN[...] = u.astype(bf)
        R[0] = (u * DV[...]).astype(bf)

    def middle_rows():
        wload(4, 0).wait()
        wload(4, 1).wait()
        m = tokens[...].astype(f32) + dot(R[0, :, 0:512], WO[0]) + dot(R[0, :, 512:1024], WO[1])
        f = lax.rsqrt(jnp.mean(m * m, axis=1, keepdims=True) + epsilon)
        scal[:, 1:2] = f
        ACC[...] = m
        mid[...] = (m * f).astype(bf)
        LT[0] = mid[...].T

    def tload(i, s):
        return [pltpu.make_async_copy(W3.at[i, :, :, :, :, h], WT.at[s, :, :, :, :, :, pl.ds(h * 128, 128)], wsem.at[s, h]) for h in (0, 1)]

    def cps(k, i, hr):
        g, s, n = lax.rem(i, NCH), lax.rem(i, 4), 3 if hr else 1
        if k == 0:
            return [rc(G.at[g, 1 - c, 0:n], RD.at[lax.rem(i, 2), 0:n], e_s.at[i], e_r.at[i], C)]
        if k == 1:
            o = [rc(G.at[g, c, 0:n, :, :, 1 - y, hr:64], R1.at[s, 0:n, :, :, hr:64], fy_s.at[i, 0], fy_r.at[i, 0], Y)]
            if hr:
                o.append(rc(G.at[g, c, 0:n, :, 1 - x, :, 0:hr], R1.at[s, 0:n, :, :, 0:hr], fx_s.at[i, 0], fx_r.at[i, 0], X))
            return o
        if k == 2:
            o = [rc(G.at[g, c, 0:n, :, 1 - x, y, hr:64], R2.at[s, 0:n, :, hr:64], fx_s.at[i, 1], fx_r.at[i, 1], X)]
            if hr:
                o.append(rc(G.at[g, c, 0:n, :, x, 1 - y, 0:hr], R2.at[s, 0:n, :, 0:hr], fy_s.at[i, 1], fy_r.at[i, 1], Y))
            return o
        if k == 3:
            return [rc(Q.at[s, 0:n, q], RZ.at[s, m, 0:n], fz_s.at[i, m], fz_r.at[i, m], dev(q, x, c, y)) for m, q in enumerate(zp)]

    def ags(k, w):
        if k == 0:
            f = FN.at[lax.rem(w, 4)]
            return [rc(f, O.at[w, z, x, c], az_s.at[w, n], az_r.at[w, n], dev(q, x, c, y)) for n, q in enumerate(zp)]
        if k == 1:
            return [rc(O.at[w, :, x, c], O.at[w, :, x, c], ax_s.at[w], ax_r.at[w], X)]
        if k == 2:
            return [rc(O.at[w, :, :, c], O.at[w, :, :, c], ad_s.at[w], ad_r.at[w], C)]

    def flush(w):
        return pltpu.make_async_copy(FN.at[lax.rem(w, 4)], O.at[w, z, x, c], fl.at[w])

    def reduce(k, i, hr):
        g, s, n = lax.rem(i, NCH), lax.rem(i, 4), 3 if hr else 1
        up = lambda v: v.astype(f32)
        if k == 1:
            G[g, c, 0:n] = (up(G[g, c, 0:n]) + up(RD[lax.rem(i, 2), 0:n])).astype(bf)
        if k == 2:
            if hr:
                G[g, c, 0:n, :, x, :, 0:hr] = (up(G[g, c, 0:n, :, x, :, 0:hr]) + up(R1[s, 0:n, :, :, 0:hr])).astype(bf)
            G[g, c, 0:n, :, :, y, hr:64] = (up(G[g, c, 0:n, :, :, y, hr:64]) + up(R1[s, 0:n, :, :, hr:64])).astype(bf)
        if k == 3:
            Q[s, 0:n] = (up(G[g, c, 0:n, :, x, y]) + up(R2[s, 0:n])).astype(bf)
        if k == 4:
            v = up(Q[s, 0:n, z])
            for m in range(3):
                v = v + up(RZ[s, m, 0:n])
            if hr:
                sh[:, :, pl.ds(pl.multiple_of(i * 128, 128), 128)] = v
            else:
                FN[lax.rem(i - NCH, 4)] = v[0].astype(bf)

    def arrive(k, i, hr):
        if k > 0:
            for cp in cps(k - 1, i, hr):
                cp.wait_recv()
        if k == 1:
            for cp in cps(0, i, hr):
                cp.wait_send()
        if k == 4:
            for kk in (1, 2, 3):
                for cp in cps(kk, i, hr):
                    cp.wait_send()
        reduce(k, i, hr)

    def leave(k, i, hr):
        for cp in cps(k, i, hr):
            cp.start()

    def both(f, k, t):
        i = t - RS_AT[k]

        @pl.when((i >= 0) & (i < NCH))
        def _():
            f(k, i, HR)

        @pl.when((i >= NCH) & (i < NALL))
        def _():
            f(k, i, 0)

    def ag_arrive(k, t):
        w = t - AG_AT[k] - NCH

        @pl.when((w >= 0) & (w < NWG))
        def _():
            for cp in ags(k, w):
                cp.wait_recv()
            if k == 0:
                for cp in ags(0, w):
                    cp.wait_send()
                flush(w).wait()

    def ag_leave(k, t):
        w = t - (AG_AT[k - 1] if k else RS_AT[4]) - NCH

        @pl.when((w >= 0) & (w < NWG))
        def _():
            for cp in ags(k, w):
                cp.start()
            if k == 0:
                flush(w).start()

    def stages(t):
        ag_arrive(2, t)
        ag_arrive(1, t)
        ag_arrive(0, t)
        ag_leave(2, t)
        both(arrive, 4, t)
        ag_leave(1, t)
        both(arrive, 3, t)
        ag_leave(0, t)
        both(arrive, 2, t)
        both(leave, 3, t)
        both(arrive, 1, t)
        for k in (2, 1, 0):
            both(leave, k, t)

    def store(g, t, r, own):
        r = r.astype(bf).reshape(4, 2, 2, 64, 256)
        for cc in (0, 1):
            G[g, cc, t, :, :, own] = r[:, :, cc, :, 0:128]
            G[g, cc, t, :, :, 1 - own] = r[:, :, cc, :, 128:256]

    def ffn(t):
        s = lax.rem(t, 2)
        for cp in tload(t, s):
            cp.wait()

        @pl.when(t + 1 < NCH)
        def _():
            for cp in tload(t + 1, 1 - s):
                cp.start()

        fv, fg, fo = [WT[s, :, n].reshape(1024, 256) for n in range(3)]
        m, g_ = mid[...], go[...]
        v, g, gh = dot(m, fv), dot(m, fg), dot(g_, fo)
        hid, dv, dg = (v * g).astype(bf), (gh * g).astype(bf), (gh * v).astype(bf)
        ACC[...] += dotnt(hid, fo)
        dtok[...] += dotnt(dv, fv) + dotnt(dg, fg)
        store(t, 0, dot(LT[0], dv), 0)
        store(t, 1, dot(LT[0], dg), 0)
        store(t, 2, dot(LT[1], hid), 0)

    def ffn_tick(t, _):
        stages(t)

        def one(n, _):
            ffn(n)
            return 0

        lax.fori_loop(jnp.maximum(t, 2 * t - 7), jnp.maximum(t + 1, 2 * t - 5), one, 0)
        return 0

    T = 9
    loops = lambda f, a, b: lax.fori_loop(a, b, f, 0)
    W = 3 * SPW
    for t in range(MEET):
        tick(t)
        if t == 0:
            rate.start()
            norm_rows()
        if t == 1:
            project_own(0, 1)
        if t == 2:
            project_own(2, 3)
        if W <= t < W + 5:
            wload(t - W, 1).start()
        if W + 1 <= t < W + 5:
            project_part(t - W - 1)
        if t == W + 3:
            rate.wait()
            loops(update, 0, 8)
            hand.start()
        if t == W + 4:
            loops(inner, 0, 8)
        if t == W + 6:
            hand.wait()
            loops(outer, 0, 8)
            gating()
            middle_rows()
            for cp in tload(0, 0):
                cp.start()

    def meet_tick(t, _):
        gather_tick(t)
        return ffn_tick(t - MEET, 0)

    lax.fori_loop(MEET, NCH + 4 * SP, meet_tick, 0)
    lax.fori_loop(NCH + 4 * SP - MEET, T, ffn_tick, 0)
    stages(T)
    keep, scale_mid, scale_out, scale_in = [scal[:, n : n + 1] for n in range(4)]
    output[...] = (ACC[...] * keep).astype(bf)
    n2 = mid[...].astype(f32)
    dm = dtok[...]
    gm = go[...].astype(f32) + scale_mid * (dm - n2 * jnp.mean(dm * n2, axis=1, keepdims=True))
    dtok[...] = gm
    gml = gm.astype(bf)
    LT[0] = gml.T
    LT[1] = NM[...].T
    for h in (0, 1):
        cols = slice(h * 512, h * 512 + 512)
        ACC[:, cols] = dotnt(gml, WO[h])
    stages(T + 1)
    dgt, un = ACC[...], UN[...].astype(f32)
    du = dgt * R[1].astype(f32)
    R[1] = (dgt * un).astype(bf)
    DMX[...] = (scale_out * (du - un * jnp.mean(du * un, axis=1, keepdims=True))).astype(bf)

    def first(h, _):
        hs = head(h)
        q = silu(R[4, :, hs].astype(f32)).astype(bf)
        gf = (DMX[:, hs].astype(f32) * jnp.exp(-rate_of(h) * (tau + 1.0))).astype(bf)
        GS2[lax.rem(h + 4, 8)] = dottn(q, gf).astype(bf)
        return 0

    lax.fori_loop(0, 8, first, 0)
    later = rc(GS2, GR2, g2s, g2r, Y)
    later.start()
    def pair(h, _):
        hs = head(h)
        qp, kp = R[4, :, hs].astype(f32), R[3, :, hs].astype(f32)
        q, k, v, dmx = silu(qp).astype(bf), silu(kp).astype(bf), R[2, :, hs], DMX[:, hs]
        cf, rf = jnp.exp(-rate_of(h) * (tau + 1.0)), jnp.exp(rate_of(h) * (rho + 1.0))
        within = jnp.where(ti >= ri, cf * rf, 0.0)
        wt = (dotnt(q, k) * within).astype(bf)
        dsc = (dotnt(dmx, v) * within).astype(bf)
        gf = (dmx.astype(f32) * cf).astype(bf)
        dq = dot(dsc, k) + dotnt(gf, state[h])
        ACC[:, hs] = dottn(dsc, q)
        DV[:, hs] = dottn(wt, dmx)
        sq = jax.nn.sigmoid(qp)
        R[4, :, hs] = (dq * (sq * (1.0 + qp * (1.0 - sq)))).astype(bf)
        return 0

    live = (y == 0).astype(f32)

    def finish(h, _):
        hs = head(h)
        gin = (GR2[h].astype(f32) * live).astype(bf)
        kp = R[3, :, hs].astype(f32)
        sk = jax.nn.sigmoid(kp)
        k = (kp * sk).astype(bf)
        lf = jnp.exp(-rate_of(h) * (511.0 - tau))
        kl = (k.astype(f32) * lf).astype(bf)
        dk = ACC[:, hs] + lf * dotnt(R[2, :, hs], gin)
        R[2, :, hs] = (DV[:, hs] + dot(kl, gin)).astype(bf)
        R[3, :, hs] = (dk * (sk * (1.0 + kp * (1.0 - sk)))).astype(bf)
        return 0

    def wgrad(p):
        j, cp = p // 4, lax.rem(p, 4)
        lo = pl.multiple_of(cp * 128, 128)
        rr = jnp.concatenate([R[j, :, pl.ds(lo, 128)], R[j, :, pl.ds(lo + 512, 128)]], axis=1)
        store(lax.rem(p, NCH), 0, dot(LT[jnp.minimum(j, 1)], rr), y)

    def wg_tick(t, _):
        stages(t)
        p = t - NCH
        wgrad(p)

        @pl.when(p < 8)
        def _():
            pair(p, 0)

        @pl.when(p == 7)
        def _():
            later.wait()
            lax.fori_loop(0, 8, finish, 0)

        for n in range(8):
            @pl.when(p == n + 8)
            def _():
                wbload(n).wait()

        @pl.when((p >= 8) & (p < 16))
        def _():
            n = p - 8
            j, h = 1 + n // 2, lax.rem(n, 2)
            part = dotnt(R[j, :, pl.ds(pl.multiple_of(h * 512, 128), 512)], WV[h])
            ACC[...] = jnp.where(n == 0, 0.0, ACC[...]) + part

        for n in range(6):
            @pl.when(p == n + 8)
            def _():
                wbload(n + 2).start()

        @pl.when(p == 16)
        def _():
            n1 = NM[...].astype(f32)
            dn = ACC[...]
            dtok[...] = dtok[...] + scale_in * (dn - n1 * jnp.mean(dn * n1, axis=1, keepdims=True))

        return 0

    mats = (wg, pg, wv, pv, wk, pk, wq, pq)

    def wbload(n):
        return pltpu.make_async_copy(mats[n], WV.at[n % 2], bsem.at[n % 2])

    wbload(0).start()
    wbload(1).start()
    lax.fori_loop(NCH, NCH + NWG, wg_tick, 0)
    def tail(t, _):
        stages(t)
        return 0

    lax.fori_loop(NALL, NALL + AG_AT[2], tail, 0)

    def drain(w, _):
        for k in (1, 2):
            for cp in ags(k, w):
                cp.wait_send()
        return 0

    lax.fori_loop(0, NWG, drain, 0)

    def drain_gather(i, _):
        for k in range(4):
            for cp in st(k, i):
                cp.wait_send()
        return 0

    lax.fori_loop(0, NCH, drain_gather, 0)
    for k in (0, 1):
        for cp in near(k):
            cp.wait_send()
    for j in range(5):
        for k in range(3):
            for cp in wst(k, j):
                cp.wait_send()


def layer_call(*ins):
    D, V, S = pltpu.SemaphoreType.DMA, pltpu.VMEM, jax.ShapeDtypeStruct
    A, VM = pl.BlockSpec(memory_space=pl.ANY), pl.BlockSpec(memory_space=pltpu.VMEM)
    act, w = (512, 1024), (1024, 512)
    outs = [S(act, bf), S(act, f32), S((3, 64, 1408), f32), S((NWG, 4, 2, 2, 64, 128), bf), S((NCH, 4, 3, 2, 2, 2, 64, 128), bf)] + [S(w, bf)] * 4 + [S(act, bf)]
    scratch = [V((NCH, 3, 64, 128), bf), V((4,) + w, bf), V((2,) + act, bf),
               V((NCH, 2, 3, 4, 2, 2, 64, 128), bf), V((2, 3, 4, 2, 2, 64, 128), bf), V((4, 3, 4, 2, 64, 128), bf), V((4, 3, 4, 64, 128), bf),
               V((4, 3, 4, 64, 128), bf), V((4, 3, 3, 64, 128), bf), V((4, 64, 128), bf), V((2, 4, 3, 2, 2, 64, 256), bf),
               V((2,) + w, bf), V(act, f32), V(act, f32), V((5,) + act, bf), V(act, bf), V(act, bf), V(act, bf), V(act, bf), V(act, bf),
               V((512, 4), f32), V((2, 8, 128), f32)] + [V((8, 128, 128), bf)] * 5
    n, m, a = (NCH,), (NALL,), (NWG,)
    scratch += [D(s) for s in ((NCH, 3), (NCH, 3), (NCH, 2, 3), (NCH, 2, 3), (NCH, 2, 3), (NCH, 2, 3), (2,), (2,), (2,), (2,), n, n,
                               (5,), (5,), (5,), (5,), (5, 2), (5, 2), (), (), (), (), (), (10,),
                               (2, 2), (2,), (), (), m, m, (NALL, 2), (NALL, 2), (NALL, 2), (NALL, 2), (NALL, 3), (NALL, 3),
                               (NWG, 3), (NWG, 3), a, a, a, a, a)]
    return pl.pallas_call(
        layer_kernel,
        out_shape=outs,
        in_specs=[VM, VM, pl.BlockSpec(memory_space=pltpu.SMEM)] + [VM] * 4 + [A] * 5,
        out_specs=[VM] * 3 + [A] * 7,
        scratch_shapes=scratch,
        compiler_params=pltpu.CompilerParams(collective_id=1, has_side_effects=True, vmem_limit_bytes=67043328),
    )(*ins)
def finish_kernel(o, sh, out, dtok, output, d_tokens, d_query, d_key, d_value, d_gate, d_out, d_f_value, d_f_gate, d_f_out):
    output[...] = out[...]
    d_tokens[...] = dtok[...]
    for n in range(4):
        cols = slice(n * 128, n * 128 + 128)
        d_out[cols, :] = o[n].astype(f32).T
        d_gate[:, cols] = o[4 + n].astype(f32)
        d_value[:, cols] = o[8 + n].astype(f32)
        d_key[:, cols] = o[12 + n].astype(f32)
        d_query[:, cols] = o[16 + n].astype(f32)

    @pl.when(pl.program_id(0) == 0)
    def _():
        d_f_value[...] = sh[0]
        d_f_gate[...] = sh[1]
        d_f_out[...] = sh[2]


def finish_call(o, sh, out, dtok):
    S = jax.ShapeDtypeStruct
    whole = lambda *s: pl.BlockSpec(s, lambda i: (0,) * len(s))
    return pl.pallas_call(
        finish_kernel,
        grid=(4,),
        out_shape=[S((512, 1024), bf), S((512, 1024), f32)] + [S((1024, 512), f32)] * 4 + [S((512, 1024), f32)] + [S((64, 1408), f32)] * 3,
        in_specs=[pl.BlockSpec((20, 256, 128), lambda i: (0, i, 0)), whole(3, 64, 1408)] + [pl.BlockSpec((128, 1024), lambda i: (i, 0))] * 2,
        out_specs=[pl.BlockSpec((128, 1024), lambda i: (i, 0))] * 2 + [pl.BlockSpec((256, 512), lambda i: (i, 0))] * 4 + [pl.BlockSpec((512, 256), lambda i: (0, i))] + [whole(64, 1408)] * 3,
        compiler_params=pltpu.CompilerParams(vmem_limit_bytes=67043328),
    )(o, sh, out, dtok)

def fast_body(tokens, lengths, decay, w_query, w_key, w_value, w_gate, w_out, f_value, f_gate, f_out, cotangent):
    dec = jnp.concatenate([jnp.broadcast_to(decay[:, None], (4, 128)), jnp.zeros((4, 128), f32)])
    weights = (w_query, w_key, w_value, w_gate, w_out)
    output, d_tokens, shares, grads, *_ = layer_call(tokens, cotangent, lengths, dec, f_value, f_gate, f_out.T, *weights)
    *results, d_f_out = finish_call(grads.reshape(NWG, 1024, 128), shares, output, d_tokens)
    return (*results, d_f_out.T)


def solution(mesh):
    placed = (
        P(("dp", "head"), None),
        P("dp"),
        P("head"),
        P(None, "head"),
        P(None, "head"),
        P(None, "head"),
        P(None, "head"),
        P("head", None),
        P("dp", "head"),
        P("dp", "head"),
        P("head", "dp"),
        P(("dp", "head"), None),
    )
    fast = mesh.shape["dp"] == 16 and mesh.shape["head"] == 2
    return jax.shard_map(
        fast_body if fast else general_body,
        mesh=mesh,
        in_specs=placed,
        out_specs=(
            P(("dp", "head"), None),
            P(("dp", "head"), None),
            P(None, "head"),
            P(None, "head"),
            P(None, "head"),
            P(None, "head"),
            P("head", None),
            P("dp", "head"),
            P("dp", "head"),
            P("head", "dp"),
        ),
        check_vma=False,
    )
```

```python
import jax
import jax.numpy as jnp
from jax import lax
from jax.experimental import pallas as pl
from jax.experimental.pallas import tpu as pltpu
from jax.sharding import PartitionSpec as P

D = 1024
HD = 128
SEQ_DEV = 1
SLOT = 1024
BLOCK = 512


epsilon = 1e-06


def normalize(values):
    factor = lax.rsqrt(jnp.mean(values * values, axis=-1, keepdims=True) + epsilon)
    return (values * factor, factor)


def norm_back(grad_normed, normed, factor):
    inner_sum = jnp.mean(grad_normed * normed, axis=-1, keepdims=True)
    return factor * (grad_normed - normed * inner_sum)


def silu_slope(values):
    sigmoid = jax.nn.sigmoid(values)
    return sigmoid * (1.0 + values * (1.0 - sigmoid))


def matmul(left_side, right_side):
    return jnp.dot(left_side, right_side, preferred_element_type=jnp.float32)


def matmul_right_t(left_side, right_side):
    return lax.dot_general(
        left_side, right_side, (((1,), (1,)), ((), ())), preferred_element_type=jnp.float32
    )


def matmul_left_t(left_side, right_side):
    return lax.dot_general(
        left_side, right_side, (((0,), (0,)), ((), ())), preferred_element_type=jnp.float32
    )


def exact(form, left_side, right_side):
    return jnp.einsum(form, left_side, right_side, precision=lax.Precision.HIGHEST)


def decay_tables(rates):
    offsets = jnp.arange(BLOCK).astype(jnp.float32)
    spread = offsets[:, None] - offsets[None, :]
    causal = spread >= 0
    within = jnp.where(
        causal[None], jnp.exp(-rates[:, None, None] * jnp.where(causal, spread, 0.0)[None]), 0.0
    )
    first_decay = jnp.exp(-rates[:, None] * (offsets[None, :] + 1.0))
    last_decay = jnp.exp(-rates[:, None] * (BLOCK - 1.0 - offsets[None, :]))
    block_decay = jnp.exp(-rates * BLOCK)
    return (within, first_decay, last_decay, block_decay)


def to_blocks(values, heads):
    shaped = values.reshape(SEQ_DEV, SLOT // BLOCK, BLOCK, heads, HD)
    return shaped.transpose(1, 0, 3, 2, 4)


def from_blocks(blocks):
    return blocks.transpose(1, 0, 3, 2, 4).reshape(-1, blocks.shape[2] * blocks.shape[4])


def lightning_forward(query, keys, values, tables):
    within, first_decay, last_decay, block_decay = tables

    def advance(carried, inputs):
        query_blk, keys_blk, values_blk = inputs
        scores = jnp.einsum(
            "shbd,shcd->shbc", query_blk, keys_blk, preferred_element_type=jnp.float32
        )
        weights = (scores * within[None]).astype(jnp.bfloat16)
        inner_sum = jnp.einsum(
            "shbc,shcd->shbd", weights, values_blk, preferred_element_type=jnp.float32
        )
        outer_sum = first_decay[None, :, :, None] * exact(
            "shbd,shde->shbe", query_blk.astype(jnp.float32), carried
        )
        keys_scaled = keys_blk.astype(jnp.float32) * last_decay[None, :, :, None]
        update = exact("shbd,shbe->shde", keys_scaled, values_blk.astype(jnp.float32))
        return (
            block_decay[None, :, None, None] * carried + update,
            (inner_sum + outer_sum, carried),
        )

    initial = jnp.zeros((SEQ_DEV, query.shape[2], HD, HD), jnp.float32)
    final_state, (mixed, states) = lax.scan(advance, initial, (query, keys, values))
    return (mixed, states)


def lightning_backward(query, keys, values, grads, states, tables):
    within, first_decay, last_decay, block_decay = tables

    def retreat(later_grad, inputs):
        query_blk, keys_blk, values_blk, grad_blk, carried = inputs
        scores = jnp.einsum(
            "shbd,shcd->shbc", query_blk, keys_blk, preferred_element_type=jnp.float32
        )
        weights = (scores * within[None]).astype(jnp.bfloat16)
        d_weights = jnp.einsum(
            "shbd,shcd->shbc", grad_blk, values_blk, preferred_element_type=jnp.float32
        )
        d_scores = (d_weights * within[None]).astype(jnp.bfloat16)
        d_query = jnp.einsum(
            "shbc,shcd->shbd", d_scores, keys_blk, preferred_element_type=jnp.float32
        )
        d_keys = jnp.einsum(
            "shbc,shbd->shcd", d_scores, query_blk, preferred_element_type=jnp.float32
        )
        d_values = jnp.einsum(
            "shbc,shbd->shcd", weights, grad_blk, preferred_element_type=jnp.float32
        )
        grad_scaled = grad_blk.astype(jnp.float32) * first_decay[None, :, :, None]
        keys_scaled = keys_blk.astype(jnp.float32) * last_decay[None, :, :, None]
        d_query = d_query + exact("shbe,shde->shbd", grad_scaled, carried)
        d_keys = d_keys + last_decay[None, :, :, None] * exact(
            "shbe,shde->shbd", values_blk.astype(jnp.float32), later_grad
        )
        d_values = d_values + exact("shbd,shde->shbe", keys_scaled, later_grad)
        earlier = block_decay[None, :, None, None] * later_grad + exact(
            "shbd,shbe->shde", query_blk.astype(jnp.float32), grad_scaled
        )
        return (earlier, (d_query, d_keys, d_values))

    initial = jnp.zeros((SEQ_DEV, query.shape[2], HD, HD), jnp.float32)
    first_grad, results = lax.scan(
        retreat, initial, (query, keys, values, grads, states), reverse=True
    )
    return results


def general_body(
    tokens,
    lengths,
    decay,
    w_query,
    w_key,
    w_value,
    w_gate,
    w_out,
    f_value,
    f_gate,
    f_out,
    cotangent,
):
    own_rows = tokens.shape[0]
    first_row = lax.axis_index("head") * own_rows
    heads_here = decay.shape[0]
    tables = decay_tables(decay)
    positions = first_row + jnp.arange(own_rows, dtype=jnp.int32)
    slot_match = (positions // SLOT)[:, None] == jnp.arange(SEQ_DEV, dtype=jnp.int32)[None, :]
    length_of = jnp.sum(jnp.where(slot_match, lengths[None, :], 0), axis=1)
    keep_rows = (positions % SLOT < length_of).astype(jnp.float32)[:, None]
    inputs_f = tokens.astype(jnp.float32)
    normed, scale_in = normalize(inputs_f)
    gathered = lax.all_gather(normed.astype(jnp.bfloat16), "head", axis=0, tiled=True)
    query_pre = matmul(gathered, w_query)
    keys_pre = matmul(gathered, w_key)
    values_pre = matmul(gathered, w_value)
    gate_pre = matmul(gathered, w_gate)
    query_blocks = to_blocks(jax.nn.silu(query_pre).astype(jnp.bfloat16), heads_here)
    keys_blocks = to_blocks(jax.nn.silu(keys_pre).astype(jnp.bfloat16), heads_here)
    values_blocks = to_blocks(values_pre.astype(jnp.bfloat16), heads_here)
    mixed_blocks, states = lightning_forward(query_blocks, keys_blocks, values_blocks, tables)
    mixed = from_blocks(mixed_blocks)
    squares = lax.psum(jnp.sum(mixed * mixed, axis=1), "head")
    scale_out = lax.rsqrt(squares / D + epsilon)[:, None]
    mixed_unit = mixed * scale_out
    gated = (mixed_unit * gate_pre).astype(jnp.bfloat16)
    branch = lax.psum_scatter(
        matmul(gated, w_out).astype(jnp.bfloat16), "head", scatter_dimension=0, tiled=True
    ).astype(jnp.float32)
    middle = inputs_f + branch
    mid_normed, scale_mid = normalize(middle)
    mid_all = lax.all_gather(mid_normed.astype(jnp.bfloat16), "head", axis=0, tiled=True)
    value_full, gate_full = (
        lax.all_gather(f_value, "dp", axis=0, tiled=True),
        lax.all_gather(f_gate, "dp", axis=0, tiled=True),
    )
    down_full = lax.all_gather(f_out, "dp", axis=1, tiled=True)
    value_ffn = matmul(mid_all, value_full)
    gate_ffn = matmul(mid_all, gate_full)
    hidden = (value_ffn * gate_ffn).astype(jnp.bfloat16)
    ffn_branch = lax.psum_scatter(
        matmul(hidden, down_full).astype(jnp.bfloat16), "head", scatter_dimension=0, tiled=True
    ).astype(jnp.float32)
    output = ((middle + ffn_branch) * keep_rows).astype(jnp.bfloat16)
    grad_out = cotangent.astype(jnp.float32) * keep_rows
    grad_all = lax.all_gather(grad_out.astype(jnp.bfloat16), "head", axis=0, tiled=True)
    grad_hidden = matmul_right_t(grad_all, down_full)
    d_value_ffn = (grad_hidden * gate_ffn).astype(jnp.bfloat16)
    d_gate_ffn = (grad_hidden * value_ffn).astype(jnp.bfloat16)
    d_mid_normed = lax.psum_scatter(
        (matmul_right_t(d_value_ffn, value_full) + matmul_right_t(d_gate_ffn, gate_full)).astype(
            jnp.bfloat16
        ),
        "head",
        scatter_dimension=0,
        tiled=True,
    ).astype(jnp.float32)
    grad_middle = grad_out + norm_back(d_mid_normed, mid_normed, scale_mid)
    joined = jnp.concatenate([d_value_ffn, d_gate_ffn], axis=1)
    hidden_here = hidden.shape[1]
    shares = lax.psum_scatter(
        jnp.concatenate(
            [matmul_left_t(mid_all, joined), matmul_left_t(grad_all, hidden)], axis=1
        ).astype(jnp.bfloat16),
        "dp",
        scatter_dimension=0,
        tiled=True,
    ).astype(jnp.float32)
    d_f_value = shares[:, :hidden_here]
    d_f_gate = shares[:, hidden_here : 2 * hidden_here]
    d_f_out = shares[:, 2 * hidden_here :].T
    grad_rows = lax.all_gather(grad_middle.astype(jnp.bfloat16), "head", axis=0, tiled=True)
    d_gated = matmul_right_t(grad_rows, w_out)
    d_w_out_local = matmul_left_t(gated, grad_rows)
    d_gate_pre = (d_gated * mixed_unit).astype(jnp.bfloat16)
    d_unit = d_gated * gate_pre
    inner_out = lax.psum(jnp.sum(d_unit * mixed_unit, axis=1), "head")
    d_mixed = (scale_out * (d_unit - mixed_unit * (inner_out / D)[:, None])).astype(jnp.bfloat16)
    d_query, d_keys, d_values = lightning_backward(
        query_blocks, keys_blocks, values_blocks, to_blocks(d_mixed, heads_here), states, tables
    )
    d_query_pre = (from_blocks(d_query) * silu_slope(query_pre)).astype(jnp.bfloat16)
    d_keys_pre = (from_blocks(d_keys) * silu_slope(keys_pre)).astype(jnp.bfloat16)
    d_values_pre = from_blocks(d_values).astype(jnp.bfloat16)
    total = matmul_right_t(d_query_pre, w_query) + matmul_right_t(d_keys_pre, w_key)
    d_normed = lax.psum_scatter(
        (total + matmul_right_t(d_values_pre, w_value) + matmul_right_t(d_gate_pre, w_gate)).astype(
            jnp.bfloat16
        ),
        "head",
        scatter_dimension=0,
        tiled=True,
    ).astype(jnp.float32)
    d_tokens = grad_middle + norm_back(d_normed, normed, scale_in)
    grads_attention = (
        lax.psum(matmul_left_t(gathered, d_query_pre).astype(jnp.bfloat16), "dp").astype(
            jnp.float32
        ),
        lax.psum(matmul_left_t(gathered, d_keys_pre).astype(jnp.bfloat16), "dp").astype(
            jnp.float32
        ),
        lax.psum(matmul_left_t(gathered, d_values_pre).astype(jnp.bfloat16), "dp").astype(
            jnp.float32
        ),
        lax.psum(matmul_left_t(gathered, d_gate_pre).astype(jnp.bfloat16), "dp").astype(
            jnp.float32
        ),
        lax.psum(d_w_out_local.astype(jnp.bfloat16), "dp").astype(jnp.float32),
    )
    return (
        output,
        d_tokens,
        grads_attention[0],
        grads_attention[1],
        grads_attention[2],
        grads_attention[3],
        grads_attention[4],
        d_f_value,
        d_f_gate,
        d_f_out,
    )


MESH = pl.DeviceIdType.MESH
NCH = 11
RA = 16
HR = 32
SP = 2
NEAR = 2
MEET = 10
W_AT = (0, 2, 4, 5)
HAND = 4
SLOTS = 4
SLOT1 = 4
NF = NCH
NWG = 20
NALL = NCH + NWG

RS_AT = (1, 2, 4, 6, 8)
AG_AT = (10, 12, 14)
TN = (((0,), (0,)), ((), ()))
bf = jnp.bfloat16
f32 = jnp.float32
NT = (((1,), (1,)), ((), ()))


def dot(a, b):
    return jnp.dot(a, b, preferred_element_type=f32)


def dotnt(a, b):
    return lax.dot_general(a, b, NT, preferred_element_type=f32)


def dottn(a, b):
    return lax.dot_general(a, b, TN, preferred_element_type=f32)


def place():
    d=lax.axis_index("dp")
    return d//4, (d//2)%2, d%2, lax.axis_index("head")
def dev(z,x,c,y): return ((z*2+x)*2+c, y)
def layer_kernel(tokens, cot, lengths, dec, fv, fg, fo, wq, wk, wv, wg, wo,
                 output, d_tokens, shares, O, W3, pq, pk, pv, pg, po,
                 S, WV, WO, G, RD, R1, R2, Q, RZ, FN, WT, LT, ACC, DV, R, UN, NM, DMX, mid, go, scal, rates, state, GS, GR, GS2, GR2, TK, OUT, dtok, sh,
                 zs, zr, xs, xr, ys, yr, nxs, nxr, nys, nyr, ds, dr, wys, wyr, wxs, wxr, wds, wdr, gss, gsr, rss, rsr, ls, ws,
                 wsem, bsem, g2s, g2r, e_s, e_r, fx_s, fx_r, fy_s, fy_r, fz_s, fz_r, az_s, az_r, ax_s, ax_r, ad_s, ad_r, fl, io):
    z, x, c, y = place()
    zp = [lax.rem(z + r, 4) for r in (1, 2, 3)]
    X, Y, C = dev(z, 1 - x, c, y), dev(z, x, c, 1 - y), dev(z, x, 1 - c, y)
    zb = lax.rem(z, 2)
    ZP = dev(z + 1 - 2 * zb, x, c, y)
    bar = pltpu.get_barrier_semaphore()
    peers = [dev(q, x, c, y) for q in zp] + [X, Y, C]
    for p in peers:
        pl.semaphore_signal(bar, inc=1, device_id=p, device_id_type=MESH)
    ins = [pltpu.make_async_copy(tokens, TK, io.at[0]), pltpu.make_async_copy(cot, go, io.at[1])]
    for cp in ins:
        cp.start()
    outs = [pltpu.make_async_copy(a, b, io.at[2 + n]) for n, (a, b) in enumerate(((OUT, output), (dtok, d_tokens), (sh, shares)))]
    own, par = (wk, wv, wq, wg, wo), (pk, pv, pq, pg, po)

    def rc(src, dst, ss, rs, d):
        return pltpu.make_async_remote_copy(src_ref=src, dst_ref=dst, send_sem=ss, recv_sem=rs, device_id=d, device_id_type=MESH)

    def wload(j, h):
        src = (own if h == 0 else par)[j]
        dst = WV.at[j] if j < 4 else WO.at[h]
        return pltpu.make_async_copy(src, dst, ws.at[2 * j + h])

    for j in range(5):
        wload(j, 0).start()
    for i in range(NCH):
        S[i, 0] = fv[:, i * 128 : i * 128 + 128]
        S[i, 1] = fg[:, i * 128 : i * 128 + 128]
        S[i, 2] = fo[:, i * 128 : i * 128 + 128]
    for h in range(4):
        rates[0, h : h + 1, :] = jnp.full((1, 128), dec[h], f32)
    dtok[...] = jnp.zeros_like(dtok)
    pl.semaphore_wait(bar, len(peers))
    mine = pltpu.make_async_copy(S, W3.at[:, z, :, x, c, y], ls)
    mine.start()
    rate = rc(rates.at[0], rates.at[1], rss, rsr, Y)

    far = [lax.rem(z + r, 4) for r in (3, 2, 1)]

    def st(k, i):
        if k == 0:
            return [rc(S.at[i], W3.at[i, z, :, x, c, y], zs.at[i, n], zr.at[i, n], dev(q, x, c, y)) for n, q in enumerate(zp)]
        if k == 1:
            o = []
            for n, q in enumerate(far):
                a, b = W3.at[i, q, :, x, c, y, 0:RA], W3.at[i, q, :, x, c, y, RA:64]
                o += [rc(a, a, xs.at[i, 0, n], xr.at[i, 0, n], X), rc(b, b, ys.at[i, 0, n], yr.at[i, 0, n], Y)]
            return o
        if k == 2:
            o = []
            for n, q in enumerate(far):
                a, b = W3.at[i, q, :, :, c, y, 0:RA], W3.at[i, q, :, x, c, :, RA:64]
                o += [rc(b, b, xs.at[i, 1, n], xr.at[i, 1, n], X), rc(a, a, ys.at[i, 1, n], yr.at[i, 1, n], Y)]
            return o
        a = W3.at[i, :, :, :, c]
        return [rc(a, a, ds.at[i], dr.at[i], C)]

    def near(k):
        if k == 0:
            return [rc(S.at[:, :, 0:RA], W3.at[:, z, :, x, c, y, 0:RA], nxs.at[0], nxr.at[0], X),
                    rc(S.at[:, :, RA:64], W3.at[:, z, :, x, c, y, RA:64], nys.at[0], nyr.at[0], Y)]
        a, b = W3.at[:, z, :, :, c, y, 0:RA], W3.at[:, z, :, x, c, :, RA:64]
        return [rc(b, b, nxs.at[1], nxr.at[1], X), rc(a, a, nys.at[1], nyr.at[1], Y)]

    def quarter(r):
        n = r.shape[0] // 4
        return lambda a, b: r.at[pl.ds(pl.multiple_of((2 * a + b) * n, 128), n)]

    def wst(k, j):
        if k == 0:
            return [rc(quarter(own[j])(zb, c), quarter(par[j])(zb, c), wys.at[j], wyr.at[j], Y)]
        if k == 1:
            a = quarter(par[j])(zb, c)
            return [rc(a, a, wxs.at[j], wxr.at[j], ZP)]
        return [rc(quarter(par[j])(b, c), quarter(par[j])(b, c), wds.at[j, b], wdr.at[j, b], C) for b in (0, 1)]

    def near_step(k):
        if k == 1:
            mine.wait()
        if k > 0:
            for cp in near(k - 1):
                cp.wait_recv()
        if k < 2:
            for cp in near(k):
                cp.start()

    def weight_step(k, j):
        if k > 0:
            for cp in wst(k - 1, j):
                cp.wait_recv()
        if k < 3:
            for cp in wst(k, j):
                cp.start()

    def gather_step(k, i):
        came = st(k - 1, i) if k > 0 else []
        new = st(k, i) if k < 4 else []
        parts = 3 if k in (1, 2) else 1
        for m in range(parts):
            for cp in came[m * len(came) // parts : (m + 1) * len(came) // parts]:
                cp.wait_recv()
            for cp in new[m * len(new) // parts : (m + 1) * len(new) // parts]:
                cp.start()

    def gather_tick(t):
        for k in (4, 3, 2, 1, 0):
            i = t - k * SP

            @pl.when((i >= 0) & (i < NCH))
            def _():
                gather_step(k, i)

    def tick(t):
        if t == 0:
            near_step(0)
        if t == NEAR:
            near_step(1)
        for k in (3, 2, 1, 0):
            if 0 <= t - W_AT[k] < 5:
                weight_step(k, t - W_AT[k])
        if t == 3 * SP:
            near_step(2)
        gather_tick(t)

    def silu(v):
        return v * jax.nn.sigmoid(v)

    def head(h):
        return pl.ds(pl.multiple_of(h * 128, 128), 128)

    tau = lax.broadcasted_iota(jnp.int32, (512, 1), 0).astype(f32)
    rho = lax.broadcasted_iota(jnp.int32, (1, 512), 1).astype(f32)

    def rate_of(h):
        return rates[h // 4, pl.ds(lax.rem(h, 4), 1), 0:1]

    def norm_rows():
        for cp in ins:
            cp.wait()
        v = TK[...].astype(f32)
        f = lax.rsqrt(jnp.mean(v * v, axis=1, keepdims=True) + epsilon)
        scal[:, 3:4] = f
        NM[...] = (v * f).astype(bf)
        pos = lax.broadcasted_iota(jnp.int32, (512, 1), 0) + y * 512
        keep = (pos < lengths[0]).astype(f32)
        scal[:, 0:1] = keep
        go[...] = (go[...].astype(f32) * keep).astype(bf)
        LT[1] = go[...].T

    def project(j, h):
        cols = slice(h * 512, h * 512 + 512)
        v = dot(NM[...], WV[j])
        if j == 2:
            R[4, :, cols] = v.astype(bf)
            DMX[:, cols] = (v * jax.nn.sigmoid(v)).astype(bf)
        if j == 0:
            R[3, :, cols] = v.astype(bf)
            UN[:, cols] = (v * jax.nn.sigmoid(v)).astype(bf)
        if j == 1:
            R[2, :, cols] = v.astype(bf)
        if j == 3:
            DV[:, cols] = v
            R[1, :, cols] = v.astype(bf)

    def project_own(*js):
        for j in js:
            wload(j, 0).wait()
            project(j, 0)

    def project_part(j):
        wload(j, 1).wait()
        project(j, 1)

    def update(h, _):
        hs = head(h)
        kl = (UN[:, hs].astype(f32) * jnp.exp(-rate_of(h) * (511.0 - tau))).astype(bf)
        GS[lax.rem(h + 4, 8)] = dottn(kl, R[2, :, hs]).astype(bf)
        return 0

    hand = rc(GS, GR, gss, gsr, Y)
    ti = lax.broadcasted_iota(jnp.int32, (512, 512), 0)
    ri = lax.broadcasted_iota(jnp.int32, (512, 512), 1)

    def inner(h, _):
        hs = head(h)
        r = rate_of(h)
        within = jnp.where(ti >= ri, jnp.exp(-r * (tau + 1.0)) * jnp.exp(r * (rho + 1.0)), 0.0)
        ACC[:, hs] = dot((dotnt(DMX[:, hs], UN[:, hs]) * within).astype(bf), R[2, :, hs])
        return 0

    alive = (y == 1).astype(f32)

    def outer(h, _):
        hs = head(h)
        s = (GR[h].astype(f32) * alive).astype(bf)
        state[h] = s
        ACC[:, hs] = ACC[:, hs] + jnp.exp(-rate_of(h) * (tau + 1.0)) * dot(DMX[:, hs], s)
        return 0

    def gating():
        m = ACC[...]
        f = lax.rsqrt(jnp.mean(m * m, axis=1, keepdims=True) + epsilon)
        scal[:, 2:3] = f
        u = m * f
        UN[...] = u.astype(bf)
        R[0] = (u * DV[...]).astype(bf)

    def middle_rows():
        wload(4, 0).wait()
        wload(4, 1).wait()
        m = TK[...].astype(f32) + dot(R[0, :, 0:512], WO[0]) + dot(R[0, :, 512:1024], WO[1])
        f = lax.rsqrt(jnp.mean(m * m, axis=1, keepdims=True) + epsilon)
        scal[:, 1:2] = f
        ACC[...] = m
        mid[...] = (m * f).astype(bf)
        LT[0] = mid[...].T

    def tload(i, s):
        return [pltpu.make_async_copy(W3.at[i, :, :, :, :, h], WT.at[s, :, :, :, :, :, pl.ds(h * 128, 128)], wsem.at[s, h]) for h in (0, 1)]

    def where(i, m):
        if m == 0:
            return i, slice(0, 3), 3, HR
        if m == 2:
            return i - NWG, slice(0, 3), 3, HR
        e = i - NF
        return e // 3, pl.ds(lax.rem(e, 3), 1), 1, 0

    def cps(k, i, m):
        (g, ts, n, hr), s, s1, sq = where(i, m), lax.rem(i, SLOTS), lax.rem(i, SLOT1), lax.rem(i, 4)
        if k == 0:
            return [rc(G.at[g, 1 - c, ts], RD.at[lax.rem(i, 2), 0:n], e_s.at[i], e_r.at[i], C)]
        if k == 1:
            o = [rc(G.at[g, c, ts, :, :, 1 - y, hr:64], R1.at[s1, 0:n, :, :, hr:64], fy_s.at[i, 0], fy_r.at[i, 0], Y)]
            if hr:
                o.append(rc(G.at[g, c, ts, :, 1 - x, :, 0:hr], R1.at[s1, 0:n, :, :, 0:hr], fx_s.at[i, 0], fx_r.at[i, 0], X))
            return o
        if k == 2:
            o = [rc(G.at[g, c, ts, :, 1 - x, y, hr:64], R2.at[s, 0:n, :, hr:64], fx_s.at[i, 1], fx_r.at[i, 1], X)]
            if hr:
                o.append(rc(G.at[g, c, ts, :, x, 1 - y, 0:hr], R2.at[s, 0:n, :, 0:hr], fy_s.at[i, 1], fy_r.at[i, 1], Y))
            return o
        if k == 3:
            return [rc(Q.at[sq, 0:n, q], RZ.at[s, u, 0:n], fz_s.at[i, u], fz_r.at[i, u], dev(q, x, c, y)) for u, q in enumerate(zp)]

    def ags(k, w):
        if k == 0:
            f = FN.at[lax.rem(w, 4)]
            return [rc(f, O.at[w, z, x, c], az_s.at[w, n], az_r.at[w, n], dev(q, x, c, y)) for n, q in enumerate(zp)]
        if k == 1:
            return [rc(O.at[w, :, x, c], O.at[w, :, x, c], ax_s.at[w], ax_r.at[w], X)]
        if k == 2:
            return [rc(O.at[w, :, :, c], O.at[w, :, :, c], ad_s.at[w], ad_r.at[w], C)]

    def flush(w):
        return pltpu.make_async_copy(FN.at[lax.rem(w, 4)], O.at[w, z, x, c], fl.at[w])

    def reduce(k, i, m):
        (g, ts, n, hr), s, s1, sq = where(i, m), lax.rem(i, SLOTS), lax.rem(i, SLOT1), lax.rem(i, 4)
        up = lambda v: v.astype(f32)
        if k == 1:
            G[g, c, ts] = (up(G[g, c, ts]) + up(RD[lax.rem(i, 2), 0:n])).astype(bf)
        if k == 2:
            if hr:
                G[g, c, ts, :, x, :, 0:hr] = (up(G[g, c, ts, :, x, :, 0:hr]) + up(R1[s1, 0:n, :, :, 0:hr])).astype(bf)
            G[g, c, ts, :, :, y, hr:64] = (up(G[g, c, ts, :, :, y, hr:64]) + up(R1[s1, 0:n, :, :, hr:64])).astype(bf)
        if k == 3:
            Q[sq, 0:n] = (up(G[g, c, ts, :, x, y]) + up(R2[s, 0:n])).astype(bf)
        if k == 4:
            v = up(Q[sq, 0:n, z])
            for u in range(3):
                v = v + up(RZ[s, u, 0:n])
            if m == 1:
                FN[lax.rem(i - NF, 4)] = v[0].astype(bf)
            else:
                sh[ts, :, pl.ds(pl.multiple_of(g * 128, 128), 128)] = v

    def arrive(k, i, m):
        if k > 0:
            for cp in cps(k - 1, i, m):
                cp.wait_recv()
        if k == 1:
            for cp in cps(0, i, m):
                cp.wait_send()
        if k == 4:
            for kk in (1, 2, 3):
                for cp in cps(kk, i, m):
                    cp.wait_send()
        reduce(k, i, m)

    def leave(k, i, m):
        for cp in cps(k, i, m):
            cp.start()

    def both(f, k, t):
        i = t - RS_AT[k]

        for m, lo, hi in ((0, 0, NF), (1, NF, NF + NWG), (2, NF + NWG, NALL)):

            @pl.when((i >= lo) & (i < hi))
            def _(m=m):
                f(k, i, m)

    def ag_arrive(k, t):
        w = t - AG_AT[k] - NF

        @pl.when((w >= 0) & (w < NWG))
        def _():
            for cp in ags(k, w):
                cp.wait_recv()
            if k == 0:
                for cp in ags(0, w):
                    cp.wait_send()
                flush(w).wait()

    def ag_leave(k, t):
        w = t - (AG_AT[k - 1] if k else RS_AT[4]) - NF

        @pl.when((w >= 0) & (w < NWG))
        def _():
            for cp in ags(k, w):
                cp.start()
            if k == 0:
                flush(w).start()

    def stages(t):
        ag_arrive(2, t)
        ag_arrive(1, t)
        ag_arrive(0, t)
        ag_leave(2, t)
        both(arrive, 4, t)
        ag_leave(1, t)
        both(arrive, 3, t)
        ag_leave(0, t)
        both(arrive, 2, t)
        both(leave, 3, t)
        both(arrive, 1, t)
        for k in (2, 1, 0):
            both(leave, k, t)

    def store(g, t, r, own):
        r = r.astype(bf).reshape(4, 2, 2, 64, 256)
        for cc in (0, 1):
            G[g, cc, t, :, :, own] = r[:, :, cc, :, 0:128]
            G[g, cc, t, :, :, 1 - own] = r[:, :, cc, :, 128:256]

    def ffn(t):
        s = lax.rem(t, 2)
        for cp in tload(t, s):
            cp.wait()

        @pl.when(t + 1 < NCH)
        def _():
            for cp in tload(t + 1, 1 - s):
                cp.start()

        fv, fg, fo = [WT[s, :, n].reshape(1024, 256) for n in range(3)]
        m, g_ = mid[...], go[...]
        v, g, gh = dot(m, fv), dot(m, fg), dot(g_, fo)
        hid, dv, dg = (v * g).astype(bf), (gh * g).astype(bf), (gh * v).astype(bf)
        ACC[...] += dotnt(hid, fo)
        dtok[...] += dotnt(dv, fv) + dotnt(dg, fg)
        store(t, 0, dot(LT[0], dv), 0)
        store(t, 1, dot(LT[0], dg), 0)
        store(t, 2, dot(LT[1], hid), 0)

    def ffn_tick(t, _):
        stages(t)

        def one(n, _):
            ffn(n)
            return 0

        lax.fori_loop(jnp.maximum(t, 2 * t - 7), jnp.maximum(t + 1, 2 * t - 5), one, 0)
        return 0

    T = 9
    loops = lambda f, a, b: lax.fori_loop(a, b, f, 0)
    W = W_AT[3]
    for t in range(MEET):
        tick(t)
        if t == 0:
            rate.start()
            norm_rows()
        if t == 1:
            project_own(0, 1)
        if t == 2:
            project_own(2, 3)
        if W <= t < W + 5:
            wload(t - W, 1).start()
        if W + 1 <= t < W + 5:
            project_part(t - W - 1)
        if t == W + 2:
            rate.wait()
            loops(update, 0, 8)
            hand.start()
        if t == W + 3:
            loops(inner, 0, 8)
        if t == W + HAND:
            hand.wait()
            loops(outer, 0, 8)
            gating()
            middle_rows()
            for cp in tload(0, 0):
                cp.start()

    def meet_tick(t, _):
        gather_tick(t)
        return ffn_tick(t - MEET, 0)

    lax.fori_loop(MEET, NCH + 4 * SP, meet_tick, 0)
    lax.fori_loop(NCH + 4 * SP - MEET, T, ffn_tick, 0)
    stages(T)
    keep, scale_mid, scale_out, scale_in = [scal[:, n : n + 1] for n in range(4)]
    OUT[...] = (ACC[...] * keep).astype(bf)
    outs[0].start()
    n2 = mid[...].astype(f32)
    dm = dtok[...]
    gm = go[...].astype(f32) + scale_mid * (dm - n2 * jnp.mean(dm * n2, axis=1, keepdims=True))
    dtok[...] = gm
    gml = gm.astype(bf)
    LT[0] = gml.T
    LT[1] = NM[...].T
    for h in (0, 1):
        cols = slice(h * 512, h * 512 + 512)
        ACC[:, cols] = dotnt(gml, WO[h])
    stages(T + 1)
    dgt, un = ACC[...], UN[...].astype(f32)
    du = dgt * R[1].astype(f32)
    R[1] = (dgt * un).astype(bf)
    DMX[...] = (scale_out * (du - un * jnp.mean(du * un, axis=1, keepdims=True))).astype(bf)

    def first(h, _):
        hs = head(h)
        q = silu(R[4, :, hs].astype(f32)).astype(bf)
        gf = (DMX[:, hs].astype(f32) * jnp.exp(-rate_of(h) * (tau + 1.0))).astype(bf)
        GS2[lax.rem(h + 4, 8)] = dottn(q, gf).astype(bf)
        return 0

    lax.fori_loop(0, 8, first, 0)
    later = rc(GS2, GR2, g2s, g2r, Y)
    later.start()
    def pair(h, _):
        hs = head(h)
        qp, kp = R[4, :, hs].astype(f32), R[3, :, hs].astype(f32)
        q, k, v, dmx = silu(qp).astype(bf), silu(kp).astype(bf), R[2, :, hs], DMX[:, hs]
        cf, rf = jnp.exp(-rate_of(h) * (tau + 1.0)), jnp.exp(rate_of(h) * (rho + 1.0))
        within = jnp.where(ti >= ri, cf * rf, 0.0)
        wt = (dotnt(q, k) * within).astype(bf)
        dsc = (dotnt(dmx, v) * within).astype(bf)
        gf = (dmx.astype(f32) * cf).astype(bf)
        dq = dot(dsc, k) + dotnt(gf, state[h])
        ACC[:, hs] = dottn(dsc, q)
        DV[:, hs] = dottn(wt, dmx)
        sq = jax.nn.sigmoid(qp)
        R[4, :, hs] = (dq * (sq * (1.0 + qp * (1.0 - sq)))).astype(bf)
        return 0

    live = (y == 0).astype(f32)

    def finish(h, _):
        hs = head(h)
        gin = (GR2[h].astype(f32) * live).astype(bf)
        kp = R[3, :, hs].astype(f32)
        sk = jax.nn.sigmoid(kp)
        k = (kp * sk).astype(bf)
        lf = jnp.exp(-rate_of(h) * (511.0 - tau))
        kl = (k.astype(f32) * lf).astype(bf)
        dk = ACC[:, hs] + lf * dotnt(R[2, :, hs], gin)
        R[2, :, hs] = (DV[:, hs] + dot(kl, gin)).astype(bf)
        R[3, :, hs] = (dk * (sk * (1.0 + kp * (1.0 - sk)))).astype(bf)
        return 0

    def wgrad(p):
        j, cp = p // 4, lax.rem(p, 4)
        lo = pl.multiple_of(cp * 128, 128)
        rr = jnp.concatenate([R[j, :, pl.ds(lo, 128)], R[j, :, pl.ds(lo + 512, 128)]], axis=1)
        store(p // 3, lax.rem(p, 3), dot(LT[jnp.minimum(j, 1)], rr), y)

    def wg_tick(t, _):
        stages(t)
        p = t - NF
        wgrad(p)

        @pl.when(p < 8)
        def _():
            pair(p, 0)

        @pl.when(p == 7)
        def _():
            later.wait()
            lax.fori_loop(0, 8, finish, 0)

        for n in range(8):
            @pl.when(p == n + 8)
            def _():
                wbload(n).wait()

        @pl.when((p >= 8) & (p < 16))
        def _():
            n = p - 8
            j, h = 1 + n // 2, lax.rem(n, 2)
            part = dotnt(R[j, :, pl.ds(pl.multiple_of(h * 512, 128), 512)], WV[h])
            ACC[...] = jnp.where(n == 0, 0.0, ACC[...]) + part

        for n in range(6):
            @pl.when(p == n + 8)
            def _():
                wbload(n + 2).start()

        @pl.when(p == 16)
        def _():
            n1 = NM[...].astype(f32)
            dn = ACC[...]
            dtok[...] = dtok[...] + scale_in * (dn - n1 * jnp.mean(dn * n1, axis=1, keepdims=True))
            outs[1].start()

        return 0

    mats = (wg, pg, wv, pv, wk, pk, wq, pq)

    def wbload(n):
        return pltpu.make_async_copy(mats[n], WV.at[n % 2], bsem.at[n % 2])

    wbload(0).start()
    wbload(1).start()
    lax.fori_loop(NF, NF + NWG, wg_tick, 0)
    def tail(t, _):
        stages(t)
        return 0

    lax.fori_loop(NF + NWG, NF + NWG + AG_AT[2], tail, 0)

    def drain(w, _):
        for k in (1, 2):
            for cp in ags(k, w):
                cp.wait_send()
        return 0

    lax.fori_loop(0, NWG, drain, 0)

    outs[2].start()

    def drain_gather(i, _):
        for k in range(4):
            for cp in st(k, i):
                cp.wait_send()
        return 0

    lax.fori_loop(0, NCH, drain_gather, 0)
    for k in (0, 1):
        for cp in near(k):
            cp.wait_send()
    for j in range(5):
        for k in range(3):
            for cp in wst(k, j):
                cp.wait_send()
    for cp in outs:
        cp.wait()


def layer_call(*ins):
    D, V, S = pltpu.SemaphoreType.DMA, pltpu.VMEM, jax.ShapeDtypeStruct
    A, VM = pl.BlockSpec(memory_space=pl.ANY), pl.BlockSpec(memory_space=pltpu.VMEM)
    act, w = (512, 1024), (1024, 512)
    outs = [S(act, bf), S(act, f32), S((3, 64, 1408), f32), S((NWG, 4, 2, 2, 64, 128), bf), S((NCH, 4, 3, 2, 2, 2, 64, 128), bf)] + [S(w, bf)] * 4 + [S(act, bf)]
    scratch = [V((NCH, 3, 64, 128), bf), V((4,) + w, bf), V((2,) + act, bf),
               V((NCH, 2, 3, 4, 2, 2, 64, 128), bf), V((2, 3, 4, 2, 2, 64, 128), bf), V((SLOT1, 3, 4, 2, 64, 128), bf), V((SLOTS, 3, 4, 64, 128), bf),
               V((4, 3, 4, 64, 128), bf), V((SLOTS, 3, 3, 64, 128), bf), V((4, 64, 128), bf), V((2, 4, 3, 2, 2, 64, 256), bf),
               V((2,) + w, bf), V(act, f32), V(act, f32), V((5,) + act, bf), V(act, bf), V(act, bf), V(act, bf), V(act, bf), V(act, bf),
               V((512, 4), f32), V((2, 8, 128), f32)] + [V((8, 128, 128), bf)] * 5 + [V(act, bf), V(act, bf), V(act, f32), V((3, 64, 1408), f32)]
    n, m, a = (NCH,), (NALL,), (NWG,)
    scratch += [D(s) for s in ((NCH, 3), (NCH, 3), (NCH, 2, 3), (NCH, 2, 3), (NCH, 2, 3), (NCH, 2, 3), (2,), (2,), (2,), (2,), n, n,
                               (5,), (5,), (5,), (5,), (5, 2), (5, 2), (), (), (), (), (), (10,),
                               (2, 2), (2,), (), (), m, m, (NALL, 2), (NALL, 2), (NALL, 2), (NALL, 2), (NALL, 3), (NALL, 3),
                               (NWG, 3), (NWG, 3), a, a, a, a, a, (5,))]
    return pl.pallas_call(
        layer_kernel,
        out_shape=outs,
        in_specs=[A, A] + [pl.BlockSpec(memory_space=pltpu.SMEM)] * 2 + [VM] * 3 + [A] * 5,
        out_specs=[A] * 10,
        scratch_shapes=scratch,
        compiler_params=pltpu.CompilerParams(collective_id=1, has_side_effects=True, vmem_limit_bytes=67043328),
    )(*ins)
def finish_kernel(o, sh, out, dtok, output, d_tokens, d_query, d_key, d_value, d_gate, d_out, d_f_value, d_f_gate, d_f_out):
    output[...] = out[...]
    d_tokens[...] = dtok[...]
    for n in range(4):
        cols = slice(n * 128, n * 128 + 128)
        d_out[cols, :] = o[n].astype(f32).T
        d_gate[:, cols] = o[4 + n].astype(f32)
        d_value[:, cols] = o[8 + n].astype(f32)
        d_key[:, cols] = o[12 + n].astype(f32)
        d_query[:, cols] = o[16 + n].astype(f32)

    @pl.when(pl.program_id(0) == 0)
    def _():
        d_f_value[...] = sh[0]
        d_f_gate[...] = sh[1]
        d_f_out[...] = sh[2]


def finish_call(o, sh, out, dtok):
    S = jax.ShapeDtypeStruct
    whole = lambda *s: pl.BlockSpec(s, lambda i: (0,) * len(s))
    return pl.pallas_call(
        finish_kernel,
        grid=(4,),
        out_shape=[S((512, 1024), bf), S((512, 1024), f32)] + [S((1024, 512), f32)] * 4 + [S((512, 1024), f32)] + [S((64, 1408), f32)] * 3,
        in_specs=[pl.BlockSpec((20, 256, 128), lambda i: (0, i, 0)), whole(3, 64, 1408)] + [pl.BlockSpec((128, 1024), lambda i: (i, 0))] * 2,
        out_specs=[pl.BlockSpec((128, 1024), lambda i: (i, 0))] * 2 + [pl.BlockSpec((256, 512), lambda i: (i, 0))] * 4 + [pl.BlockSpec((512, 256), lambda i: (0, i))] + [whole(64, 1408)] * 3,
        compiler_params=pltpu.CompilerParams(vmem_limit_bytes=67043328),
    )(o, sh, out, dtok)

def fast_body(tokens, lengths, decay, w_query, w_key, w_value, w_gate, w_out, f_value, f_gate, f_out, cotangent):
    weights = (w_query, w_key, w_value, w_gate, w_out)
    output, d_tokens, shares, grads, *_ = layer_call(tokens, cotangent, lengths, decay, f_value, f_gate, f_out.T, *weights)
    *results, d_f_out = finish_call(grads.reshape(NWG, 1024, 128), shares, output, d_tokens)
    return (*results, d_f_out.T)


def solution(mesh):
    placed = (
        P(("dp", "head"), None),
        P("dp"),
        P("head"),
        P(None, "head"),
        P(None, "head"),
        P(None, "head"),
        P(None, "head"),
        P("head", None),
        P("dp", "head"),
        P("dp", "head"),
        P("head", "dp"),
        P(("dp", "head"), None),
    )
    fast = mesh.shape["dp"] == 16 and mesh.shape["head"] == 2
    return jax.shard_map(
        fast_body if fast else general_body,
        mesh=mesh,
        in_specs=placed,
        out_specs=(
            P(("dp", "head"), None),
            P(("dp", "head"), None),
            P(None, "head"),
            P(None, "head"),
            P(None, "head"),
            P(None, "head"),
            P("head", None),
            P("dp", "head"),
            P("dp", "head"),
            P("head", "dp"),
        ),
        check_vma=False,
    )
```

```python
import jax
import jax.numpy as jnp
from jax import lax
from jax.experimental import pallas as pl
from jax.experimental.pallas import tpu as pltpu
from jax.sharding import PartitionSpec as P

D = 1024
HD = 128
SEQ_DEV = 1
SLOT = 1024
BLOCK = 512


epsilon = 1e-06


def normalize(values):
    factor = lax.rsqrt(jnp.mean(values * values, axis=-1, keepdims=True) + epsilon)
    return (values * factor, factor)


def norm_back(grad_normed, normed, factor):
    inner_sum = jnp.mean(grad_normed * normed, axis=-1, keepdims=True)
    return factor * (grad_normed - normed * inner_sum)


def silu_slope(values):
    sigmoid = jax.nn.sigmoid(values)
    return sigmoid * (1.0 + values * (1.0 - sigmoid))


def matmul(left_side, right_side):
    return jnp.dot(left_side, right_side, preferred_element_type=jnp.float32)


def matmul_right_t(left_side, right_side):
    return lax.dot_general(
        left_side, right_side, (((1,), (1,)), ((), ())), preferred_element_type=jnp.float32
    )


def matmul_left_t(left_side, right_side):
    return lax.dot_general(
        left_side, right_side, (((0,), (0,)), ((), ())), preferred_element_type=jnp.float32
    )


def exact(form, left_side, right_side):
    return jnp.einsum(form, left_side, right_side, precision=lax.Precision.HIGHEST)


def decay_tables(rates):
    offsets = jnp.arange(BLOCK).astype(jnp.float32)
    spread = offsets[:, None] - offsets[None, :]
    causal = spread >= 0
    within = jnp.where(
        causal[None], jnp.exp(-rates[:, None, None] * jnp.where(causal, spread, 0.0)[None]), 0.0
    )
    first_decay = jnp.exp(-rates[:, None] * (offsets[None, :] + 1.0))
    last_decay = jnp.exp(-rates[:, None] * (BLOCK - 1.0 - offsets[None, :]))
    block_decay = jnp.exp(-rates * BLOCK)
    return (within, first_decay, last_decay, block_decay)


def to_blocks(values, heads):
    shaped = values.reshape(SEQ_DEV, SLOT // BLOCK, BLOCK, heads, HD)
    return shaped.transpose(1, 0, 3, 2, 4)


def from_blocks(blocks):
    return blocks.transpose(1, 0, 3, 2, 4).reshape(-1, blocks.shape[2] * blocks.shape[4])


def lightning_forward(query, keys, values, tables):
    within, first_decay, last_decay, block_decay = tables

    def advance(carried, inputs):
        query_blk, keys_blk, values_blk = inputs
        scores = jnp.einsum(
            "shbd,shcd->shbc", query_blk, keys_blk, preferred_element_type=jnp.float32
        )
        weights = (scores * within[None]).astype(jnp.bfloat16)
        inner_sum = jnp.einsum(
            "shbc,shcd->shbd", weights, values_blk, preferred_element_type=jnp.float32
        )
        outer_sum = first_decay[None, :, :, None] * exact(
            "shbd,shde->shbe", query_blk.astype(jnp.float32), carried
        )
        keys_scaled = keys_blk.astype(jnp.float32) * last_decay[None, :, :, None]
        update = exact("shbd,shbe->shde", keys_scaled, values_blk.astype(jnp.float32))
        return (
            block_decay[None, :, None, None] * carried + update,
            (inner_sum + outer_sum, carried),
        )

    initial = jnp.zeros((SEQ_DEV, query.shape[2], HD, HD), jnp.float32)
    final_state, (mixed, states) = lax.scan(advance, initial, (query, keys, values))
    return (mixed, states)


def lightning_backward(query, keys, values, grads, states, tables):
    within, first_decay, last_decay, block_decay = tables

    def retreat(later_grad, inputs):
        query_blk, keys_blk, values_blk, grad_blk, carried = inputs
        scores = jnp.einsum(
            "shbd,shcd->shbc", query_blk, keys_blk, preferred_element_type=jnp.float32
        )
        weights = (scores * within[None]).astype(jnp.bfloat16)
        d_weights = jnp.einsum(
            "shbd,shcd->shbc", grad_blk, values_blk, preferred_element_type=jnp.float32
        )
        d_scores = (d_weights * within[None]).astype(jnp.bfloat16)
        d_query = jnp.einsum(
            "shbc,shcd->shbd", d_scores, keys_blk, preferred_element_type=jnp.float32
        )
        d_keys = jnp.einsum(
            "shbc,shbd->shcd", d_scores, query_blk, preferred_element_type=jnp.float32
        )
        d_values = jnp.einsum(
            "shbc,shbd->shcd", weights, grad_blk, preferred_element_type=jnp.float32
        )
        grad_scaled = grad_blk.astype(jnp.float32) * first_decay[None, :, :, None]
        keys_scaled = keys_blk.astype(jnp.float32) * last_decay[None, :, :, None]
        d_query = d_query + exact("shbe,shde->shbd", grad_scaled, carried)
        d_keys = d_keys + last_decay[None, :, :, None] * exact(
            "shbe,shde->shbd", values_blk.astype(jnp.float32), later_grad
        )
        d_values = d_values + exact("shbd,shde->shbe", keys_scaled, later_grad)
        earlier = block_decay[None, :, None, None] * later_grad + exact(
            "shbd,shbe->shde", query_blk.astype(jnp.float32), grad_scaled
        )
        return (earlier, (d_query, d_keys, d_values))

    initial = jnp.zeros((SEQ_DEV, query.shape[2], HD, HD), jnp.float32)
    first_grad, results = lax.scan(
        retreat, initial, (query, keys, values, grads, states), reverse=True
    )
    return results


def general_body(
    tokens,
    lengths,
    decay,
    w_query,
    w_key,
    w_value,
    w_gate,
    w_out,
    f_value,
    f_gate,
    f_out,
    cotangent,
):
    own_rows = tokens.shape[0]
    first_row = lax.axis_index("head") * own_rows
    heads_here = decay.shape[0]
    tables = decay_tables(decay)
    positions = first_row + jnp.arange(own_rows, dtype=jnp.int32)
    slot_match = (positions // SLOT)[:, None] == jnp.arange(SEQ_DEV, dtype=jnp.int32)[None, :]
    length_of = jnp.sum(jnp.where(slot_match, lengths[None, :], 0), axis=1)
    keep_rows = (positions % SLOT < length_of).astype(jnp.float32)[:, None]
    inputs_f = tokens.astype(jnp.float32)
    normed, scale_in = normalize(inputs_f)
    gathered = lax.all_gather(normed.astype(jnp.bfloat16), "head", axis=0, tiled=True)
    query_pre = matmul(gathered, w_query)
    keys_pre = matmul(gathered, w_key)
    values_pre = matmul(gathered, w_value)
    gate_pre = matmul(gathered, w_gate)
    query_blocks = to_blocks(jax.nn.silu(query_pre).astype(jnp.bfloat16), heads_here)
    keys_blocks = to_blocks(jax.nn.silu(keys_pre).astype(jnp.bfloat16), heads_here)
    values_blocks = to_blocks(values_pre.astype(jnp.bfloat16), heads_here)
    mixed_blocks, states = lightning_forward(query_blocks, keys_blocks, values_blocks, tables)
    mixed = from_blocks(mixed_blocks)
    squares = lax.psum(jnp.sum(mixed * mixed, axis=1), "head")
    scale_out = lax.rsqrt(squares / D + epsilon)[:, None]
    mixed_unit = mixed * scale_out
    gated = (mixed_unit * gate_pre).astype(jnp.bfloat16)
    branch = lax.psum_scatter(
        matmul(gated, w_out).astype(jnp.bfloat16), "head", scatter_dimension=0, tiled=True
    ).astype(jnp.float32)
    middle = inputs_f + branch
    mid_normed, scale_mid = normalize(middle)
    mid_all = lax.all_gather(mid_normed.astype(jnp.bfloat16), "head", axis=0, tiled=True)
    value_full, gate_full = (
        lax.all_gather(f_value, "dp", axis=0, tiled=True),
        lax.all_gather(f_gate, "dp", axis=0, tiled=True),
    )
    down_full = lax.all_gather(f_out, "dp", axis=1, tiled=True)
    value_ffn = matmul(mid_all, value_full)
    gate_ffn = matmul(mid_all, gate_full)
    hidden = (value_ffn * gate_ffn).astype(jnp.bfloat16)
    ffn_branch = lax.psum_scatter(
        matmul(hidden, down_full).astype(jnp.bfloat16), "head", scatter_dimension=0, tiled=True
    ).astype(jnp.float32)
    output = ((middle + ffn_branch) * keep_rows).astype(jnp.bfloat16)
    grad_out = cotangent.astype(jnp.float32) * keep_rows
    grad_all = lax.all_gather(grad_out.astype(jnp.bfloat16), "head", axis=0, tiled=True)
    grad_hidden = matmul_right_t(grad_all, down_full)
    d_value_ffn = (grad_hidden * gate_ffn).astype(jnp.bfloat16)
    d_gate_ffn = (grad_hidden * value_ffn).astype(jnp.bfloat16)
    d_mid_normed = lax.psum_scatter(
        (matmul_right_t(d_value_ffn, value_full) + matmul_right_t(d_gate_ffn, gate_full)).astype(
            jnp.bfloat16
        ),
        "head",
        scatter_dimension=0,
        tiled=True,
    ).astype(jnp.float32)
    grad_middle = grad_out + norm_back(d_mid_normed, mid_normed, scale_mid)
    joined = jnp.concatenate([d_value_ffn, d_gate_ffn], axis=1)
    hidden_here = hidden.shape[1]
    shares = lax.psum_scatter(
        jnp.concatenate(
            [matmul_left_t(mid_all, joined), matmul_left_t(grad_all, hidden)], axis=1
        ).astype(jnp.bfloat16),
        "dp",
        scatter_dimension=0,
        tiled=True,
    ).astype(jnp.float32)
    d_f_value = shares[:, :hidden_here]
    d_f_gate = shares[:, hidden_here : 2 * hidden_here]
    d_f_out = shares[:, 2 * hidden_here :].T
    grad_rows = lax.all_gather(grad_middle.astype(jnp.bfloat16), "head", axis=0, tiled=True)
    d_gated = matmul_right_t(grad_rows, w_out)
    d_w_out_local = matmul_left_t(gated, grad_rows)
    d_gate_pre = (d_gated * mixed_unit).astype(jnp.bfloat16)
    d_unit = d_gated * gate_pre
    inner_out = lax.psum(jnp.sum(d_unit * mixed_unit, axis=1), "head")
    d_mixed = (scale_out * (d_unit - mixed_unit * (inner_out / D)[:, None])).astype(jnp.bfloat16)
    d_query, d_keys, d_values = lightning_backward(
        query_blocks, keys_blocks, values_blocks, to_blocks(d_mixed, heads_here), states, tables
    )
    d_query_pre = (from_blocks(d_query) * silu_slope(query_pre)).astype(jnp.bfloat16)
    d_keys_pre = (from_blocks(d_keys) * silu_slope(keys_pre)).astype(jnp.bfloat16)
    d_values_pre = from_blocks(d_values).astype(jnp.bfloat16)
    total = matmul_right_t(d_query_pre, w_query) + matmul_right_t(d_keys_pre, w_key)
    d_normed = lax.psum_scatter(
        (total + matmul_right_t(d_values_pre, w_value) + matmul_right_t(d_gate_pre, w_gate)).astype(
            jnp.bfloat16
        ),
        "head",
        scatter_dimension=0,
        tiled=True,
    ).astype(jnp.float32)
    d_tokens = grad_middle + norm_back(d_normed, normed, scale_in)
    grads_attention = (
        lax.psum(matmul_left_t(gathered, d_query_pre).astype(jnp.bfloat16), "dp").astype(
            jnp.float32
        ),
        lax.psum(matmul_left_t(gathered, d_keys_pre).astype(jnp.bfloat16), "dp").astype(
            jnp.float32
        ),
        lax.psum(matmul_left_t(gathered, d_values_pre).astype(jnp.bfloat16), "dp").astype(
            jnp.float32
        ),
        lax.psum(matmul_left_t(gathered, d_gate_pre).astype(jnp.bfloat16), "dp").astype(
            jnp.float32
        ),
        lax.psum(d_w_out_local.astype(jnp.bfloat16), "dp").astype(jnp.float32),
    )
    return (
        output,
        d_tokens,
        grads_attention[0],
        grads_attention[1],
        grads_attention[2],
        grads_attention[3],
        grads_attention[4],
        d_f_value,
        d_f_gate,
        d_f_out,
    )


MESH = pl.DeviceIdType.MESH
NCH = 11
RA = 16
HR = 32
SP = 2
NEAR = 2
MEET = 10
W_AT = (0, 2, 4, 5)
HAND = 4
RN = 16
SLOTS = 4
SLOT1 = 6
NF = NCH
NWG = 20
NALL = NCH + NWG

RS_AT = (1, 2, 5, 7, 9)
AG_AT = (11, 13, 15)
TN = (((0,), (0,)), ((), ()))
bf = jnp.bfloat16
f32 = jnp.float32
NT = (((1,), (1,)), ((), ()))


def dot(a, b):
    return jnp.dot(a, b, preferred_element_type=f32)


def dotnt(a, b):
    return lax.dot_general(a, b, NT, preferred_element_type=f32)


def dottn(a, b):
    return lax.dot_general(a, b, TN, preferred_element_type=f32)


def place():
    d=lax.axis_index("dp")
    return d//4, (d//2)%2, d%2, lax.axis_index("head")
def dev(z,x,c,y): return ((z*2+x)*2+c, y)
def layer_kernel(tokens, cot, lengths, dec, fv, fg, fo, wq, wk, wv, wg, wo,
                 output, d_tokens, shares, O, W3, pq, pk, pv, pg, po,
                 S, WV, WO, G, RD, R1, R2, Q, RZ, FN, WT, LT, ACC, DV, R, UN, NM, DMX, mid, go, scal, rates, state, GS, GR, GS2, GR2, TK, OUT, dtok, sh,
                 zs, zr, xs, xr, ys, yr, nxs, nxr, nys, nyr, ds, dr, wys, wyr, wxs, wxr, wds, wdr, gss, gsr, rss, rsr, ls, ws,
                 wsem, bsem, g2s, g2r, e_s, e_r, fx_s, fx_r, fy_s, fy_r, fz_s, fz_r, az_s, az_r, ax_s, ax_r, ad_s, ad_r, fl, io):
    z, x, c, y = place()
    zp = [lax.rem(z + r, 4) for r in (1, 2, 3)]
    X, Y, C = dev(z, 1 - x, c, y), dev(z, x, c, 1 - y), dev(z, x, 1 - c, y)
    zb = lax.rem(z, 2)
    ZP = dev(z + 1 - 2 * zb, x, c, y)
    bar = pltpu.get_barrier_semaphore()
    peers = [dev(q, x, c, y) for q in zp] + [X, Y, C]
    for p in peers:
        pl.semaphore_signal(bar, inc=1, device_id=p, device_id_type=MESH)
    ins = [pltpu.make_async_copy(tokens, TK, io.at[0]), pltpu.make_async_copy(cot, go, io.at[1])]
    for cp in ins:
        cp.start()
    outs = [pltpu.make_async_copy(a, b, io.at[2 + n]) for n, (a, b) in enumerate(((OUT, output), (dtok, d_tokens), (sh, shares)))]
    own, par = (wk, wv, wq, wg, wo), (pk, pv, pq, pg, po)

    def rc(src, dst, ss, rs, d):
        return pltpu.make_async_remote_copy(src_ref=src, dst_ref=dst, send_sem=ss, recv_sem=rs, device_id=d, device_id_type=MESH)

    def wload(j, h):
        src = (own if h == 0 else par)[j]
        dst = WV.at[j] if j < 4 else WO.at[h]
        return pltpu.make_async_copy(src, dst, ws.at[2 * j + h])

    for j in range(5):
        wload(j, 0).start()
    for i in range(NCH):
        S[i, 0] = fv[:, i * 128 : i * 128 + 128]
        S[i, 1] = fg[:, i * 128 : i * 128 + 128]
        S[i, 2] = fo[:, i * 128 : i * 128 + 128]
    for h in range(4):
        rates[0, h : h + 1, :] = jnp.full((1, 128), dec[h], f32)
    dtok[...] = jnp.zeros_like(dtok)
    pl.semaphore_wait(bar, len(peers))
    mine = pltpu.make_async_copy(S, W3.at[:, z, :, x, c, y], ls)
    mine.start()
    rate = rc(rates.at[0], rates.at[1], rss, rsr, Y)

    far = [lax.rem(z + r, 4) for r in (3, 2, 1)]

    def st(k, i):
        if k == 0:
            return [rc(S.at[i], W3.at[i, z, :, x, c, y], zs.at[i, n], zr.at[i, n], dev(q, x, c, y)) for n, q in enumerate(zp)]
        if k == 1:
            o = []
            for n, q in enumerate(far):
                a, b = W3.at[i, q, :, x, c, y, 0:RA], W3.at[i, q, :, x, c, y, RA:64]
                o += [rc(a, a, xs.at[i, 0, n], xr.at[i, 0, n], X), rc(b, b, ys.at[i, 0, n], yr.at[i, 0, n], Y)]
            return o
        if k == 2:
            o = []
            for n, q in enumerate(far):
                a, b = W3.at[i, q, :, :, c, y, 0:RA], W3.at[i, q, :, x, c, :, RA:64]
                o += [rc(b, b, xs.at[i, 1, n], xr.at[i, 1, n], X), rc(a, a, ys.at[i, 1, n], yr.at[i, 1, n], Y)]
            return o
        a = W3.at[i, :, :, :, c]
        return [rc(a, a, ds.at[i], dr.at[i], C)]

    def near(k):
        if k == 0:
            return [rc(S.at[:, :, 0:RN], W3.at[:, z, :, x, c, y, 0:RN], nxs.at[0], nxr.at[0], X),
                    rc(S.at[:, :, RN:64], W3.at[:, z, :, x, c, y, RN:64], nys.at[0], nyr.at[0], Y)]
        a, b = W3.at[:, z, :, :, c, y, 0:RN], W3.at[:, z, :, x, c, :, RN:64]
        return [rc(b, b, nxs.at[1], nxr.at[1], X), rc(a, a, nys.at[1], nyr.at[1], Y)]

    def quarter(r):
        n = r.shape[0] // 4
        return lambda a, b: r.at[pl.ds(pl.multiple_of((2 * a + b) * n, 128), n)]

    def wst(k, j):
        if k == 0:
            return [rc(quarter(own[j])(zb, c), quarter(par[j])(zb, c), wys.at[j], wyr.at[j], Y)]
        if k == 1:
            a = quarter(par[j])(zb, c)
            return [rc(a, a, wxs.at[j], wxr.at[j], ZP)]
        return [rc(quarter(par[j])(b, c), quarter(par[j])(b, c), wds.at[j, b], wdr.at[j, b], C) for b in (0, 1)]

    def near_step(k):
        if k == 1:
            mine.wait()
        if k > 0:
            for cp in near(k - 1):
                cp.wait_recv()
        if k < 2:
            for cp in near(k):
                cp.start()

    def weight_step(k, j):
        if k > 0:
            for cp in wst(k - 1, j):
                cp.wait_recv()
        if k < 3:
            for cp in wst(k, j):
                cp.start()

    def gather_step(k, i):
        came = st(k - 1, i) if k > 0 else []
        new = st(k, i) if k < 4 else []
        parts = 3 if k in (1, 2) else 1
        for m in range(parts):
            for cp in came[m * len(came) // parts : (m + 1) * len(came) // parts]:
                cp.wait_recv()
            for cp in new[m * len(new) // parts : (m + 1) * len(new) // parts]:
                cp.start()

    def gather_tick(t):
        for k in (4, 3, 2, 1, 0):
            i = t - k * SP

            @pl.when((i >= 0) & (i < NCH))
            def _():
                gather_step(k, i)

    def tick(t):
        if t == 0:
            near_step(0)
        if t == NEAR:
            near_step(1)
        for k in (3, 2, 1, 0):
            if 0 <= t - W_AT[k] < 5:
                weight_step(k, t - W_AT[k])
        if t == 3 * SP:
            near_step(2)
        gather_tick(t)

    def silu(v):
        return v * jax.nn.sigmoid(v)

    def head(h):
        return pl.ds(pl.multiple_of(h * 128, 128), 128)

    tau = lax.broadcasted_iota(jnp.int32, (512, 1), 0).astype(f32)
    rho = lax.broadcasted_iota(jnp.int32, (1, 512), 1).astype(f32)

    def rate_of(h):
        return rates[h // 4, pl.ds(lax.rem(h, 4), 1), 0:1]

    def norm_rows():
        for cp in ins:
            cp.wait()
        v = TK[...].astype(f32)
        f = lax.rsqrt(jnp.mean(v * v, axis=1, keepdims=True) + epsilon)
        scal[:, 3:4] = f
        NM[...] = (v * f).astype(bf)
        pos = lax.broadcasted_iota(jnp.int32, (512, 1), 0) + y * 512
        keep = (pos < lengths[0]).astype(f32)
        scal[:, 0:1] = keep
        go[...] = (go[...].astype(f32) * keep).astype(bf)
        LT[1] = go[...].T

    def project(j, h):
        cols = slice(h * 512, h * 512 + 512)
        v = dot(NM[...], WV[j])
        if j == 2:
            R[4, :, cols] = v.astype(bf)
            DMX[:, cols] = (v * jax.nn.sigmoid(v)).astype(bf)
        if j == 0:
            R[3, :, cols] = v.astype(bf)
            UN[:, cols] = (v * jax.nn.sigmoid(v)).astype(bf)
        if j == 1:
            R[2, :, cols] = v.astype(bf)
        if j == 3:
            DV[:, cols] = v
            R[1, :, cols] = v.astype(bf)

    def project_own(*js):
        for j in js:
            wload(j, 0).wait()
            project(j, 0)

    def project_part(j):
        wload(j, 1).wait()
        project(j, 1)

    def update(h, _):
        hs = head(h)
        kl = (UN[:, hs].astype(f32) * jnp.exp(-rate_of(h) * (511.0 - tau))).astype(bf)
        GS[lax.rem(h + 4, 8)] = dottn(kl, R[2, :, hs]).astype(bf)
        return 0

    hand = rc(GS, GR, gss, gsr, Y)
    ti = lax.broadcasted_iota(jnp.int32, (512, 512), 0)
    ri = lax.broadcasted_iota(jnp.int32, (512, 512), 1)

    def inner(h, _):
        hs = head(h)
        r = rate_of(h)
        within = jnp.where(ti >= ri, jnp.exp(-r * (tau + 1.0)) * jnp.exp(r * (rho + 1.0)), 0.0)
        ACC[:, hs] = dot((dotnt(DMX[:, hs], UN[:, hs]) * within).astype(bf), R[2, :, hs])
        return 0

    alive = (y == 1).astype(f32)

    def outer(h, _):
        hs = head(h)
        s = (GR[h].astype(f32) * alive).astype(bf)
        state[h] = s
        ACC[:, hs] = ACC[:, hs] + jnp.exp(-rate_of(h) * (tau + 1.0)) * dot(DMX[:, hs], s)
        return 0

    def gating():
        m = ACC[...]
        f = lax.rsqrt(jnp.mean(m * m, axis=1, keepdims=True) + epsilon)
        scal[:, 2:3] = f
        u = m * f
        UN[...] = u.astype(bf)
        R[0] = (u * DV[...]).astype(bf)

    def middle_rows():
        wload(4, 0).wait()
        wload(4, 1).wait()
        m = TK[...].astype(f32) + dot(R[0, :, 0:512], WO[0]) + dot(R[0, :, 512:1024], WO[1])
        f = lax.rsqrt(jnp.mean(m * m, axis=1, keepdims=True) + epsilon)
        scal[:, 1:2] = f
        ACC[...] = m
        mid[...] = (m * f).astype(bf)
        LT[0] = mid[...].T

    def tload(i, s):
        return [pltpu.make_async_copy(W3.at[i, :, :, :, :, h], WT.at[s, :, :, :, :, :, pl.ds(h * 128, 128)], wsem.at[s, h]) for h in (0, 1)]

    def where(i, m):
        if m == 0:
            return i, slice(0, 3), 3, HR
        if m == 2:
            return i - NWG, slice(0, 3), 3, HR
        e = i - NF
        return e // 3, pl.ds(lax.rem(e, 3), 1), 1, 0

    def cps(k, i, m):
        (g, ts, n, hr), s, s1, sq = where(i, m), lax.rem(i, SLOTS), lax.rem(i, SLOT1), lax.rem(i, 4)
        if k == 0:
            return [rc(G.at[g, 1 - c, ts], RD.at[lax.rem(i, 2), 0:n], e_s.at[i], e_r.at[i], C)]
        if k == 1:
            o = [rc(G.at[g, c, ts, :, :, 1 - y, hr:64], R1.at[s1, 0:n, :, :, hr:64], fy_s.at[i, 0], fy_r.at[i, 0], Y)]
            if hr:
                o.append(rc(G.at[g, c, ts, :, 1 - x, :, 0:hr], R1.at[s1, 0:n, :, :, 0:hr], fx_s.at[i, 0], fx_r.at[i, 0], X))
            return o
        if k == 2:
            o = [rc(G.at[g, c, ts, :, 1 - x, y, hr:64], R2.at[s, 0:n, :, hr:64], fx_s.at[i, 1], fx_r.at[i, 1], X)]
            if hr:
                o.append(rc(G.at[g, c, ts, :, x, 1 - y, 0:hr], R2.at[s, 0:n, :, 0:hr], fy_s.at[i, 1], fy_r.at[i, 1], Y))
            return o
        if k == 3:
            return [rc(Q.at[sq, 0:n, q], RZ.at[s, u, 0:n], fz_s.at[i, u], fz_r.at[i, u], dev(q, x, c, y)) for u, q in enumerate(zp)]

    def ags(k, w):
        if k == 0:
            f = FN.at[lax.rem(w, 4)]
            return [rc(f, O.at[w, z, x, c], az_s.at[w, n], az_r.at[w, n], dev(q, x, c, y)) for n, q in enumerate(zp)]
        if k == 1:
            return [rc(O.at[w, :, x, c], O.at[w, :, x, c], ax_s.at[w], ax_r.at[w], X)]
        if k == 2:
            return [rc(O.at[w, :, :, c], O.at[w, :, :, c], ad_s.at[w], ad_r.at[w], C)]

    def flush(w):
        return pltpu.make_async_copy(FN.at[lax.rem(w, 4)], O.at[w, z, x, c], fl.at[w])

    def reduce(k, i, m):
        (g, ts, n, hr), s, s1, sq = where(i, m), lax.rem(i, SLOTS), lax.rem(i, SLOT1), lax.rem(i, 4)
        up = lambda v: v.astype(f32)
        if k == 1:
            G[g, c, ts] = (up(G[g, c, ts]) + up(RD[lax.rem(i, 2), 0:n])).astype(bf)
        if k == 2:
            if hr:
                G[g, c, ts, :, x, :, 0:hr] = (up(G[g, c, ts, :, x, :, 0:hr]) + up(R1[s1, 0:n, :, :, 0:hr])).astype(bf)
            G[g, c, ts, :, :, y, hr:64] = (up(G[g, c, ts, :, :, y, hr:64]) + up(R1[s1, 0:n, :, :, hr:64])).astype(bf)
        if k == 3:
            Q[sq, 0:n] = (up(G[g, c, ts, :, x, y]) + up(R2[s, 0:n])).astype(bf)
        if k == 4:
            v = up(Q[sq, 0:n, z])
            for u in range(3):
                v = v + up(RZ[s, u, 0:n])
            if m == 1:
                FN[lax.rem(i - NF, 4)] = v[0].astype(bf)
            else:
                sh[ts, :, pl.ds(pl.multiple_of(g * 128, 128), 128)] = v

    def arrive(k, i, m):
        if k > 0:
            for cp in cps(k - 1, i, m):
                cp.wait_recv()
        if k == 1:
            for cp in cps(0, i, m):
                cp.wait_send()
        if k == 4:
            for kk in (1, 2, 3):
                for cp in cps(kk, i, m):
                    cp.wait_send()
        reduce(k, i, m)

    def leave(k, i, m):
        for cp in cps(k, i, m):
            cp.start()

    def both(f, k, t):
        i = t - RS_AT[k]

        for m, lo, hi in ((0, 0, NF), (1, NF, NF + NWG), (2, NF + NWG, NALL)):

            @pl.when((i >= lo) & (i < hi))
            def _(m=m):
                f(k, i, m)

    def ag_arrive(k, t):
        w = t - AG_AT[k] - NF

        @pl.when((w >= 0) & (w < NWG))
        def _():
            for cp in ags(k, w):
                cp.wait_recv()
            if k == 0:
                for cp in ags(0, w):
                    cp.wait_send()
                flush(w).wait()

    def ag_leave(k, t):
        w = t - (AG_AT[k - 1] if k else RS_AT[4]) - NF

        @pl.when((w >= 0) & (w < NWG))
        def _():
            for cp in ags(k, w):
                cp.start()
            if k == 0:
                flush(w).start()

    def stages(t):
        ag_arrive(2, t)
        ag_arrive(1, t)
        ag_arrive(0, t)
        ag_leave(2, t)
        both(arrive, 4, t)
        ag_leave(1, t)
        both(arrive, 3, t)
        ag_leave(0, t)
        both(arrive, 2, t)
        both(leave, 3, t)
        both(arrive, 1, t)
        for k in (2, 1, 0):
            both(leave, k, t)

    def store(g, t, r, own):
        r = r.astype(bf).reshape(4, 2, 2, 64, 256)
        for cc in (0, 1):
            G[g, cc, t, :, :, own] = r[:, :, cc, :, 0:128]
            G[g, cc, t, :, :, 1 - own] = r[:, :, cc, :, 128:256]

    def ffn(t):
        s = lax.rem(t, 2)
        for cp in tload(t, s):
            cp.wait()

        @pl.when(t + 1 < NCH)
        def _():
            for cp in tload(t + 1, 1 - s):
                cp.start()

        fv, fg, fo = [WT[s, :, n].reshape(1024, 256) for n in range(3)]
        m, g_ = mid[...], go[...]
        v, g, gh = dot(m, fv), dot(m, fg), dot(g_, fo)
        hid, dv, dg = (v * g).astype(bf), (gh * g).astype(bf), (gh * v).astype(bf)
        ACC[...] += dotnt(hid, fo)
        dtok[...] += dotnt(dv, fv) + dotnt(dg, fg)
        store(t, 0, dot(LT[0], dv), 0)
        store(t, 1, dot(LT[0], dg), 0)
        store(t, 2, dot(LT[1], hid), 0)

    def ffn_tick(t, _):
        stages(t)

        def one(n, _):
            ffn(n)
            return 0

        lax.fori_loop(jnp.maximum(t, 2 * t - 7), jnp.maximum(t + 1, 2 * t - 5), one, 0)
        return 0

    T = 9
    loops = lambda f, a, b: lax.fori_loop(a, b, f, 0)
    W = W_AT[3]
    for t in range(MEET):
        tick(t)
        if t == 0:
            rate.start()
            norm_rows()
        if t == 1:
            project_own(0, 1)
        if t == 2:
            project_own(2, 3)
        if W <= t < W + 5:
            wload(t - W, 1).start()
        if W + 1 <= t < W + 5:
            project_part(t - W - 1)
        if t == W + 2:
            rate.wait()
            loops(update, 0, 8)
            hand.start()
        if t == W + 3:
            loops(inner, 0, 8)
        if t == W + HAND:
            hand.wait()
            loops(outer, 0, 8)
            gating()
            middle_rows()
            for cp in tload(0, 0):
                cp.start()

    def meet_tick(t, _):
        gather_tick(t)
        return ffn_tick(t - MEET, 0)

    lax.fori_loop(MEET, NCH + 4 * SP, meet_tick, 0)
    lax.fori_loop(NCH + 4 * SP - MEET, T, ffn_tick, 0)
    stages(T)
    keep, scale_mid, scale_out, scale_in = [scal[:, n : n + 1] for n in range(4)]
    OUT[...] = (ACC[...] * keep).astype(bf)
    outs[0].start()
    n2 = mid[...].astype(f32)
    dm = dtok[...]
    gm = go[...].astype(f32) + scale_mid * (dm - n2 * jnp.mean(dm * n2, axis=1, keepdims=True))
    dtok[...] = gm
    gml = gm.astype(bf)
    LT[0] = gml.T
    LT[1] = NM[...].T
    for h in (0, 1):
        cols = slice(h * 512, h * 512 + 512)
        ACC[:, cols] = dotnt(gml, WO[h])
    stages(T + 1)
    dgt, un = ACC[...], UN[...].astype(f32)
    du = dgt * R[1].astype(f32)
    R[1] = (dgt * un).astype(bf)
    DMX[...] = (scale_out * (du - un * jnp.mean(du * un, axis=1, keepdims=True))).astype(bf)

    def first(h, _):
        hs = head(h)
        q = silu(R[4, :, hs].astype(f32)).astype(bf)
        gf = (DMX[:, hs].astype(f32) * jnp.exp(-rate_of(h) * (tau + 1.0))).astype(bf)
        GS2[lax.rem(h + 4, 8)] = dottn(q, gf).astype(bf)
        return 0

    lax.fori_loop(0, 8, first, 0)
    later = rc(GS2, GR2, g2s, g2r, Y)
    later.start()
    def pair(h, _):
        hs = head(h)
        qp, kp = R[4, :, hs].astype(f32), R[3, :, hs].astype(f32)
        q, k, v, dmx = silu(qp).astype(bf), silu(kp).astype(bf), R[2, :, hs], DMX[:, hs]
        cf, rf = jnp.exp(-rate_of(h) * (tau + 1.0)), jnp.exp(rate_of(h) * (rho + 1.0))
        within = jnp.where(ti >= ri, cf * rf, 0.0)
        wt = (dotnt(q, k) * within).astype(bf)
        dsc = (dotnt(dmx, v) * within).astype(bf)
        gf = (dmx.astype(f32) * cf).astype(bf)
        dq = dot(dsc, k) + dotnt(gf, state[h])
        ACC[:, hs] = dottn(dsc, q)
        DV[:, hs] = dottn(wt, dmx)
        sq = jax.nn.sigmoid(qp)
        R[4, :, hs] = (dq * (sq * (1.0 + qp * (1.0 - sq)))).astype(bf)
        return 0

    live = (y == 0).astype(f32)

    def finish(h, _):
        hs = head(h)
        gin = (GR2[h].astype(f32) * live).astype(bf)
        kp = R[3, :, hs].astype(f32)
        sk = jax.nn.sigmoid(kp)
        k = (kp * sk).astype(bf)
        lf = jnp.exp(-rate_of(h) * (511.0 - tau))
        kl = (k.astype(f32) * lf).astype(bf)
        dk = ACC[:, hs] + lf * dotnt(R[2, :, hs], gin)
        R[2, :, hs] = (DV[:, hs] + dot(kl, gin)).astype(bf)
        R[3, :, hs] = (dk * (sk * (1.0 + kp * (1.0 - sk)))).astype(bf)
        return 0

    def wgrad(p):
        j, cp = p // 4, lax.rem(p, 4)
        lo = pl.multiple_of(cp * 128, 128)
        rr = jnp.concatenate([R[j, :, pl.ds(lo, 128)], R[j, :, pl.ds(lo + 512, 128)]], axis=1)
        store(p // 3, lax.rem(p, 3), dot(LT[jnp.minimum(j, 1)], rr), y)

    def wg_tick(t, _):
        stages(t)
        p = t - NF
        wgrad(p)

        @pl.when(p < 8)
        def _():
            pair(p, 0)

        @pl.when(p == 7)
        def _():
            later.wait()
            lax.fori_loop(0, 8, finish, 0)

        for n in range(8):
            @pl.when(p == n + 8)
            def _():
                wbload(n).wait()

        @pl.when((p >= 8) & (p < 16))
        def _():
            n = p - 8
            j, h = 1 + n // 2, lax.rem(n, 2)
            part = dotnt(R[j, :, pl.ds(pl.multiple_of(h * 512, 128), 512)], WV[h])
            ACC[...] = jnp.where(n == 0, 0.0, ACC[...]) + part

        for n in range(6):
            @pl.when(p == n + 8)
            def _():
                wbload(n + 2).start()

        @pl.when(p == 16)
        def _():
            n1 = NM[...].astype(f32)
            dn = ACC[...]
            dtok[...] = dtok[...] + scale_in * (dn - n1 * jnp.mean(dn * n1, axis=1, keepdims=True))
            outs[1].start()

        return 0

    mats = (wg, pg, wv, pv, wk, pk, wq, pq)

    def wbload(n):
        return pltpu.make_async_copy(mats[n], WV.at[n % 2], bsem.at[n % 2])

    wbload(0).start()
    wbload(1).start()
    lax.fori_loop(NF, NF + NWG, wg_tick, 0)
    def tail(t, _):
        stages(t)
        return 0

    lax.fori_loop(NF + NWG, NF + NWG + AG_AT[2], tail, 0)

    def drain(w, _):
        for k in (1, 2):
            for cp in ags(k, w):
                cp.wait_send()
        return 0

    lax.fori_loop(0, NWG, drain, 0)

    outs[2].start()

    def drain_gather(i, _):
        for k in range(4):
            for cp in st(k, i):
                cp.wait_send()
        return 0

    lax.fori_loop(0, NCH, drain_gather, 0)
    for k in (0, 1):
        for cp in near(k):
            cp.wait_send()
    for j in range(5):
        for k in range(3):
            for cp in wst(k, j):
                cp.wait_send()
    for cp in outs:
        cp.wait()


def layer_call(*ins):
    D, V, S = pltpu.SemaphoreType.DMA, pltpu.VMEM, jax.ShapeDtypeStruct
    A, VM = pl.BlockSpec(memory_space=pl.ANY), pl.BlockSpec(memory_space=pltpu.VMEM)
    act, w = (512, 1024), (1024, 512)
    outs = [S(act, bf), S(act, f32), S((3, 64, 1408), f32), S((NWG, 4, 2, 2, 64, 128), bf), S((NCH, 4, 3, 2, 2, 2, 64, 128), bf)] + [S(w, bf)] * 4 + [S(act, bf)]
    scratch = [V((NCH, 3, 64, 128), bf), V((4,) + w, bf), V((2,) + act, bf),
               V((NCH, 2, 3, 4, 2, 2, 64, 128), bf), V((2, 3, 4, 2, 2, 64, 128), bf), V((SLOT1, 3, 4, 2, 64, 128), bf), V((SLOTS, 3, 4, 64, 128), bf),
               V((4, 3, 4, 64, 128), bf), V((SLOTS, 3, 3, 64, 128), bf), V((4, 64, 128), bf), V((2, 4, 3, 2, 2, 64, 256), bf),
               V((2,) + w, bf), V(act, f32), V(act, f32), V((5,) + act, bf), V(act, bf), V(act, bf), V(act, bf), V(act, bf), V(act, bf),
               V((512, 4), f32), V((2, 8, 128), f32)] + [V((8, 128, 128), bf)] * 5 + [V(act, bf), V(act, bf), V(act, f32), V((3, 64, 1408), f32)]
    n, m, a = (NCH,), (NALL,), (NWG,)
    scratch += [D(s) for s in ((NCH, 3), (NCH, 3), (NCH, 2, 3), (NCH, 2, 3), (NCH, 2, 3), (NCH, 2, 3), (2,), (2,), (2,), (2,), n, n,
                               (5,), (5,), (5,), (5,), (5, 2), (5, 2), (), (), (), (), (), (10,),
                               (2, 2), (2,), (), (), m, m, (NALL, 2), (NALL, 2), (NALL, 2), (NALL, 2), (NALL, 3), (NALL, 3),
                               (NWG, 3), (NWG, 3), a, a, a, a, a, (5,))]
    return pl.pallas_call(
        layer_kernel,
        out_shape=outs,
        in_specs=[A, A] + [pl.BlockSpec(memory_space=pltpu.SMEM)] * 2 + [VM] * 3 + [A] * 5,
        out_specs=[A] * 10,
        scratch_shapes=scratch,
        compiler_params=pltpu.CompilerParams(collective_id=1, has_side_effects=True, vmem_limit_bytes=67043328),
    )(*ins)
def finish_kernel(o, sh, out, dtok, output, d_tokens, d_query, d_key, d_value, d_gate, d_out, d_f_value, d_f_gate, d_f_out):
    output[...] = out[...]
    d_tokens[...] = dtok[...]
    for n in range(4):
        cols = slice(n * 128, n * 128 + 128)
        d_out[cols, :] = o[n].astype(f32).T
        d_gate[:, cols] = o[4 + n].astype(f32)
        d_value[:, cols] = o[8 + n].astype(f32)
        d_key[:, cols] = o[12 + n].astype(f32)
        d_query[:, cols] = o[16 + n].astype(f32)

    @pl.when(pl.program_id(0) == 0)
    def _():
        d_f_value[...] = sh[0]
        d_f_gate[...] = sh[1]
        d_f_out[...] = sh[2]


def finish_call(o, sh, out, dtok):
    S = jax.ShapeDtypeStruct
    whole = lambda *s: pl.BlockSpec(s, lambda i: (0,) * len(s))
    return pl.pallas_call(
        finish_kernel,
        grid=(2,),
        out_shape=[S((512, 1024), bf), S((512, 1024), f32)] + [S((1024, 512), f32)] * 4 + [S((512, 1024), f32)] + [S((64, 1408), f32)] * 3,
        in_specs=[pl.BlockSpec((20, 512, 128), lambda i: (0, i, 0)), whole(3, 64, 1408)] + [pl.BlockSpec((256, 1024), lambda i: (i, 0))] * 2,
        out_specs=[pl.BlockSpec((256, 1024), lambda i: (i, 0))] * 2 + [pl.BlockSpec((512, 512), lambda i: (i, 0))] * 4 + [pl.BlockSpec((512, 512), lambda i: (0, i))] + [whole(64, 1408)] * 3,
        compiler_params=pltpu.CompilerParams(vmem_limit_bytes=67043328),
    )(o, sh, out, dtok)

def fast_body(tokens, lengths, decay, w_query, w_key, w_value, w_gate, w_out, f_value, f_gate, f_out, cotangent):
    weights = (w_query, w_key, w_value, w_gate, w_out)
    output, d_tokens, shares, grads, *_ = layer_call(tokens, cotangent, lengths, decay, f_value, f_gate, f_out.T, *weights)
    *results, d_f_out = finish_call(grads.reshape(NWG, 1024, 128), shares, output, d_tokens)
    return (*results, d_f_out.T)


def solution(mesh):
    placed = (
        P(("dp", "head"), None),
        P("dp"),
        P("head"),
        P(None, "head"),
        P(None, "head"),
        P(None, "head"),
        P(None, "head"),
        P("head", None),
        P("dp", "head"),
        P("dp", "head"),
        P("head", "dp"),
        P(("dp", "head"), None),
    )
    fast = mesh.shape["dp"] == 16 and mesh.shape["head"] == 2
    return jax.shard_map(
        fast_body if fast else general_body,
        mesh=mesh,
        in_specs=placed,
        out_specs=(
            P(("dp", "head"), None),
            P(("dp", "head"), None),
            P(None, "head"),
            P(None, "head"),
            P(None, "head"),
            P(None, "head"),
            P("head", None),
            P("dp", "head"),
            P("dp", "head"),
            P("head", "dp"),
        ),
        check_vma=False,
    )
```
